256 devices in a mesh: row: 8 (over x, core), col: 32 (over y, z).
Axes of the slice: x: 4, y: 4, z: 8, core: 2. Of those that a mesh axis runs over, the one named last changes fastest.
Arguments:
- deflation: bfloat16 [16, 256, 16, 3072], P('row', 'col'), may hold values from 0 to 0.019897461
- coefficient: float32 [16, 256, 16], P('row', 'col'), may hold values from 1 to 10
- gradients: bfloat16 [3, 64, 64], replicated, may hold values from -0.75 to 0.75
- x_penalty: float32 [24, 256, 16], P('row', 'col'), may hold values from 1 to 10, as said below
- y_penalty: float32 [16, 288, 16], P('row', 'col'), may hold values from 1 to 10, as said below
- z_penalty: float32 [16, 256, 17], P('row', 'col'), may hold values from 1 to 10
- coarse_order: int32 [1024], replicated, may hold values from 0 to 1023, as said below
Outputs:
- coarse_blocks: float32 [1024, 7, 2304], P(('row', 'col'))
- panel: float32 [1024, 48, 528], P(('row', 'col'))
The draws below stay inside these ranges and needn't reach their ends.
Inputs may be any that keep to these rules, and one draw needn't show every extreme that they name: `coarse_order`: each subdomain number appears once; subdomains with consecutive coarse numbers are mostly neighbours along the third or second dimension. `x_penalty`: row i * 3 + 2 equals row (i + 1) * 3: a face between two devices' blocks is held by both. `y_penalty`: column j * 9 + 8 equals column (j + 1) * 9: a face between two devices' blocks is held by both.
All inputs are finite; a program needn't handle non-finite values.
Results may differ from the reference program's by a relative error of at most 0.00044.
Values may be sent and summed in bfloat16 or wider, within the bound.
No kernel may reach another device: no remote copies, remote signals or barrier semaphores. Data moves between devices by JAX's collectives and lax.ppermute only.
A program may use at most 128 MiB of HBM per device.

```python
import math
import jax
import jax.numpy as jnp
from jax import lax

NV = 48
EX = 2
EY = 8
SUB_DEV = 4
PB = 11
NXE = 16
NYE = 256
NZE = 16
SUBS = 1024
N_ROW = 8
N_COL = 32


def draw_x_penalty(key, part):
    base = jnp.exp(jax.random.uniform(key, (NXE + 1, NYE, NZE), jnp.float32, 0.0, math.log(10.0)))
    places = jnp.arange(NXE + N_ROW, dtype=jnp.int32)
    faces = places // (EX + 1) * EX + places % (EX + 1)
    return base[faces]


def draw_y_penalty(key, part):
    base = jnp.exp(jax.random.uniform(key, (NXE, NYE + 1, NZE), jnp.float32, 0.0, math.log(10.0)))
    places = jnp.arange(NYE + N_COL, dtype=jnp.int32)
    faces = places // (EY + 1) * EY + places % (EY + 1)
    return base[:, faces]


def draw_coarse_order(key, part):
    start_key = jax.random.fold_in(key, 11)
    sense_key = jax.random.fold_in(key, 23)
    device = jax.random.randint(start_key, (), 0, N_ROW * N_COL, dtype=jnp.int32)
    flip = jax.random.randint(sense_key, (), 0, 2, dtype=jnp.int32)
    start = device * SUB_DEV + flip * (SUB_DEV - 1)
    sign = 1 - 2 * flip
    owner = jnp.arange(SUBS, dtype=jnp.int32)
    return jnp.mod((owner - start) * sign, SUBS).astype(jnp.int32)


def shard_levels(rng, shape, cuts, low, top_value):
    loudness, own = 1.0, jax.random.fold_in(rng, 6)
    for dim, blocks in cuts:
        steps = jnp.exp(jax.random.uniform(jax.random.fold_in(own, dim), (blocks,), jnp.float32, low / len(cuts), top_value / len(cuts)))
        loudness = loudness * jnp.repeat(steps, shape[dim] // blocks).reshape([-1 if axis == dim else 1 for axis in range(len(shape))])
    return loudness


def bell_draw(own_key, shape, deviation, reach, kind=jnp.bfloat16):
    drawn = jax.random.normal(own_key, shape, jnp.float32) * deviation
    return jnp.minimum(jnp.maximum(drawn, -reach), reach).astype(kind)


def setup_inputs(seed: int = 0) -> dict:
    key_of = jax.random.split(jax.random.key(seed), 8)
    return {
        "deflation": jnp.clip(0.019897461 * jax.random.uniform(key_of[0], (NXE, NYE, NZE, 64 * NV), jnp.float32) ** shard_levels(key_of[0], (NXE, NYE, NZE, 64 * NV), ((0, 8), (1, 32)), -0.2, 0.2), 0.0, 0.019897461).astype(jnp.bfloat16),
        "coefficient": jnp.clip(jnp.exp(math.log(10.0) - 2.3025851 * jax.random.uniform(key_of[1], (NXE, NYE, NZE), jnp.float32) ** shard_levels(key_of[1], (NXE, NYE, NZE), ((0, 8), (1, 32)), -0.2, 0.2)), 1.0, 10.0),
        "gradients": bell_draw(key_of[2], (3, 64, 64), 64 ** -0.5, 0.75),
        "x_penalty": draw_x_penalty(jax.random.fold_in(key_of[7], 71), 0),
        "y_penalty": draw_y_penalty(jax.random.fold_in(key_of[7], 71), 0),
        "z_penalty": jnp.clip(jnp.exp(math.log(10.0) - 2.3025851 * jax.random.uniform(key_of[5], (NXE, NYE, NZE + 1), jnp.float32) ** shard_levels(key_of[5], (NXE, NYE, NZE + 1), ((0, 8), (1, 32)), -0.2, 0.2)), 1.0, 10.0),
        "coarse_order": draw_coarse_order(jax.random.fold_in(key_of[7], 71), 0),
    }


LINE_WEIGHTS = (1.0 / 6.0, 5.0 / 6.0, 5.0 / 6.0, 1.0 / 6.0)

def node_weights():
    line = jnp.array(LINE_WEIGHTS, jnp.float32)
    return (line[:, None, None] * line[None, :, None] * line[None, None, :]).reshape(64)

def contract(form, left, right):
    return jnp.einsum(form, left.astype(jnp.float32), right.astype(jnp.float32))

def traces(values, axis, side):
    lead = values.ndim - 1
    nodes = values.reshape(values.shape[:lead] + (4, 4, 4, NV))
    picked = lax.index_in_dim(nodes, side, lead + axis, keepdims=False)
    return picked.reshape(values.shape[:lead] + (16, NV))

def scaled(trace, root):
    return (root[..., None, None] * trace.astype(jnp.float32)).astype(jnp.bfloat16)

def grouped(left, right, groups):
    shape = left.shape
    split = shape[:2] + (groups, shape[2] // groups) + shape[3:]
    return contract('xyskav,xyskaw->svw', left.reshape(split), right.reshape(split))

def lateral(plus, minus, root, below, above, groups):
    jump = (root[1:-1, :, :, None, None] * (plus[:-1].astype(jnp.float32) - minus[1:].astype(jnp.float32))).astype(jnp.bfloat16)
    low_own = scaled(minus[0], root[0])
    low_other = scaled(below, root[0])
    high_own = scaled(plus[-1], root[-1])
    high_other = scaled(above, root[-1])
    self_part = grouped(jump, jump, groups) + grouped(low_own[None], low_own[None], groups) + grouped(high_own[None], high_own[None], groups)
    return (self_part, -grouped(low_own[None], low_other[None], groups), -grouped(high_own[None], high_other[None], groups))

def vertical(plus, minus, root, groups):
    width, length, depth = plus.shape[:3]
    height = depth // groups
    plus = plus.reshape(width, length, groups, height, 16, NV)
    minus = minus.reshape(width, length, groups, height, 16, NV)
    inner_root = root[:, :, :depth].reshape(width, length, groups, height)[:, :, :, 1:]
    jump = (inner_root[..., None, None] * (plus[:, :, :, :-1].astype(jnp.float32) - minus[:, :, :, 1:].astype(jnp.float32))).astype(jnp.bfloat16)
    edge_root = root[:, :, ::height]
    first = minus[:, :, :, 0]
    last = plus[:, :, :, -1]
    blank = jnp.zeros_like(last[:, :, :1])
    low_own = scaled(first, edge_root[:, :, :groups])
    low_other = scaled(jnp.concatenate([blank, last[:, :, :-1]], axis=2), edge_root[:, :, :groups])
    high_own = scaled(last, edge_root[:, :, 1:])
    high_other = scaled(jnp.concatenate([first[:, :, 1:], blank], axis=2), edge_root[:, :, 1:])
    pairing = 'xysav,xysaw->svw'
    self_part = contract('xyskav,xyskaw->svw', jump, jump) + contract(pairing, low_own, low_own) + contract(pairing, high_own, high_own)
    return (self_part, -contract(pairing, low_own, low_other), -contract(pairing, high_own, high_other))

def volume(values, coefficient, gradients, groups):
    width, length, depth = values.shape[:3]
    nodes = values.reshape(width, length, depth, 64, NV)
    factor = jnp.sqrt(coefficient[..., None] * node_weights())
    total = jnp.zeros((groups, NV, NV), jnp.float32)
    for axis in range(3):
        product = contract('ab,xyzbv->xyzav', gradients[axis], nodes)
        rounded = (product * factor[..., None]).astype(jnp.bfloat16)
        rounded = rounded.reshape(width, length, groups, depth // groups, 64, NV)
        total = total + contract('xyskav,xyskaw->svw', rounded, rounded)
    return total

def column_blocks(values, coefficient, gradients, x_root, y_root, z_root, below_x, above_x, below_y, above_y, groups):
    self_x, low_x, high_x = lateral(traces(values, 0, 3), traces(values, 0, 0), x_root, below_x, above_x, groups)
    self_y, low_y, high_y = lateral(jnp.swapaxes(traces(values, 1, 3), 0, 1), jnp.swapaxes(traces(values, 1, 0), 0, 1), jnp.swapaxes(y_root, 0, 1), below_y, above_y, groups)
    self_z, low_z, high_z = vertical(traces(values, 2, 3), traces(values, 2, 0), z_root, groups)
    diagonal = volume(values, coefficient, gradients, groups) + self_x + self_y + self_z
    return jnp.stack([diagonal, low_x, high_x, low_y, high_y, low_z, high_z], axis=1)

def panel_rows(blocks, column_block, present):
    picks = (present[:, :, None] & (column_block[:, :, None] == jnp.arange(PB, dtype=jnp.int32)[None, None, :])).astype(jnp.float32)
    rows = jnp.einsum('stp,stvw->svpw', picks, blocks, precision=lax.Precision.HIGHEST).reshape(blocks.shape[0], NV, PB * NV)
    select = (column_block[:, :1] == jnp.arange(PB, dtype=jnp.int32)[None, :]).astype(jnp.float32)
    share = jnp.einsum('sp,svq->pvq', select, rows, precision=lax.Precision.HIGHEST)
    return (rows, select, share)

def finish(rows, select, assembled):
    whole = assembled.reshape(PB * NV, PB * NV)
    factor = jnp.linalg.cholesky(0.5 * (whole + whole.T))
    count = rows.shape[0]
    solved = jax.scipy.linalg.solve_triangular(factor, rows.reshape(count * NV, PB * NV).T, lower=True).T.reshape(count, NV, PB * NV)
    inside = jnp.einsum('sp,pvq->svq', select, factor.reshape(PB, NV, PB * NV), precision=lax.Precision.HIGHEST)
    return jnp.where(lax.optimization_barrier(jnp.sum(select, axis=1))[:, None, None] > 0, inside, solved)

def reference(deflation, coefficient, gradients, x_penalty, y_penalty, z_penalty, coarse_order):
    anchor = jnp.zeros((), jnp.int32)

    def one_column(index):
        row_pos = (index // N_COL).astype(jnp.int32)
        col_pos = (index % N_COL).astype(jnp.int32)
        start_x = (row_pos * EX).astype(jnp.int32)
        start_y = (col_pos * EY).astype(jnp.int32)
        values = lax.dynamic_slice(deflation, (start_x, start_y, anchor, anchor), (EX, EY, NZE, 64 * NV))
        local_coef = lax.dynamic_slice(coefficient, (start_x, start_y, anchor), (EX, EY, NZE))
        x_root = jnp.sqrt(lax.dynamic_slice(x_penalty, ((row_pos * (EX + 1)).astype(jnp.int32), start_y, anchor), (EX + 1, EY, NZE)))
        y_root = jnp.sqrt(lax.dynamic_slice(y_penalty, (start_x, (col_pos * (EY + 1)).astype(jnp.int32), anchor), (EX, EY + 1, NZE)))
        z_root = jnp.sqrt(lax.dynamic_slice(z_penalty, (start_x, start_y, anchor), (EX, EY, NZE + 1)))
        plane = lax.dynamic_slice(deflation, (jnp.maximum(start_x - 1, 0).astype(jnp.int32), start_y, anchor, anchor), (1, EY, NZE, 64 * NV))[0]
        below_x = traces(jnp.where(row_pos > 0, plane, jnp.zeros_like(plane)), 0, 3)
        plane = lax.dynamic_slice(deflation, (jnp.minimum(start_x + EX, NXE - 1).astype(jnp.int32), start_y, anchor, anchor), (1, EY, NZE, 64 * NV))[0]
        above_x = traces(jnp.where(row_pos < N_ROW - 1, plane, jnp.zeros_like(plane)), 0, 0)
        plane = lax.dynamic_slice(deflation, (start_x, jnp.maximum(start_y - 1, 0).astype(jnp.int32), anchor, anchor), (EX, 1, NZE, 64 * NV))[:, 0]
        below_y = traces(jnp.where(col_pos > 0, plane, jnp.zeros_like(plane)), 1, 3)
        plane = lax.dynamic_slice(deflation, (start_x, jnp.minimum(start_y + EY, NYE - 1).astype(jnp.int32), anchor, anchor), (EX, 1, NZE, 64 * NV))[:, 0]
        above_y = traces(jnp.where(col_pos < N_COL - 1, plane, jnp.zeros_like(plane)), 1, 0)
        return column_blocks(values, local_coef, gradients, x_root, y_root, z_root, below_x, above_x, below_y, above_y, SUB_DEV)
    blocks = lax.map(one_column, jnp.arange(N_ROW * N_COL, dtype=jnp.int32)).reshape(SUBS, 7, NV, NV)
    owner = jnp.arange(SUBS, dtype=jnp.int32)
    device = owner // SUB_DEV
    local = owner % SUB_DEV
    row_pos = device // N_COL
    col_pos = device % N_COL
    stride = N_COL * SUB_DEV
    neighbours = jnp.stack([owner, owner - stride, owner + stride, owner - SUB_DEV, owner + SUB_DEV, owner - 1, owner + 1], axis=1)
    present = jnp.stack([owner >= 0, row_pos > 0, row_pos < N_ROW - 1, col_pos > 0, col_pos < N_COL - 1, local > 0, local < SUB_DEV - 1], axis=1)
    column_block = jnp.take(coarse_order, jnp.clip(neighbours, 0, SUBS - 1)).astype(jnp.int32)
    rows, select, share = panel_rows(blocks, column_block, present)
    panel = finish(rows, select, share)
    return (blocks.reshape(SUBS, 7, NV * NV), panel)
```

```python
import jax
import jax.numpy as jnp
from jax import lax
from jax.experimental import pallas as pl
from jax.experimental.pallas import tpu as pltpu
from jax.sharding import PartitionSpec as P

NV = 48
SUB_DEV = 4
PB = 11
SUBS = 1024
N_ROW = 8
N_COL = 32


LINE_WEIGHTS = (1.0 / 6.0, 5.0 / 6.0, 5.0 / 6.0, 1.0 / 6.0)


def with_halo(shard, sides, width):
    for axis, dim in sides:
        size, length = (lax.axis_size(axis), shard.shape[dim])
        up = [(i, (i + 1) % size) for i in range(size - 1)]
        down = [(j, i) for i, j in up]
        last = lax.slice_in_dim(shard, length - width, length, axis=dim)
        initial = lax.slice_in_dim(shard, 0, width, axis=dim)
        before = lax.ppermute(last, axis, up)
        after = lax.ppermute(initial, axis, down)
        shard = jnp.concatenate([before, shard, after], axis=dim)
    return shard


def node_weights():
    line = jnp.array(LINE_WEIGHTS, jnp.float32)
    return (line[:, None, None] * line[None, :, None] * line[None, None, :]).reshape(64)


def contract(form, left, right):
    return jnp.einsum(form, left, right, preferred_element_type=jnp.float32)


def traces(values, axis, side):
    lead = values.ndim - 1
    nodes = values.reshape(values.shape[:lead] + (4, 4, 4, NV))
    picked = lax.index_in_dim(nodes, side, lead + axis, keepdims=False)
    return picked.reshape(values.shape[:lead] + (16, NV))


def scaled(trace, root):
    return (root[..., None, None] * trace.astype(jnp.float32)).astype(jnp.bfloat16)


def grouped(left, right, groups):
    shape = left.shape
    split = shape[:2] + (groups, shape[2] // groups) + shape[3:]
    return contract("xyskav,xyskaw->svw", left.reshape(split), right.reshape(split))


def lateral(plus, minus, root, below, above, groups):
    jump = (
        root[1:-1, :, :, None, None]
        * (plus[:-1].astype(jnp.float32) - minus[1:].astype(jnp.float32))
    ).astype(jnp.bfloat16)
    low_own = scaled(minus[0], root[0])
    low_other = scaled(below, root[0])
    high_own = scaled(plus[-1], root[-1])
    high_other = scaled(above, root[-1])
    self_part = (
        grouped(jump, jump, groups)
        + grouped(low_own[None], low_own[None], groups)
        + grouped(high_own[None], high_own[None], groups)
    )
    return (
        self_part,
        -grouped(low_own[None], low_other[None], groups),
        -grouped(high_own[None], high_other[None], groups),
    )


def vertical(plus, minus, root, groups):
    width, length, depth = plus.shape[:3]
    height = depth // groups
    plus = plus.reshape(width, length, groups, height, 16, NV)
    minus = minus.reshape(width, length, groups, height, 16, NV)
    inner_root = root[:, :, :depth].reshape(width, length, groups, height)[:, :, :, 1:]
    jump = (
        inner_root[..., None, None]
        * (plus[:, :, :, :-1].astype(jnp.float32) - minus[:, :, :, 1:].astype(jnp.float32))
    ).astype(jnp.bfloat16)
    edge_root = root[:, :, ::height]
    first = minus[:, :, :, 0]
    last = plus[:, :, :, -1]
    blank = jnp.zeros_like(last[:, :, :1])
    low_own = scaled(first, edge_root[:, :, :groups])
    low_other = scaled(jnp.concatenate([blank, last[:, :, :-1]], axis=2), edge_root[:, :, :groups])
    high_own = scaled(last, edge_root[:, :, 1:])
    high_other = scaled(jnp.concatenate([first[:, :, 1:], blank], axis=2), edge_root[:, :, 1:])
    pairing = "xysav,xysaw->svw"
    self_part = (
        contract("xyskav,xyskaw->svw", jump, jump)
        + contract(pairing, low_own, low_own)
        + contract(pairing, high_own, high_own)
    )
    return (
        self_part,
        -contract(pairing, low_own, low_other),
        -contract(pairing, high_own, high_other),
    )


def volume(values, coefficient, gradients, groups):
    width, length, depth = values.shape[:3]
    nodes = values.reshape(width, length, depth, 64, NV)
    factor = jnp.sqrt(coefficient[..., None] * node_weights())
    total = jnp.zeros((groups, NV, NV), jnp.float32)
    for axis in range(3):
        product = contract("ab,xyzbv->xyzav", gradients[axis], nodes)
        rounded = (product * factor[..., None]).astype(jnp.bfloat16)
        rounded = rounded.reshape(width, length, groups, depth // groups, 64, NV)
        total = total + contract("xyskav,xyskaw->svw", rounded, rounded)
    return total


def eliminate(work):
    groups = [work[8 * v : 8 * v + 8] for v in range(6)]
    sub = lax.broadcasted_iota(jnp.int32, (8, 128), 0)
    scales = []
    for g in range(6):
        splat = [
            [jnp.broadcast_to(groups[v][:, 64 + 8 * g + k : 65 + 8 * g + k], (8, 128)) for v in range(g, 6)]
            for k in range(8)
        ]
        head = groups[g]
        scale = jnp.zeros((8, 128), jnp.float32)
        for k in range(8):
            pivot = jnp.broadcast_to(splat[k][0][k : k + 1, :], (8, 128))
            inverse = 1.0 / pivot
            scale = jnp.where(sub == k, lax.rsqrt(pivot), scale)
            factors = [c * inverse for c in splat[k]]
            factors[0] = jnp.where(sub > k, factors[0], 0.0)
            for m in range(k + 1, 8):
                upper = jnp.broadcast_to(splat[m][0][k : k + 1, :], (8, 128))
                splat[m] = [c - f * upper for c, f in zip(splat[m], factors)]
            row = jnp.broadcast_to(head[k : k + 1, :], (8, 128))
            head = head - factors[0] * row
            for v in range(g + 1, 6):
                groups[v] = groups[v] - factors[v - g] * row
        groups[g] = head
        scales.append(scale)
    return jnp.concatenate([a * b for a, b in zip(groups, scales)], axis=0)


def halves(values):
    high = values.astype(jnp.bfloat16)
    low = (values - high.astype(jnp.float32)).astype(jnp.bfloat16)
    return high, low


def across(left, right):
    return lax.dot_general(left, right, (((1,), (1,)), ((), ())), preferred_element_type=jnp.float32)


def factor_kernel(order, meta, own, below, above, extra, blocks, out, grid, got, got_x, lhs, rhs, sems):
    device = meta[0]
    lane = lax.broadcasted_iota(jnp.int32, (NV, 128), 1)

    def place(value, half, row, column):
        parity = column % 2
        shift = 64 * ((parity + half) % 2)
        moved = pltpu.roll(value, shift, 1)
        inside = (lane >= 64 * parity) & (lane < 64 * parity + NV)
        at = pl.ds(pl.multiple_of(row, 16), NV)
        grid[column // 2, at, :] += jnp.where(inside, moved, 0.0)

    def ordered(subdomain):
        return order[jnp.clip(subdomain, 0, SUBS - 1)]

    def neighbours(subdomain):
        column = (subdomain // SUB_DEV) % N_COL
        local = subdomain % SUB_DEV
        stride = N_COL * SUB_DEV
        return (
            (subdomain, subdomain >= 0),
            (subdomain - stride, subdomain >= stride),
            (subdomain + stride, subdomain < SUBS - stride),
            (subdomain - SUB_DEV, column > 0),
            (subdomain + SUB_DEV, column < N_COL - 1),
            (subdomain - 1, local > 0),
            (subdomain + 1, local < SUB_DEV - 1),
        )

    relevant = jnp.int32(0)
    for l in range(SUB_DEV):
        for near, there in neighbours(device * SUB_DEV + l):
            relevant += (there & (ordered(near) < PB)).astype(jnp.int32)

    @pl.when(relevant == 0)
    def _():
        out[...] = jnp.zeros_like(out)

    @pl.when(relevant > 0)
    def _():
        for index, source in enumerate((own, below, above)):

            @pl.when(meta[1] == index)
            def _():
                pltpu.make_async_copy(source, got, sems.at[0]).start()

        pltpu.make_async_copy(extra, got_x, sems.at[1]).start()
        grid[...] = jnp.zeros_like(grid)
        rhs[...] = jnp.zeros_like(rhs)
        for l in range(SUB_DEV):
            for kind, (near, there) in enumerate(neighbours(device * SUB_DEV + l)):
                column = ordered(near)

                @pl.when(there & (column < PB))
                def _():
                    block = blocks[l, kind]
                    place(jnp.concatenate([block, jnp.zeros((NV, 128 - NV), jnp.float32)], axis=1), 0, PB * NV + NV * l, column)

        pltpu.make_async_copy(own, got, sems.at[0]).wait()
        pltpu.make_async_copy(extra, got_x, sems.at[1]).wait()
        for slot in range(12):
            i, l = slot // SUB_DEV, slot % SUB_DEV
            s = meta[4 + slot]
            p = ordered(s)
            near = neighbours(s)
            for kind, (t, there) in enumerate((near[0], near[3], near[5], near[1])):
                q = ordered(t)

                @pl.when((s >= 0) & there & (p < PB) & (q < PB))
                def _():
                    if kind < 3:
                        value, half = got[i, (l % 2) * 3 + kind], l // 2
                    else:
                        value, half = got_x[slot % 6], slot // 6
                    place(value, half, NV * jnp.maximum(p, q), jnp.minimum(p, q))

        rows48 = lax.broadcasted_iota(jnp.int32, (NV, 128), 0)

        def step(k, carry):
            tile = k // 2
            parity = k % 2
            at = pl.ds(pl.multiple_of(k * NV, 16), NV)
            diag = pltpu.roll(grid[tile, at, :], 64 * (1 - parity), 1)
            work = jnp.where(lane < 64, (lane == rows48).astype(jnp.float32), jnp.where(lane < 64 + NV, diag, 0.0))
            inverse = jnp.where(lane < NV, eliminate(work), 0.0)
            inverse = pltpu.roll(inverse, 64 * parity, 1)
            gap = jnp.zeros((16, 128), jnp.float32)
            b_high, b_low = halves(jnp.concatenate([inverse, gap, inverse, gap], axis=0))
            column = grid[tile]
            c_high, c_low = halves(column)
            solved = across(jnp.concatenate([c_high, c_low], axis=1), jnp.concatenate([b_high, b_high], axis=1)) + across(c_high, b_low)
            lane_all = lax.broadcasted_iota(jnp.int32, solved.shape, 1)
            row_all = lax.broadcasted_iota(jnp.int32, solved.shape, 0) - k * NV
            keep = (row_all >= NV) | ((lane_all % 64) <= row_all)
            solved = jnp.where(keep, solved, 0.0)
            grid[tile] = jnp.where(lane_all // 64 == parity, solved, column)
            s_high, s_low = halves(solved)
            lhs[:, :128] = s_high
            lhs[:, 128:] = s_low
            mixed = jnp.where(lane_all < 64, s_high.astype(jnp.float32), s_low.astype(jnp.float32)).astype(jnp.bfloat16)
            for i in range(PB):
                rhs[64 * i : 64 * i + NV, :] = jnp.where(i > k, mixed[NV * i : NV * i + NV], jnp.zeros((NV, 128), jnp.bfloat16))

            def trail(t, c):
                other = rhs[pl.ds(pl.multiple_of(128 * t, 128), 128), :]
                grid[t] -= across(lhs[...], jnp.concatenate([other, other], axis=1))
                return c

            lax.fori_loop((k + 1) // 2, 6, trail, 0)
            return carry

        lax.fori_loop(0, PB, step, 0)
        for l in range(SUB_DEV):
            p = ordered(device * SUB_DEV + l)
            inside = p < PB
            start = jnp.where(inside, NV * p, PB * NV + NV * l)
            at = pl.ds(pl.multiple_of(start, 16), NV)
            pieces = []
            for j in range(PB):
                piece = grid[j // 2, at, :][:, 64 * (j % 2) : 64 * (j % 2) + NV]
                pieces.append(jnp.where(inside & (j > p), 0.0, piece))
            out[l] = jnp.concatenate(pieces, axis=1)


def factor(order, meta, own, below, above, extra, blocks):
    smem = pl.BlockSpec(memory_space=pltpu.SMEM)
    hbm = pl.BlockSpec(memory_space=pl.ANY)
    vmem = pl.BlockSpec(memory_space=pltpu.VMEM)
    return pl.pallas_call(
        factor_kernel,
        out_shape=jax.ShapeDtypeStruct((SUB_DEV, NV, PB * NV), jnp.float32),
        in_specs=[smem, smem, hbm, hbm, hbm, hbm, vmem],
        out_specs=vmem,
        scratch_shapes=[
            pltpu.VMEM((6, PB * NV + SUB_DEV * NV, 128), jnp.float32),
            pltpu.VMEM((3, 6, NV, 128), jnp.float32),
            pltpu.VMEM((6, NV, 128), jnp.float32),
            pltpu.VMEM((PB * NV + SUB_DEV * NV, 256), jnp.bfloat16),
            pltpu.VMEM((12 * 64, 128), jnp.bfloat16),
            pltpu.SemaphoreType.DMA((2,)),
        ],
        name="factor",
    )(order, meta, own, below, above, extra, blocks)


def shifted(value, amount):
    size = N_ROW * N_COL
    return lax.ppermute(value, ("row", "col"), [(i, (i + amount) % size) for i in range(size)])


def packed(blocks):
    wide = jnp.pad(blocks, ((0, 0), (0, 0), (0, 64 - NV)))
    return jnp.concatenate([wide[:6], wide[6:]], axis=2)


def everywhere(value):
    size = N_ROW * N_COL
    step = 1
    while step < size:
        value = value + lax.ppermute(value, ("row", "col"), [(i, i ^ step) for i in range(size)])
        step *= 2
    return value


def exchange(device, order, own_blocks):
    subdomain = jnp.arange(SUBS, dtype=jnp.int32)
    first = jnp.sum(jnp.where(order == 0, subdomain // SUB_DEV, 0))
    size = N_ROW * N_COL
    distance = (subdomain // SUB_DEV - first + size // 2) % size - size // 2
    inside = order < PB
    least = jnp.min(jnp.where(inside, distance, size))
    most = jnp.max(jnp.where(inside, distance, -size))
    near = (most - least) <= 2
    base = (first + least) % size
    mine = device * SUB_DEV + jnp.arange(SUB_DEV, dtype=jnp.int32)
    my_order = lax.dynamic_slice(order, (device * SUB_DEV,), (SUB_DEV,))

    def oriented(block, offset):
        other = lax.dynamic_slice(jnp.concatenate([order[:128], order]), (128 + device * SUB_DEV - offset,), (SUB_DEV,))
        return jnp.where((my_order > other)[:, None, None], block, jnp.swapaxes(block, 1, 2))

    diag = own_blocks[:, 0]
    low_y = oriented(own_blocks[:, 3], SUB_DEV)
    low_z = oriented(own_blocks[:, 5], 1)
    low_x = oriented(own_blocks[:, 1], N_COL * SUB_DEV)
    share = packed(jnp.stack([diag, low_y, low_z], axis=1).reshape(12, NV, NV))
    right1 = shifted(share, 1)
    left1 = shifted(share, -1)
    right2 = shifted(right1, 1)
    left2 = shifted(left1, -1)
    offset = (base - device + size // 2) % size - size // 2
    middle = jnp.stack([right2, right1, share, left1, left2])
    window = lax.dynamic_slice(middle, (jnp.clip(offset + 2, 0, 2), 0, 0, 0), (3,) + share.shape)
    below = shifted(window, N_COL)
    above = shifted(window, -N_COL)
    right3 = shifted(right2, 1)
    left3 = shifted(left2, -1)
    ends = jnp.where(offset < 0, jnp.stack([right3, right2, right1]), jnp.stack([left1, left2, left3]))
    window = jnp.where((offset >= -2) & (offset <= 0), window, ends)
    from_below = (offset + N_COL + 2) % size <= 2
    from_above = (offset - N_COL + 2) % size <= 2
    flat = (offset >= -3) & (offset <= 1)
    pick = jnp.where(flat, 0, jnp.where(from_below, 1, jnp.where(from_above, 2, 0)))

    def local_path(_):
        listed = (base * SUB_DEV + jnp.arange(12, dtype=jnp.int32)) % SUBS
        return (window, jnp.zeros((6, NV, 128), jnp.float32), listed, pick)

    def global_path(_):
        slots = jnp.arange(12, dtype=jnp.int32)
        hit = (order[None, :] == slots[:, None]) & (slots[:, None] < PB)
        listed = jnp.where(slots < PB, jnp.sum(jnp.where(hit, subdomain[None, :], 0), axis=1), -1)
        mask = ((my_order[None, :] == slots[:, None]) & (slots[:, None] < PB)).astype(jnp.float32)
        kinds = jnp.stack([diag, low_y, low_z, low_x], axis=1)
        placed = jnp.einsum("ps,skvw->pkvw", mask, kinds, precision=lax.Precision.HIGHEST)
        whole = everywhere(
            jnp.stack([packed(placed[4 * i : 4 * i + 4, :3].reshape(12, NV, NV)) for i in range(3)] + [packed(placed[:, 3])])
        )
        return (whole[:3], whole[3], listed, jnp.int32(0))

    window, extra, listed, pick = lax.cond(near, local_path, global_path, None)
    meta = jnp.concatenate([jnp.stack([device, pick, jnp.int32(0), jnp.int32(0)]), listed]).astype(jnp.int32)
    return factor(order, meta, window, below, above, extra, own_blocks)


def shards(deflation, coefficient, gradients, x_penalty, y_penalty, z_penalty, coarse_order):
    plus_x = traces(deflation, 0, 3)
    minus_x = traces(deflation, 0, 0)
    plus_y = traces(deflation, 1, 3)
    minus_y = traces(deflation, 1, 0)
    padded = with_halo(deflation, (("row", 0), ("col", 1)), 1)
    below_x = traces(padded[0, 1:-1], 0, 3)
    above_x = traces(padded[-1, 1:-1], 0, 0)
    below_y = traces(padded[1:-1, 0], 1, 3)
    above_y = traces(padded[1:-1, -1], 1, 0)
    x_root = jnp.sqrt(x_penalty)
    y_root = jnp.sqrt(y_penalty)
    z_root = jnp.sqrt(z_penalty)
    self_x, low_x, high_x = lateral(plus_x, minus_x, x_root, below_x, above_x, SUB_DEV)
    self_y, low_y, high_y = lateral(
        jnp.swapaxes(plus_y, 0, 1),
        jnp.swapaxes(minus_y, 0, 1),
        jnp.swapaxes(y_root, 0, 1),
        below_y,
        above_y,
        SUB_DEV,
    )
    self_z, low_z, high_z = vertical(
        traces(deflation, 2, 3), traces(deflation, 2, 0), z_root, SUB_DEV
    )
    diagonal = volume(deflation, coefficient, gradients, SUB_DEV) + self_x + self_y + self_z
    blocks = jnp.stack([diagonal, low_x, high_x, low_y, high_y, low_z, high_z], axis=1)
    device = (lax.axis_index("row") * N_COL + lax.axis_index("col")).astype(jnp.int32)
    panel = exchange(device, coarse_order, blocks)
    return (blocks.reshape(SUB_DEV, 7, NV * NV), panel)


def solution(mesh):
    in_specs = (
        P("row", "col", None, None),
        P("row", "col", None),
        P(),
        P("row", "col", None),
        P("row", "col", None),
        P("row", "col", None),
        P(),
    )
    out_specs = (P(("row", "col"), None, None), P(("row", "col"), None, None))
    return jax.shard_map(shards, mesh=mesh, in_specs=in_specs, out_specs=out_specs, check_vma=False)
```

```python
import jax
import jax.numpy as jnp
from jax import lax
from jax.experimental import pallas as pl
from jax.experimental.pallas import tpu as pltpu
from jax.sharding import PartitionSpec as P

NV = 48
SUB_DEV = 4
PB = 11
SUBS = 1024
N_ROW = 8
N_COL = 32


LINE_WEIGHTS = (1.0 / 6.0, 5.0 / 6.0, 5.0 / 6.0, 1.0 / 6.0)
COEF, XPEN, YPEN, ZPEN = 0, 16, 40, 58


def fetch(tiles, start, target):
    lane = lax.broadcasted_iota(jnp.int32, tiles[0].shape, 1)
    tile, offset = start // 128, start % 128
    shift = (target - offset) % 128
    first = pltpu.roll(tiles[tile], shift, 1) if shift else tiles[tile]
    if offset + NV <= 128:
        return first
    second = pltpu.roll(tiles[tile + 1], shift, 1) if shift else tiles[tile + 1]
    return jnp.where(lane >= target + 128 - offset, second, first)


def paired(even, odd, start):
    lane = lax.broadcasted_iota(jnp.int32, even[0].shape, 1)
    return jnp.where(lane < 64, fetch(even, start, 0), fetch(odd, start, 64))


def lane_tiles(values):
    wide = values.astype(jnp.float32)
    return [wide[:, 128 * t : 128 * t + 128] for t in range(wide.shape[1] // 128)]


def gram(left, right):
    return lax.dot_general(left, right, (((0,), (0,)), ((), ())), preferred_element_type=jnp.float32)


def assemble_kernel(deflation, gradients, table, main, own_x, own_y, roots_x, roots_y, nodes, sides, stack, total, roots, low_z, other_z):
    rooted = jnp.sqrt(jnp.transpose(table[...]))[:24]
    half = lax.broadcasted_iota(jnp.int32, (24, 128), 1) < 64

    def spread(even, odd):
        left = jnp.broadcast_to(rooted[:, even : even + 1], (24, 128))
        right = jnp.broadcast_to(rooted[:, odd : odd + 1], (24, 128))
        return jnp.where(half, left, right)

    for i in range(4):
        for x in range(2):
            roots[0, i, x] = spread(COEF + 8 * x + 2 * i, COEF + 8 * x + 2 * i + 1)
            roots[1, i, x] = spread(XPEN + 16 * x + 2 * i, XPEN + 16 * x + 2 * i + 1)
            roots[2, i, x] = spread(XPEN + 8 + 2 * i, XPEN + 8 + 2 * i + 1)
            roots[3, i, x] = spread(YPEN + 9 * x + 2 * i + 1, YPEN + 9 * x + 2 * i + 2)
            roots[4, i, x] = spread(ZPEN + 8 * x + 2 * i, ZPEN + 8 * x + 2 * i + 1)
            roots[5, i, x] = jnp.where(half & (i == 0), jnp.broadcast_to(rooted[:, YPEN + 9 * x : YPEN + 9 * x + 1], (24, 128)), 0.0)
            roots_x[x, i] = roots[1, i, x, :16]
    for side in range(2):
        roots_y[side] = spread(YPEN + 8 * side, YPEN + 9 + 8 * side)[:16]

    def relay(i, carry):
        for x in range(2):
            even = lane_tiles(deflation[x, 2 * i])
            odd = lane_tiles(deflation[x, 2 * i + 1])
            for n in range(64):
                a, b, c = n // 16, n // 4 % 4, n % 4
                both = paired(even, odd, NV * n)
                nodes[i, x, pl.ds(n, 16, stride=64), :] = both
                if b % 3 == 0:
                    sides[i, x, b // 3, pl.ds(4 * a + c, 16, stride=16), :] = both
        return carry

    lax.fori_loop(0, 4, relay, 0)
    total[...] = jnp.zeros_like(total)
    node = lax.broadcasted_iota(jnp.int32, (64, 128), 0)

    def edge(position):
        return jnp.where((position == 0) | (position == 3), LINE_WEIGHTS[0], LINE_WEIGHTS[1])

    weight = jnp.sqrt(edge(node // 16) * edge(node // 4 % 4) * edge(node % 4))
    first_half = lax.broadcasted_iota(jnp.int32, (16, 128), 1) < 64

    def part(step, carry):
        s, i = step // 4, step % 4
        low = jnp.bfloat16

        def root(kind, x, z, rows):
            return jnp.broadcast_to(roots[kind, i, x, pl.ds(z, 1), :], (rows, 128))

        inner = []
        for zz in range(4):
            z = 4 * s + zz
            at = pl.ds(pl.multiple_of(64 * z, 64), 64)
            block = [nodes[i, x, at, :] for x in range(2)]
            z_rows = jnp.concatenate(block, axis=1).astype(low)
            product = jnp.dot(gradients[...], z_rows, preferred_element_type=jnp.float32)
            factor_z = jnp.concatenate([weight * root(0, x, z, 64) for x in range(2)], axis=1)
            for d in range(3):
                stack[192 * zz + 64 * d : 192 * zz + 64 * d + 64, :] = (product[64 * d : 64 * d + 64] * factor_z).astype(low)
            near = (block[0][:16] * root(1, 0, z, 16)).astype(low)
            far = (block[1][48:] * root(1, 1, z, 16)).astype(low)
            stack[768 + 16 * zz : 784 + 16 * zz, :] = jnp.concatenate([near, far], axis=1)
            here = pl.ds(pl.multiple_of(16 * z, 16), 16)
            own_x[0, i, here, :] = near
            own_x[1, i, here, :] = far
            inner.append((root(2, 0, z, 16) * (block[0][48:] - block[1][:16])).astype(low))
            lows, jumps = [], []
            after = jnp.minimum(i + 1, 3)
            for x in range(2):
                lower = sides[i, x, 0, here, :]
                swapped = pltpu.roll(lower, 64, 1)
                later = jnp.where(i < 3, pltpu.roll(sides[after, x, 0, here, :], 64, 1), 0.0)
                jumps.append((root(3, x, z, 16) * (sides[i, x, 1, here, :] - jnp.where(first_half, swapped, later))).astype(low))
                lows.append((root(5, x, z, 16) * lower).astype(low))
            stack[864 + 16 * zz : 880 + 16 * zz, :] = jnp.concatenate(jumps, axis=1)
            stack[928 + 16 * zz : 944 + 16 * zz, :] = jnp.concatenate(lows, axis=1)
            ups, firsts, befores = [], [], []
            for x in range(2):
                upper = nodes[i, x, pl.ds(64 * z + 3, 16, stride=4), :]
                if zz < 3:
                    upper = upper - nodes[i, x, pl.ds(64 * z + 64, 16, stride=4), :]
                ups.append((root(4, x, z + 1, 16) * upper).astype(low))
                if zz == 0:
                    firsts.append((root(4, x, z, 16) * nodes[i, x, pl.ds(64 * z, 16, stride=4), :]).astype(low))
                    before = nodes[i, x, pl.ds(64 * jnp.maximum(z - 1, 0) + 3, 16, stride=4), :]
                    befores.append(jnp.where(s > 0, root(4, x, z, 16) * before, 0.0).astype(low))
            stack[992 + 16 * zz : 1008 + 16 * zz, :] = jnp.concatenate(ups, axis=1)
            if zz == 0:
                stack[1056:1072, :] = jnp.concatenate(firsts, axis=1)
                row = pl.ds(pl.multiple_of(16 * i, 16), 16)
                low_z[s, row, :] = jnp.concatenate(firsts, axis=1)
                other_z[s, row, :] = jnp.concatenate(befores, axis=1)
        stack[832:848, :] = jnp.concatenate(inner[:2], axis=1)
        stack[848:864, :] = jnp.concatenate(inner[2:], axis=1)
        total[s] += gram(stack[...], stack[...])
        return carry

    lax.fori_loop(0, 16, part, 0)

    def folded(square):
        return (
            square[:NV, :128]
            + pltpu.roll(square[64 : 64 + NV, :128], 64, 1)
            + square[128 : 128 + NV, 128:]
            + pltpu.roll(square[192 : 192 + NV, 128:], 64, 1)
        )

    for s in range(4):
        main[s, 0] = folded(total[s])
        below = -folded(gram(low_z[s], other_z[s]))
        main[s, 1] = below
        if s:
            main[s - 1, 2] = jnp.transpose(jnp.concatenate([below, jnp.zeros((80, 128), jnp.float32)], axis=0))[:NV]
    main[3, 2] = jnp.zeros((NV, 128), jnp.float32)
    for z in range(16):
        here = slice(16 * z, 16 * z + 16)
        lower = [sides[0, x, 0, here, :] for x in range(2)]
        upper = [sides[3, x, 1, here, :] for x in range(2)]
        near = jnp.where(first_half, lower[0], pltpu.roll(lower[1], 64, 1))
        far = jnp.where(first_half, pltpu.roll(upper[0], 64, 1), upper[1])
        own_y[0, here, :] = (near * jnp.broadcast_to(roots_y[0, z : z + 1, :], (16, 128))).astype(jnp.bfloat16)
        own_y[1, here, :] = (far * jnp.broadcast_to(roots_y[1, z : z + 1, :], (16, 128))).astype(jnp.bfloat16)


def assemble(deflation, gradients, table):
    vmem = pl.BlockSpec(memory_space=pltpu.VMEM)
    f32, low = jnp.float32, jnp.bfloat16
    return pl.pallas_call(
        assemble_kernel,
        out_shape=(
            jax.ShapeDtypeStruct((4, 3, NV, 128), f32),
            jax.ShapeDtypeStruct((2, 4, 256, 128), low),
            jax.ShapeDtypeStruct((2, 256, 128), low),
            jax.ShapeDtypeStruct((2, 4, 16, 128), f32),
            jax.ShapeDtypeStruct((2, 16, 128), f32),
        ),
        in_specs=[vmem] * 3,
        out_specs=(vmem,) * 5,
        scratch_shapes=[
            pltpu.VMEM((4, 2, 1024, 128), f32),
            pltpu.VMEM((4, 2, 2, 256, 128), f32),
            pltpu.VMEM((1072, 256), low),
            pltpu.VMEM((4, 256, 256), f32),
            pltpu.VMEM((6, 4, 2, 24, 128), f32),
            pltpu.VMEM((4, 64, 256), low),
            pltpu.VMEM((4, 64, 256), low),
        ],
        cost_estimate=pl.CostEstimate(flops=2_000_000_000, bytes_accessed=3_000_000, transcendentals=0),
        name="assemble",
    )(deflation, gradients, table)


def lateral_kernel(order, meta, below_x, above_x, below_y, above_y, main, own_x, own_y, roots_x, roots_y, blocks, share, halo_x, halo_y):
    device = meta[0]
    low = jnp.bfloat16
    inside = lax.broadcasted_iota(jnp.int32, (NV, 128), 1) < NV
    for side, source in enumerate((below_x, above_x)):

        def relay(i, carry):
            even = lane_tiles(source[2 * i])
            odd = lane_tiles(source[2 * i + 1])
            for m in range(16):
                halo_x[side, i, pl.ds(m, 16, stride=16), :] = paired(even, odd, NV * m) * roots_x[side, i]
            return carry

        lax.fori_loop(0, 4, relay, 0)
    for side, source in enumerate((below_y, above_y)):
        even = lane_tiles(source[0])
        odd = lane_tiles(source[1])
        for m in range(16):
            n = 16 * (m // 4) + 12 * (1 - side) + m % 4
            halo_y[side, pl.ds(m, 16, stride=16), :] = paired(even, odd, NV * n) * roots_y[side]

    def folded(square):
        return jnp.where(inside, -(square[:NV] + pltpu.roll(square[64 : 64 + NV], 64, 1)), 0.0)

    def flipped(block):
        return jnp.transpose(jnp.concatenate([block, jnp.zeros((80, 128), jnp.float32)], axis=0))[:NV]

    for s in range(SUB_DEV):
        at = slice(64 * s, 64 * s + 64)
        diag = jnp.where(inside, main[s, 0], 0.0)
        low_z = jnp.where(inside, main[s, 1], 0.0)
        blocks[s, 0] = diag
        blocks[s, 5] = low_z
        blocks[s, 6] = jnp.where(inside, main[s, 2], 0.0)
        lower = None
        for side in range(2):
            mine = jnp.concatenate([own_x[side, i, at, :] for i in range(4)], axis=0)
            theirs = jnp.concatenate([halo_x[side, i, at, :].astype(low) for i in range(4)], axis=0)
            blocks[s, 1 + side] = folded(gram(mine, theirs))
            cross = folded(gram(own_y[side, at, :], halo_y[side, at, :].astype(low)))
            blocks[s, 3 + side] = cross
            if side == 0:
                lower = cross
        here = device * SUB_DEV + s
        rank = order[here]
        low_y = jnp.where(rank > order[jnp.maximum(here - SUB_DEV, 0)], lower, flipped(lower))
        low_z = jnp.where(rank > order[jnp.maximum(here - 1, 0)], low_z, flipped(low_z))
        for kind, value in enumerate((diag, low_y, low_z)):
            row = (s % 2) * 3 + kind
            if s < 2:
                share[row] = value
            else:
                share[row] += pltpu.roll(value, 64, 1)


def lateral(order, meta, below_x, above_x, below_y, above_y, main, own_x, own_y, roots_x, roots_y):
    smem = pl.BlockSpec(memory_space=pltpu.SMEM)
    vmem = pl.BlockSpec(memory_space=pltpu.VMEM)
    f32 = jnp.float32
    return pl.pallas_call(
        lateral_kernel,
        out_shape=(
            jax.ShapeDtypeStruct((SUB_DEV, 7, NV, 128), f32),
            jax.ShapeDtypeStruct((6, NV, 128), f32),
        ),
        in_specs=[smem] * 2 + [vmem] * 9,
        out_specs=(vmem, vmem),
        scratch_shapes=[
            pltpu.VMEM((2, 4, 256, 128), f32),
            pltpu.VMEM((2, 256, 128), f32),
        ],
        name="lateral",
    )(order, meta, below_x, above_x, below_y, above_y, main, own_x, own_y, roots_x, roots_y)


def flatten_kernel(blocks, out, turned):
    lane = lax.broadcasted_iota(jnp.int32, (8, 128), 1)
    for s in range(SUB_DEV):
        for kind in range(7):
            turned[s, pl.ds(kind, NV, stride=8), :] = blocks[s, kind]
    for s in range(SUB_DEV):
        for t in range(18):
            value = None
            for v in range(NV):
                shift = NV * v - 128 * t
                if shift <= -NV or shift >= 128:
                    continue
                row = turned[s, 8 * v : 8 * v + 8, :]
                row = pltpu.roll(row, shift % 128, 1) if shift % 128 else row
                here = (lane >= shift) & (lane < shift + NV)
                value = jnp.where(here, row, 0.0 if value is None else value)
            out[s, :, 128 * t : 128 * t + 128] = value[:7]


def flatten(blocks):
    vmem = pl.BlockSpec(memory_space=pltpu.VMEM)
    return pl.pallas_call(
        flatten_kernel,
        out_shape=jax.ShapeDtypeStruct((SUB_DEV, 7, NV * NV), jnp.float32),
        in_specs=[vmem],
        out_specs=vmem,
        scratch_shapes=[pltpu.VMEM((SUB_DEV, NV * 8, 128), jnp.float32)],
        cost_estimate=pl.CostEstimate(flops=1_000_000, bytes_accessed=2_000_000, transcendentals=0),
        name="flatten",
    )(blocks)


def eliminate(work):
    groups = [work[8 * v : 8 * v + 8] for v in range(6)]
    sub = lax.broadcasted_iota(jnp.int32, (8, 128), 0)
    scales = []
    for g in range(6):
        splat = [
            [jnp.broadcast_to(groups[v][:, 64 + 8 * g + k : 65 + 8 * g + k], (8, 128)) for v in range(g, 6)]
            for k in range(8)
        ]
        head = groups[g]
        scale = jnp.zeros((8, 128), jnp.float32)
        for k in range(8):
            pivot = jnp.broadcast_to(splat[k][0][k : k + 1, :], (8, 128))
            inverse = 1.0 / pivot
            scale = jnp.where(sub == k, lax.rsqrt(pivot), scale)
            factors = [c * inverse for c in splat[k]]
            factors[0] = jnp.where(sub > k, factors[0], 0.0)
            for m in range(k + 1, 8):
                upper = jnp.broadcast_to(splat[m][0][k : k + 1, :], (8, 128))
                splat[m] = [c - f * upper for c, f in zip(splat[m], factors)]
            row = jnp.broadcast_to(head[k : k + 1, :], (8, 128))
            head = head - factors[0] * row
            for v in range(g + 1, 6):
                groups[v] = groups[v] - factors[v - g] * row
        groups[g] = head
        scales.append(scale)
    return jnp.concatenate([a * b for a, b in zip(groups, scales)], axis=0)


def halves(values):
    high = values.astype(jnp.bfloat16)
    low = (values - high.astype(jnp.float32)).astype(jnp.bfloat16)
    return high, low


def across(left, right):
    return lax.dot_general(left, right, (((1,), (1,)), ((), ())), preferred_element_type=jnp.float32)


def factor_kernel(order, meta, own, below, above, extra, blocks, out, grid, got, got_x, lhs, rhs, sems):
    device = meta[0]
    lane = lax.broadcasted_iota(jnp.int32, (NV, 128), 1)

    def place(value, half, row, column):
        parity = column % 2
        shift = 64 * ((parity + half) % 2)
        moved = pltpu.roll(value, shift, 1)
        inside = (lane >= 64 * parity) & (lane < 64 * parity + NV)
        at = pl.ds(pl.multiple_of(row, 16), NV)
        grid[column // 2, at, :] += jnp.where(inside, moved, 0.0)

    def ordered(subdomain):
        return order[jnp.clip(subdomain, 0, SUBS - 1)]

    def neighbours(subdomain):
        column = (subdomain // SUB_DEV) % N_COL
        local = subdomain % SUB_DEV
        stride = N_COL * SUB_DEV
        return (
            (subdomain, subdomain >= 0),
            (subdomain - stride, subdomain >= stride),
            (subdomain + stride, subdomain < SUBS - stride),
            (subdomain - SUB_DEV, column > 0),
            (subdomain + SUB_DEV, column < N_COL - 1),
            (subdomain - 1, local > 0),
            (subdomain + 1, local < SUB_DEV - 1),
        )

    relevant = jnp.int32(0)
    for l in range(SUB_DEV):
        for near, there in neighbours(device * SUB_DEV + l):
            relevant += (there & (ordered(near) < PB)).astype(jnp.int32)

    @pl.when(relevant == 0)
    def _():
        out[...] = jnp.zeros_like(out)

    @pl.when(relevant > 0)
    def _():
        for index, source in enumerate((own, below, above)):

            @pl.when(meta[1] == index)
            def _():
                pltpu.make_async_copy(source, got, sems.at[0]).start()

        pltpu.make_async_copy(extra, got_x, sems.at[1]).start()
        grid[...] = jnp.zeros_like(grid)
        rhs[...] = jnp.zeros_like(rhs)
        for l in range(SUB_DEV):
            for kind, (near, there) in enumerate(neighbours(device * SUB_DEV + l)):
                column = ordered(near)

                @pl.when(there & (column < PB))
                def _():
                    place(blocks[l, kind], 0, PB * NV + NV * l, column)

        pltpu.make_async_copy(own, got, sems.at[0]).wait()
        pltpu.make_async_copy(extra, got_x, sems.at[1]).wait()
        for slot in range(12):
            i, l = slot // SUB_DEV, slot % SUB_DEV
            s = meta[4 + slot]
            p = ordered(s)
            near = neighbours(s)
            for kind, (t, there) in enumerate((near[0], near[3], near[5], near[1])):
                q = ordered(t)

                @pl.when((s >= 0) & there & (p < PB) & (q < PB))
                def _():
                    if kind < 3:
                        value, half = got[i, (l % 2) * 3 + kind], l // 2
                    else:
                        value, half = got_x[slot % 6], slot // 6
                    place(value, half, NV * jnp.maximum(p, q), jnp.minimum(p, q))

        rows48 = lax.broadcasted_iota(jnp.int32, (NV, 128), 0)

        def step(k, carry):
            tile = k // 2
            parity = k % 2
            at = pl.ds(pl.multiple_of(k * NV, 16), NV)
            diag = pltpu.roll(grid[tile, at, :], 64 * (1 - parity), 1)
            work = jnp.where(lane < 64, (lane == rows48).astype(jnp.float32), jnp.where(lane < 64 + NV, diag, 0.0))
            inverse = jnp.where(lane < NV, eliminate(work), 0.0)
            inverse = pltpu.roll(inverse, 64 * parity, 1)
            gap = jnp.zeros((16, 128), jnp.float32)
            b_high, b_low = halves(jnp.concatenate([inverse, gap, inverse, gap], axis=0))
            column = grid[tile]
            c_high, c_low = halves(column)
            solved = across(jnp.concatenate([c_high, c_low], axis=1), jnp.concatenate([b_high, b_high], axis=1)) + across(c_high, b_low)
            lane_all = lax.broadcasted_iota(jnp.int32, solved.shape, 1)
            row_all = lax.broadcasted_iota(jnp.int32, solved.shape, 0) - k * NV
            keep = (row_all >= NV) | ((lane_all % 64) <= row_all)
            solved = jnp.where(keep, solved, 0.0)
            grid[tile] = jnp.where(lane_all // 64 == parity, solved, column)
            s_high, s_low = halves(solved)
            lhs[:, :128] = s_high
            lhs[:, 128:] = s_low
            mixed = jnp.where(lane_all < 64, s_high.astype(jnp.float32), s_low.astype(jnp.float32)).astype(jnp.bfloat16)
            for i in range(PB):
                rhs[64 * i : 64 * i + NV, :] = jnp.where(i > k, mixed[NV * i : NV * i + NV], jnp.zeros((NV, 128), jnp.bfloat16))

            def trail(t, c):
                other = rhs[pl.ds(pl.multiple_of(128 * t, 128), 128), :]
                grid[t] -= across(lhs[...], jnp.concatenate([other, other], axis=1))
                return c

            lax.fori_loop((k + 1) // 2, 6, trail, 0)
            return carry

        lax.fori_loop(0, PB, step, 0)
        for l in range(SUB_DEV):
            p = ordered(device * SUB_DEV + l)
            inside = p < PB
            start = jnp.where(inside, NV * p, PB * NV + NV * l)
            at = pl.ds(pl.multiple_of(start, 16), NV)
            pieces = []
            for j in range(PB):
                piece = grid[j // 2, at, :][:, 64 * (j % 2) : 64 * (j % 2) + NV]
                pieces.append(jnp.where(inside & (j > p), 0.0, piece))
            out[l] = jnp.concatenate(pieces, axis=1)


def factor(order, meta, own, below, above, extra, blocks):
    smem = pl.BlockSpec(memory_space=pltpu.SMEM)
    hbm = pl.BlockSpec(memory_space=pl.ANY)
    vmem = pl.BlockSpec(memory_space=pltpu.VMEM)
    return pl.pallas_call(
        factor_kernel,
        out_shape=jax.ShapeDtypeStruct((SUB_DEV, NV, PB * NV), jnp.float32),
        in_specs=[smem, smem, hbm, hbm, hbm, hbm, vmem],
        out_specs=vmem,
        scratch_shapes=[
            pltpu.VMEM((6, PB * NV + SUB_DEV * NV, 128), jnp.float32),
            pltpu.VMEM((3, 6, NV, 128), jnp.float32),
            pltpu.VMEM((6, NV, 128), jnp.float32),
            pltpu.VMEM((PB * NV + SUB_DEV * NV, 256), jnp.bfloat16),
            pltpu.VMEM((12 * 64, 128), jnp.bfloat16),
            pltpu.SemaphoreType.DMA((2,)),
        ],
        name="factor",
    )(order, meta, own, below, above, extra, blocks)


def shifted(value, amount):
    size = N_ROW * N_COL
    return lax.ppermute(value, ("row", "col"), [(i, (i + amount) % size) for i in range(size)])


def packed(blocks):
    wide = jnp.pad(blocks, ((0, 0), (0, 0), (0, 64 - NV)))
    return jnp.concatenate([wide[:6], wide[6:]], axis=2)


def everywhere(value):
    size = N_ROW * N_COL
    step = 1
    while step < size:
        value = value + lax.ppermute(value, ("row", "col"), [(i, i ^ step) for i in range(size)])
        step *= 2
    return value


def exchange(device, order, blocks, share):
    subdomain = jnp.arange(SUBS, dtype=jnp.int32)
    first = jnp.sum(jnp.where(order == 0, subdomain // SUB_DEV, 0))
    size = N_ROW * N_COL
    distance = (subdomain // SUB_DEV - first + size // 2) % size - size // 2
    inside = order < PB
    least = jnp.min(jnp.where(inside, distance, size))
    most = jnp.max(jnp.where(inside, distance, -size))
    near = (most - least) <= 2
    base = (first + least) % size
    mine = device * SUB_DEV + jnp.arange(SUB_DEV, dtype=jnp.int32)
    my_order = lax.dynamic_slice(order, (device * SUB_DEV,), (SUB_DEV,))

    right1 = shifted(share, 1)
    left1 = shifted(share, -1)
    right2 = shifted(right1, 1)
    left2 = shifted(left1, -1)
    offset = (base - device + size // 2) % size - size // 2
    middle = jnp.stack([right2, right1, share, left1, left2])
    window = lax.dynamic_slice(middle, (jnp.clip(offset + 2, 0, 2), 0, 0, 0), (3,) + share.shape)
    below = shifted(window, N_COL)
    above = shifted(window, -N_COL)
    right3 = shifted(right2, 1)
    left3 = shifted(left2, -1)
    ends = jnp.where(offset < 0, jnp.stack([right3, right2, right1]), jnp.stack([left1, left2, left3]))
    window = jnp.where((offset >= -2) & (offset <= 0), window, ends)
    from_below = (offset + N_COL + 2) % size <= 2
    from_above = (offset - N_COL + 2) % size <= 2
    flat = (offset >= -3) & (offset <= 1)
    pick = jnp.where(flat, 0, jnp.where(from_below, 1, jnp.where(from_above, 2, 0)))

    def local_path(_):
        listed = (base * SUB_DEV + jnp.arange(12, dtype=jnp.int32)) % SUBS
        return (window, jnp.zeros((6, NV, 128), jnp.float32), listed, pick)

    def global_path(_):
        slots = jnp.arange(12, dtype=jnp.int32)
        hit = (order[None, :] == slots[:, None]) & (slots[:, None] < PB)
        listed = jnp.where(slots < PB, jnp.sum(jnp.where(hit, subdomain[None, :], 0), axis=1), -1)
        mask = ((my_order[None, :] == slots[:, None]) & (slots[:, None] < PB)).astype(jnp.float32)
        def oriented(block, offset):
            other = lax.dynamic_slice(jnp.concatenate([order[:128], order]), (128 + device * SUB_DEV - offset,), (SUB_DEV,))
            return jnp.where((my_order > other)[:, None, None], block, jnp.swapaxes(block, 1, 2))

        kinds = jnp.stack(
            [
                blocks[:, 0, :, :NV],
                oriented(blocks[:, 3, :, :NV], SUB_DEV),
                oriented(blocks[:, 5, :, :NV], 1),
                oriented(blocks[:, 1, :, :NV], N_COL * SUB_DEV),
            ],
            axis=1,
        )
        placed = jnp.einsum("ps,skvw->pkvw", mask, kinds, precision=lax.Precision.HIGHEST)
        whole = everywhere(
            jnp.stack([packed(placed[4 * i : 4 * i + 4, :3].reshape(12, NV, NV)) for i in range(3)] + [packed(placed[:, 3])])
        )
        return (whole[:3], whole[3], listed, jnp.int32(0))

    window, extra, listed, pick = lax.cond(near, local_path, global_path, None)
    meta = jnp.concatenate([jnp.stack([device, pick, jnp.int32(0), jnp.int32(0)]), listed]).astype(jnp.int32)
    return factor(order, meta, window, below, above, extra, blocks)


def from_next(value, axis, amount):
    size = lax.axis_size(axis)
    pairs = [(i, i + amount) for i in range(size) if 0 <= i + amount < size]
    return lax.ppermute(value, axis, pairs)


def shards(deflation, coefficient, gradients, x_penalty, y_penalty, z_penalty, coarse_order):
    device = (lax.axis_index("row") * N_COL + lax.axis_index("col")).astype(jnp.int32)
    below_x = from_next(deflation[1, :, :, 48 * NV :], "row", 1)
    above_x = from_next(deflation[0, :, :, : 16 * NV], "row", -1)
    below_y = from_next(deflation[:, 7], "col", 1)
    above_y = from_next(deflation[:, 0], "col", -1)
    flat = jnp.concatenate([coefficient.reshape(16, 16), x_penalty.reshape(24, 16), y_penalty.reshape(18, 16)], axis=0)
    table = jnp.concatenate([jnp.pad(flat, ((0, 0), (0, 112))), jnp.pad(z_penalty.reshape(16, 17), ((0, 54), (0, 111)))], axis=0)
    main, own_x, own_y, roots_x, roots_y = assemble(deflation, gradients.reshape(192, 64), table)
    meta = jnp.full((8,), device, jnp.int32)
    blocks, share = lateral(coarse_order, meta, below_x, above_x, below_y, above_y, main, own_x, own_y, roots_x, roots_y)
    panel = exchange(device, coarse_order, blocks, share)
    return (flatten(blocks), panel)


def solution(mesh):
    in_specs = (
        P("row", "col", None, None),
        P("row", "col", None),
        P(),
        P("row", "col", None),
        P("row", "col", None),
        P("row", "col", None),
        P(),
    )
    out_specs = (P(("row", "col"), None, None), P(("row", "col"), None, None))
    return jax.shard_map(shards, mesh=mesh, in_specs=in_specs, out_specs=out_specs, check_vma=False)
```

```python
import jax
import jax.numpy as jnp
from jax import lax
from jax.experimental import pallas as pl
from jax.experimental.pallas import tpu as pltpu
from jax.sharding import PartitionSpec as P

NV = 48
SUB_DEV = 4
PB = 11
SUBS = 1024
N_ROW = 8
N_COL = 32


LINE_WEIGHTS = (1.0 / 6.0, 5.0 / 6.0, 5.0 / 6.0, 1.0 / 6.0)
COEF, XPEN, YPEN, ZPEN = 0, 16, 40, 58


def fetch(tiles, start, target):
    lane = lax.broadcasted_iota(jnp.int32, tiles[0].shape, 1)
    tile, offset = start // 128, start % 128
    shift = (target - offset) % 128
    first = pltpu.roll(tiles[tile], shift, 1) if shift else tiles[tile]
    if offset + NV <= 128:
        return first
    second = pltpu.roll(tiles[tile + 1], shift, 1) if shift else tiles[tile + 1]
    return jnp.where(lane >= target + 128 - offset, second, first)


def paired(even, odd, start):
    lane = lax.broadcasted_iota(jnp.int32, even[0].shape, 1)
    return jnp.where(lane < 64, fetch(even, start, 0), fetch(odd, start, 64))


def lane_tiles(values):
    wide = values.astype(jnp.float32)
    return [wide[:, 128 * t : 128 * t + 128] for t in range(wide.shape[1] // 128)]


def gram(left, right):
    return lax.dot_general(left, right, (((0,), (0,)), ((), ())), preferred_element_type=jnp.float32)


def assemble_kernel(deflation, gradients, table, main, own_x, own_y, roots_x, roots_y, nodes, sides, stack, total, roots, low_z, other_z):
    rooted = jnp.sqrt(jnp.transpose(table[...]))[:24]
    half = lax.broadcasted_iota(jnp.int32, (24, 128), 1) < 64

    def spread(even, odd):
        left = jnp.broadcast_to(rooted[:, even : even + 1], (24, 128))
        right = jnp.broadcast_to(rooted[:, odd : odd + 1], (24, 128))
        return jnp.where(half, left, right)

    for i in range(4):
        for x in range(2):
            roots[0, i, x] = spread(COEF + 8 * x + 2 * i, COEF + 8 * x + 2 * i + 1)
            roots[1, i, x] = spread(XPEN + 16 * x + 2 * i, XPEN + 16 * x + 2 * i + 1)
            roots[2, i, x] = spread(XPEN + 8 + 2 * i, XPEN + 8 + 2 * i + 1)
            roots[3, i, x] = spread(YPEN + 9 * x + 2 * i + 1, YPEN + 9 * x + 2 * i + 2)
            roots[4, i, x] = spread(ZPEN + 8 * x + 2 * i, ZPEN + 8 * x + 2 * i + 1)
            roots[5, i, x] = jnp.where(half & (i == 0), jnp.broadcast_to(rooted[:, YPEN + 9 * x : YPEN + 9 * x + 1], (24, 128)), 0.0)
            roots_x[x, i] = roots[1, i, x, :16]
    for side in range(2):
        roots_y[side] = spread(YPEN + 8 * side, YPEN + 9 + 8 * side)[:16]

    def relay(i, carry):
        for x in range(2):
            even = lane_tiles(deflation[x, 2 * i])
            odd = lane_tiles(deflation[x, 2 * i + 1])
            for n in range(64):
                a, b, c = n // 16, n // 4 % 4, n % 4
                both = paired(even, odd, NV * n)
                nodes[i, x, pl.ds(n, 16, stride=64), :] = both
                if b % 3 == 0:
                    sides[i, x, b // 3, pl.ds(4 * a + c, 16, stride=16), :] = both
        return carry

    lax.fori_loop(0, 4, relay, 0)
    total[...] = jnp.zeros_like(total)
    node = lax.broadcasted_iota(jnp.int32, (64, 128), 0)

    def edge(position):
        return jnp.where((position == 0) | (position == 3), LINE_WEIGHTS[0], LINE_WEIGHTS[1])

    weight = jnp.sqrt(edge(node // 16) * edge(node // 4 % 4) * edge(node % 4))
    first_half = lax.broadcasted_iota(jnp.int32, (16, 128), 1) < 64

    def part(step, carry):
        s, i = step // 4, step % 4
        low = jnp.bfloat16

        def root(kind, x, z, rows):
            return jnp.broadcast_to(roots[kind, i, x, pl.ds(z, 1), :], (rows, 128))

        inner = []
        for zz in range(4):
            z = 4 * s + zz
            at = pl.ds(pl.multiple_of(64 * z, 64), 64)
            block = [nodes[i, x, at, :] for x in range(2)]
            z_rows = jnp.concatenate(block, axis=1).astype(low)
            product = jnp.dot(gradients[...], z_rows, preferred_element_type=jnp.float32)
            factor_z = jnp.concatenate([weight * root(0, x, z, 64) for x in range(2)], axis=1)
            for d in range(3):
                stack[192 * zz + 64 * d : 192 * zz + 64 * d + 64, :] = (product[64 * d : 64 * d + 64] * factor_z).astype(low)
            near = (block[0][:16] * root(1, 0, z, 16)).astype(low)
            far = (block[1][48:] * root(1, 1, z, 16)).astype(low)
            stack[768 + 16 * zz : 784 + 16 * zz, :] = jnp.concatenate([near, far], axis=1)
            here = pl.ds(pl.multiple_of(16 * z, 16), 16)
            own_x[0, i, here, :] = near
            own_x[1, i, here, :] = far
            inner.append((root(2, 0, z, 16) * (block[0][48:] - block[1][:16])).astype(low))
            lows, jumps = [], []
            after = jnp.minimum(i + 1, 3)
            for x in range(2):
                lower = sides[i, x, 0, here, :]
                swapped = pltpu.roll(lower, 64, 1)
                later = jnp.where(i < 3, pltpu.roll(sides[after, x, 0, here, :], 64, 1), 0.0)
                jumps.append((root(3, x, z, 16) * (sides[i, x, 1, here, :] - jnp.where(first_half, swapped, later))).astype(low))
                lows.append((root(5, x, z, 16) * lower).astype(low))
            stack[864 + 16 * zz : 880 + 16 * zz, :] = jnp.concatenate(jumps, axis=1)
            stack[928 + 16 * zz : 944 + 16 * zz, :] = jnp.concatenate(lows, axis=1)
            ups, firsts, befores = [], [], []
            for x in range(2):
                upper = nodes[i, x, pl.ds(64 * z + 3, 16, stride=4), :]
                if zz < 3:
                    upper = upper - nodes[i, x, pl.ds(64 * z + 64, 16, stride=4), :]
                ups.append((root(4, x, z + 1, 16) * upper).astype(low))
                if zz == 0:
                    firsts.append((root(4, x, z, 16) * nodes[i, x, pl.ds(64 * z, 16, stride=4), :]).astype(low))
                    before = nodes[i, x, pl.ds(64 * jnp.maximum(z - 1, 0) + 3, 16, stride=4), :]
                    befores.append(jnp.where(s > 0, root(4, x, z, 16) * before, 0.0).astype(low))
            stack[992 + 16 * zz : 1008 + 16 * zz, :] = jnp.concatenate(ups, axis=1)
            if zz == 0:
                stack[1056:1072, :] = jnp.concatenate(firsts, axis=1)
                row = pl.ds(pl.multiple_of(16 * i, 16), 16)
                low_z[s, row, :] = jnp.concatenate(firsts, axis=1)
                other_z[s, row, :] = jnp.concatenate(befores, axis=1)
        stack[832:848, :] = jnp.concatenate(inner[:2], axis=1)
        stack[848:864, :] = jnp.concatenate(inner[2:], axis=1)
        total[s] += gram(stack[...], stack[...])
        return carry

    lax.fori_loop(0, 16, part, 0)

    def folded(square):
        return (
            square[:NV, :128]
            + pltpu.roll(square[64 : 64 + NV, :128], 64, 1)
            + square[128 : 128 + NV, 128:]
            + pltpu.roll(square[192 : 192 + NV, 128:], 64, 1)
        )

    for s in range(4):
        main[s, 0] = folded(total[s])
        below = -folded(gram(low_z[s], other_z[s]))
        main[s, 1] = below
        if s:
            main[s - 1, 2] = jnp.transpose(jnp.concatenate([below, jnp.zeros((80, 128), jnp.float32)], axis=0))[:NV]
    main[3, 2] = jnp.zeros((NV, 128), jnp.float32)
    for z in range(16):
        here = slice(16 * z, 16 * z + 16)
        lower = [sides[0, x, 0, here, :] for x in range(2)]
        upper = [sides[3, x, 1, here, :] for x in range(2)]
        near = jnp.where(first_half, lower[0], pltpu.roll(lower[1], 64, 1))
        far = jnp.where(first_half, pltpu.roll(upper[0], 64, 1), upper[1])
        own_y[0, here, :] = (near * jnp.broadcast_to(roots_y[0, z : z + 1, :], (16, 128))).astype(jnp.bfloat16)
        own_y[1, here, :] = (far * jnp.broadcast_to(roots_y[1, z : z + 1, :], (16, 128))).astype(jnp.bfloat16)


def assemble(deflation, gradients, table):
    vmem = pl.BlockSpec(memory_space=pltpu.VMEM)
    f32, low = jnp.float32, jnp.bfloat16
    return pl.pallas_call(
        assemble_kernel,
        out_shape=(
            jax.ShapeDtypeStruct((4, 3, NV, 128), f32),
            jax.ShapeDtypeStruct((2, 4, 256, 128), low),
            jax.ShapeDtypeStruct((2, 256, 128), low),
            jax.ShapeDtypeStruct((2, 4, 16, 128), f32),
            jax.ShapeDtypeStruct((2, 16, 128), f32),
        ),
        in_specs=[vmem] * 3,
        out_specs=(vmem,) * 5,
        scratch_shapes=[
            pltpu.VMEM((4, 2, 1024, 128), f32),
            pltpu.VMEM((4, 2, 2, 256, 128), f32),
            pltpu.VMEM((1072, 256), low),
            pltpu.VMEM((4, 256, 256), f32),
            pltpu.VMEM((6, 4, 2, 24, 128), f32),
            pltpu.VMEM((4, 64, 256), low),
            pltpu.VMEM((4, 64, 256), low),
        ],
        cost_estimate=pl.CostEstimate(flops=2_000_000_000, bytes_accessed=3_000_000, transcendentals=0),
        name="assemble",
    )(deflation, gradients, table)


def lateral_kernel(order, meta, below_x, above_x, below_y, above_y, main, own_x, own_y, roots_x, roots_y, blocks, share, halo_x, halo_y):
    device = meta[0]
    low = jnp.bfloat16
    inside = lax.broadcasted_iota(jnp.int32, (NV, 128), 1) < NV
    for side, source in enumerate((below_x, above_x)):

        def relay(i, carry):
            even = lane_tiles(source[2 * i])
            odd = lane_tiles(source[2 * i + 1])
            for m in range(16):
                halo_x[side, i, pl.ds(m, 16, stride=16), :] = paired(even, odd, NV * m) * roots_x[side, i]
            return carry

        lax.fori_loop(0, 4, relay, 0)
    for side, source in enumerate((below_y, above_y)):
        even = lane_tiles(source[0])
        odd = lane_tiles(source[1])
        for m in range(16):
            n = 16 * (m // 4) + 12 * (1 - side) + m % 4
            halo_y[side, pl.ds(m, 16, stride=16), :] = paired(even, odd, NV * n) * roots_y[side]

    def folded(square):
        return jnp.where(inside, -(square[:NV] + pltpu.roll(square[64 : 64 + NV], 64, 1)), 0.0)

    def flipped(block):
        return jnp.transpose(jnp.concatenate([block, jnp.zeros((80, 128), jnp.float32)], axis=0))[:NV]

    for s in range(SUB_DEV):
        at = slice(64 * s, 64 * s + 64)
        diag = jnp.where(inside, main[s, 0], 0.0)
        low_z = jnp.where(inside, main[s, 1], 0.0)
        blocks[s, 0] = diag
        blocks[s, 5] = low_z
        blocks[s, 6] = jnp.where(inside, main[s, 2], 0.0)
        lower = None
        for side in range(2):
            mine = jnp.concatenate([own_x[side, i, at, :] for i in range(4)], axis=0)
            theirs = jnp.concatenate([halo_x[side, i, at, :].astype(low) for i in range(4)], axis=0)
            blocks[s, 1 + side] = folded(gram(mine, theirs))
            cross = folded(gram(own_y[side, at, :], halo_y[side, at, :].astype(low)))
            blocks[s, 3 + side] = cross
            if side == 0:
                lower = cross
        here = device * SUB_DEV + s
        rank = order[here]
        low_y = jnp.where(rank > order[jnp.maximum(here - SUB_DEV, 0)], lower, flipped(lower))
        low_z = jnp.where(rank > order[jnp.maximum(here - 1, 0)], low_z, flipped(low_z))
        for kind, value in enumerate((diag, low_y, low_z)):
            row = (s % 2) * 3 + kind
            if s < 2:
                share[row] = value
            else:
                share[row] += pltpu.roll(value, 64, 1)


def lateral(order, meta, below_x, above_x, below_y, above_y, main, own_x, own_y, roots_x, roots_y):
    smem = pl.BlockSpec(memory_space=pltpu.SMEM)
    vmem = pl.BlockSpec(memory_space=pltpu.VMEM)
    f32 = jnp.float32
    return pl.pallas_call(
        lateral_kernel,
        out_shape=(
            jax.ShapeDtypeStruct((SUB_DEV, 7, NV, 128), f32),
            jax.ShapeDtypeStruct((6, NV, 128), f32),
        ),
        in_specs=[smem] * 2 + [vmem] * 9,
        out_specs=(vmem, vmem),
        scratch_shapes=[
            pltpu.VMEM((2, 4, 256, 128), f32),
            pltpu.VMEM((2, 256, 128), f32),
        ],
        name="lateral",
    )(order, meta, below_x, above_x, below_y, above_y, main, own_x, own_y, roots_x, roots_y)


def flatten_kernel(blocks, out, turned):
    lane = lax.broadcasted_iota(jnp.int32, (8, 128), 1)
    for s in range(SUB_DEV):
        for kind in range(7):
            turned[s, pl.ds(kind, NV, stride=8), :] = blocks[s, kind]
    for s in range(SUB_DEV):
        for t in range(18):
            value = None
            for v in range(NV):
                shift = NV * v - 128 * t
                if shift <= -NV or shift >= 128:
                    continue
                row = turned[s, 8 * v : 8 * v + 8, :]
                row = pltpu.roll(row, shift % 128, 1) if shift % 128 else row
                here = (lane >= shift) & (lane < shift + NV)
                value = jnp.where(here, row, 0.0 if value is None else value)
            out[s, :, 128 * t : 128 * t + 128] = value[:7]


def flatten(blocks):
    vmem = pl.BlockSpec(memory_space=pltpu.VMEM)
    return pl.pallas_call(
        flatten_kernel,
        out_shape=jax.ShapeDtypeStruct((SUB_DEV, 7, NV * NV), jnp.float32),
        in_specs=[vmem],
        out_specs=vmem,
        scratch_shapes=[pltpu.VMEM((SUB_DEV, NV * 8, 128), jnp.float32)],
        cost_estimate=pl.CostEstimate(flops=1_000_000, bytes_accessed=2_000_000, transcendentals=0),
        name="flatten",
    )(blocks)


def eliminate(work, unit):
    groups = [work[8 * v : 8 * v + 8] for v in range(6)]
    sub = lax.broadcasted_iota(jnp.int32, (8, 128), 0)

    def row_of(value, k):
        return jnp.broadcast_to(value[k : k + 1, :], (8, 128))

    def column_of(value, k):
        return jnp.broadcast_to(value[:, k : k + 1], (8, 128))

    for g in range(6):
        head = groups[g]
        splat = [column_of(head, 64 + 8 * g + k) * unit for k in range(8)]
        below = [[column_of(groups[v], 64 + 8 * g + k) for k in range(8)] for v in range(g + 1, 6)]
        done = jnp.zeros((8, 128), jnp.float32)
        for k in range(0, 8, 2):
            x, y = splat[k], splat[k + 1]
            a, b, c = row_of(x, k), row_of(y, k), row_of(y, k + 1)
            inverse = 1.0 / (a * c - b * b)
            ratio = b / a
            top, low = row_of(head, k), row_of(head, k + 1)
            done = jnp.where(sub == k, top * lax.rsqrt(a), done)
            done = jnp.where(sub == k + 1, (low - ratio * top) * lax.rsqrt(c - ratio * b), done)

            def reduced(value, upper, lower):
                one = (c * upper - b * lower) * inverse
                two = (a * lower - b * upper) * inverse
                return jnp.where(sub == k, one, jnp.where(sub == k + 1, two, value - x * one - y * two))

            for m in range(k + 2, 8):
                splat[m] = reduced(splat[m], row_of(splat[m], k), row_of(splat[m], k + 1))
            head = reduced(head, top, low)
        rows = [row_of(head, k) for k in range(8)]
        for v in range(g + 1, 6):
            terms = [s * r for s, r in zip(below[v - g - 1], rows)]
            while len(terms) > 1:
                terms = [p + q for p, q in zip(terms[::2], terms[1::2])]
            groups[v] = groups[v] - terms[0]
        groups[g] = done
    return jnp.concatenate(groups, axis=0)


def halves(values):
    high = values.astype(jnp.bfloat16)
    low = (values - high.astype(jnp.float32)).astype(jnp.bfloat16)
    return high, low


def across(left, right):
    return lax.dot_general(left, right, (((1,), (1,)), ((), ())), preferred_element_type=jnp.float32)


ROWS = SUB_DEV * NV
BAND = 4


def factor_kernel(order, meta, own, right1, right2, right3, left1, left2, left3, below, above, rescue, blocks, out, grid, got, lhs, rhs, sems):
    device = meta[0]
    lane = lax.broadcasted_iota(jnp.int32, (NV, 128), 1)

    def place(value, half, row, column, wanted):
        parity = column % 2
        moved = pltpu.roll(value, 64 * ((parity + half) % 2), 1)
        inside = (lane >= 64 * parity) & (lane < 64 * parity + NV)
        tile = jnp.where(wanted, column // 2, 7)
        at = pl.ds(pl.multiple_of(jnp.where(wanted, row, 0), 16), NV)
        pltpu.store(grid.at[tile, at, :], moved, mask=inside)

    def ordered(subdomain):
        return order[jnp.clip(subdomain, 0, SUBS - 1)]

    def neighbours(subdomain):
        column = (subdomain // SUB_DEV) % N_COL
        local = subdomain % SUB_DEV
        stride = N_COL * SUB_DEV
        return (
            (subdomain, subdomain >= 0),
            (subdomain - stride, subdomain >= stride),
            (subdomain + stride, (subdomain >= 0) & (subdomain < SUBS - stride)),
            (subdomain - SUB_DEV, (subdomain >= 0) & (column > 0)),
            (subdomain + SUB_DEV, (subdomain >= 0) & (column < N_COL - 1)),
            (subdomain - 1, (subdomain >= 0) & (local > 0)),
            (subdomain + 1, (subdomain >= 0) & (local < SUB_DEV - 1)),
        )

    relevant = jnp.int32(0)
    for l in range(SUB_DEV):
        for near, there in neighbours(device * SUB_DEV + l):
            relevant += (there & (ordered(near) < PB)).astype(jnp.int32)

    @pl.when(relevant == 0)
    def _():
        out[...] = jnp.zeros_like(out)

    @pl.when(relevant > 0)
    def _():
        near_sources = [right3, right2, right1, own, left1, left2, left3]
        for case in range(5):

            @pl.when(meta[1] == case)
            def _():
                for i in range(3):
                    pltpu.make_async_copy(near_sources[case + i], got.at[i], sems.at[i]).start()

        for case, source in ((5, below), (6, above), (7, rescue)):

            @pl.when(meta[1] == case)
            def _():
                for i in range(3):
                    pltpu.make_async_copy(source.at[i], got.at[i], sems.at[i]).start()

        pltpu.make_async_copy(rescue.at[3], got.at[3], sems.at[3]).start()
        grid[:6, : ROWS + PB * NV + BAND * NV, :] = jnp.zeros((6, ROWS + PB * NV + BAND * NV, 128), jnp.float32)
        rhs[...] = jnp.zeros_like(rhs)
        lhs[...] = jnp.zeros_like(lhs)
        for l in range(SUB_DEV):
            for kind, (near, there) in enumerate(neighbours(device * SUB_DEV + l)):
                column = ordered(near)
                place(blocks[l, kind], 0, NV * l, column, there & (column < PB))
        for i in range(4):
            pltpu.make_async_copy(rescue.at[3], got.at[i], sems.at[i]).wait()
        reach = jnp.int32(0)
        for slot in range(12):
            i, l = slot // SUB_DEV, slot % SUB_DEV
            s = meta[4 + slot]
            p = ordered(s)
            near = neighbours(s)
            for kind, (t, there) in enumerate((near[0], near[3], near[5], near[1])):
                q = ordered(t)
                wanted = there & (p < PB) & (q < PB)
                reach = jnp.maximum(reach, jnp.where(wanted, jnp.abs(p - q), 0))
                if kind < 3:
                    value, half = got[i, (l % 2) * 3 + kind], l // 2
                else:
                    value, half = got[3, slot % 6], slot // 6
                place(value, half, ROWS + NV * jnp.maximum(p, q), jnp.minimum(p, q), wanted)

        rows48 = lax.broadcasted_iota(jnp.int32, (NV, 128), 0)

        unit = jnp.full((8, 128), jnp.where(device >= 0, 1.0, 0.0), jnp.float32)

        def step(band, k, deferred):
            tile = k // 2
            parity = k % 2
            depth = ROWS + band * NV
            window = pl.ds(pl.multiple_of(ROWS + k * NV, 16), NV + band * NV)
            later = pl.ds(pl.multiple_of(ROWS + (k + 1) * NV, 16), band * NV)
            at = pl.ds(pl.multiple_of(ROWS + k * NV, 16), NV)
            diag = pltpu.roll(grid[tile, at, :], 64 * (1 - parity), 1)
            deferred()
            work = jnp.where(lane < 64, (lane == rows48).astype(jnp.float32), jnp.where(lane < 64 + NV, diag, 0.0))
            inverse = jnp.where(lane < NV, eliminate(work, unit), 0.0)
            inverse = pltpu.roll(inverse, 64 * parity, 1)
            column = jnp.concatenate([grid[tile, :ROWS, :], grid[tile, window, :]], axis=0)
            gap = jnp.zeros((16, 128), jnp.float32)
            b_high, b_low = halves(jnp.concatenate([inverse, gap, inverse, gap], axis=0))
            c_high, c_low = halves(column)
            solved = across(jnp.concatenate([c_high, c_low], axis=1), jnp.concatenate([b_high, b_high], axis=1)) + across(c_high, b_low)
            corner = jnp.where((lane % 64) <= rows48, solved[ROWS : ROWS + NV], 0.0)
            chosen = lane // 64 == parity
            chosen_all = lax.broadcasted_iota(jnp.int32, (depth, 128), 1) // 64 == parity
            rest = jnp.concatenate([solved[:ROWS], solved[ROWS + NV :]], axis=0)
            kept = jnp.where(chosen_all, rest, jnp.concatenate([column[:ROWS], column[ROWS + NV :]], axis=0))
            grid[tile, :ROWS, :] = kept[:ROWS]
            grid[tile, later, :] = kept[ROWS:]
            grid[tile, at, :] = jnp.where(chosen, corner, column[ROWS : ROWS + NV])
            s_high, s_low = halves(rest)
            lhs[:depth, :128] = s_high
            lhs[:depth, 128:] = s_low
            left_half = lax.broadcasted_iota(jnp.int32, (band * NV, 128), 1) < 64
            mixed = jnp.where(left_half, s_high[ROWS:].astype(jnp.float32), s_low[ROWS:].astype(jnp.float32)).astype(jnp.bfloat16)
            rhs[pl.ds(pl.multiple_of(64 * k, 64), 64), :] = jnp.zeros((64, 128), jnp.bfloat16)
            for w in range(band):
                rhs[pl.ds(pl.multiple_of(64 * (k + 1 + w), 64), NV), :] = mixed[NV * w : NV * w + NV]

        def trail(band, k, t):
            depth = ROWS + band * NV
            later = pl.ds(pl.multiple_of(ROWS + (k + 1) * NV, 16), band * NV)
            other = rhs[pl.ds(pl.multiple_of(128 * t, 128), 128), :]
            change = across(lhs[:depth, :], jnp.concatenate([other, other], axis=1))
            grid[t, :ROWS, :] -= change[:ROWS]
            grid[t, later, :] -= change[ROWS:]

        @pl.when(reach <= BAND)
        def _():
            def body(k, carry):
                def deferred():
                    for j in range(1, 3):
                        trail(BAND, jnp.maximum(k - 1, 0), k // 2 + j)

                step(BAND, k, deferred)
                trail(BAND, k, (k + 1) // 2)
                return carry

            lax.fori_loop(0, PB, body, 0)

        @pl.when(reach > BAND)
        def _():
            start = ROWS + PB * NV + BAND * NV
            grid[:6, start:, :] = jnp.zeros((6, grid.shape[1] - start, 128), jnp.float32)

            def body(k, carry):
                step(PB - 1, k, lambda: None)

                def inner(t, c):
                    trail(PB - 1, k, t)
                    return c

                lax.fori_loop((k + 1) // 2, 6, inner, 0)
                return carry

            lax.fori_loop(0, PB, body, 0)

        for l in range(SUB_DEV):
            p = ordered(device * SUB_DEV + l)
            inside = p < PB
            start = jnp.where(inside, ROWS + NV * p, NV * l)
            at = pl.ds(pl.multiple_of(start, 16), NV)
            pieces = []
            for j in range(PB):
                piece = grid[j // 2, at, :][:, 64 * (j % 2) : 64 * (j % 2) + NV]
                pieces.append(jnp.where(inside & (j > p), 0.0, piece))
            out[l] = jnp.concatenate(pieces, axis=1)


def factor(order, meta, shares, below, above, rescue, blocks):
    smem = pl.BlockSpec(memory_space=pltpu.SMEM)
    hbm = pl.BlockSpec(memory_space=pl.ANY)
    vmem = pl.BlockSpec(memory_space=pltpu.VMEM)
    return pl.pallas_call(
        factor_kernel,
        out_shape=jax.ShapeDtypeStruct((SUB_DEV, NV, PB * NV), jnp.float32),
        in_specs=[smem] * 2 + [hbm] * 10 + [vmem],
        out_specs=vmem,
        scratch_shapes=[
            pltpu.VMEM((8, ROWS + PB * NV + PB * NV, 128), jnp.float32),
            pltpu.VMEM((4, 6, NV, 128), jnp.float32),
            pltpu.VMEM((ROWS + (PB - 1) * NV, 256), jnp.bfloat16),
            pltpu.VMEM(((2 * PB + 2) * 64, 128), jnp.bfloat16),
            pltpu.SemaphoreType.DMA((4,)),
        ],
        name="factor",
    )(order, meta, *shares, below, above, rescue, blocks)


def shifted(value, amount):
    size = N_ROW * N_COL
    return lax.ppermute(value, ("row", "col"), [(i, (i + amount) % size) for i in range(size)])


def packed(blocks):
    wide = jnp.pad(blocks, ((0, 0), (0, 0), (0, 64 - NV)))
    return jnp.concatenate([wide[:6], wide[6:]], axis=2)


def everywhere(value):
    size = N_ROW * N_COL
    step = 1
    while step < size:
        value = value + lax.ppermute(value, ("row", "col"), [(i, i ^ step) for i in range(size)])
        step *= 2
    return value


def exchange(device, order, blocks, share):
    subdomain = jnp.arange(SUBS, dtype=jnp.int32)
    first = jnp.sum(jnp.where(order == 0, subdomain // SUB_DEV, 0))
    size = N_ROW * N_COL
    distance = (subdomain // SUB_DEV - first + size // 2) % size - size // 2
    inside = order < PB
    least = jnp.min(jnp.where(inside, distance, size))
    most = jnp.max(jnp.where(inside, distance, -size))
    near = (most - least) <= 2
    base = (first + least) % size
    mine = device * SUB_DEV + jnp.arange(SUB_DEV, dtype=jnp.int32)
    my_order = lax.dynamic_slice(order, (device * SUB_DEV,), (SUB_DEV,))

    right1 = shifted(share, 1)
    left1 = shifted(share, -1)
    right2 = shifted(right1, 1)
    left2 = shifted(left1, -1)
    offset = (base - device + size // 2) % size - size // 2
    window = jnp.where(
        offset == 0,
        jnp.stack([share, left1, left2]),
        jnp.where(offset == -1, jnp.stack([right1, share, left1]), jnp.stack([right2, right1, share])),
    )
    below = shifted(window, N_COL)
    above = shifted(window, -N_COL)
    right3 = shifted(right2, 1)
    left3 = shifted(left2, -1)
    from_below = (offset + N_COL + 2) % size <= 2
    from_above = (offset - N_COL + 2) % size <= 2
    flat = (offset >= -3) & (offset <= 1)
    pick = jnp.where(flat, offset + 3, jnp.where(from_below, 5, jnp.where(from_above, 6, 0)))
    pick = jnp.where(near, pick, 7)

    def local_path(_):
        listed = (base * SUB_DEV + jnp.arange(12, dtype=jnp.int32)) % SUBS
        return (jnp.zeros((4, 6, NV, 128), jnp.float32), listed)

    def global_path(_):
        slots = jnp.arange(12, dtype=jnp.int32)
        hit = (order[None, :] == slots[:, None]) & (slots[:, None] < PB)
        listed = jnp.where(slots < PB, jnp.sum(jnp.where(hit, subdomain[None, :], 0), axis=1), -1)
        mask = ((my_order[None, :] == slots[:, None]) & (slots[:, None] < PB)).astype(jnp.float32)
        def oriented(block, offset):
            other = lax.dynamic_slice(jnp.concatenate([order[:128], order]), (128 + device * SUB_DEV - offset,), (SUB_DEV,))
            return jnp.where((my_order > other)[:, None, None], block, jnp.swapaxes(block, 1, 2))

        kinds = jnp.stack(
            [
                blocks[:, 0, :, :NV],
                oriented(blocks[:, 3, :, :NV], SUB_DEV),
                oriented(blocks[:, 5, :, :NV], 1),
                oriented(blocks[:, 1, :, :NV], N_COL * SUB_DEV),
            ],
            axis=1,
        )
        placed = jnp.einsum("ps,skvw->pkvw", mask, kinds, precision=lax.Precision.HIGHEST)
        whole = everywhere(
            jnp.stack([packed(placed[4 * i : 4 * i + 4, :3].reshape(12, NV, NV)) for i in range(3)] + [packed(placed[:, 3])])
        )
        return (whole, listed)

    rescue, listed = lax.cond(near, local_path, global_path, None)
    meta = jnp.concatenate([jnp.stack([device, pick, jnp.int32(0), jnp.int32(0)]), listed]).astype(jnp.int32)
    shares = (share, right1, right2, right3, left1, left2, left3)
    return factor(order, meta, shares, below, above, rescue, blocks)


def from_next(value, axis, amount):
    size = lax.axis_size(axis)
    pairs = [(i, i + amount) for i in range(size) if 0 <= i + amount < size]
    return lax.ppermute(value, axis, pairs)


def shards(deflation, coefficient, gradients, x_penalty, y_penalty, z_penalty, coarse_order):
    device = (lax.axis_index("row") * N_COL + lax.axis_index("col")).astype(jnp.int32)
    below_x = from_next(deflation[1, :, :, 48 * NV :], "row", 1)
    above_x = from_next(deflation[0, :, :, : 16 * NV], "row", -1)
    below_y = from_next(deflation[:, 7], "col", 1)
    above_y = from_next(deflation[:, 0], "col", -1)
    flat = jnp.concatenate([coefficient.reshape(16, 16), x_penalty.reshape(24, 16), y_penalty.reshape(18, 16)], axis=0)
    table = jnp.concatenate([jnp.pad(flat, ((0, 0), (0, 112))), jnp.pad(z_penalty.reshape(16, 17), ((0, 54), (0, 111)))], axis=0)
    main, own_x, own_y, roots_x, roots_y = assemble(deflation, gradients.reshape(192, 64), table)
    meta = jnp.full((8,), device, jnp.int32)
    blocks, share = lateral(coarse_order, meta, below_x, above_x, below_y, above_y, main, own_x, own_y, roots_x, roots_y)
    panel = exchange(device, coarse_order, blocks, share)
    return (flatten(blocks), panel)


def solution(mesh):
    in_specs = (
        P("row", "col", None, None),
        P("row", "col", None),
        P(),
        P("row", "col", None),
        P("row", "col", None),
        P("row", "col", None),
        P(),
    )
    out_specs = (P(("row", "col"), None, None), P(("row", "col"), None, None))
    return jax.shard_map(shards, mesh=mesh, in_specs=in_specs, out_specs=out_specs, check_vma=False)
```

```python
import jax
import jax.numpy as jnp
from jax import lax
from jax.experimental import pallas as pl
from jax.experimental.pallas import tpu as pltpu
from jax.sharding import PartitionSpec as P

NV = 48
SUB_DEV = 4
PB = 11
SUBS = 1024
N_ROW = 8
N_COL = 32


LINE_WEIGHTS = (1.0 / 6.0, 5.0 / 6.0, 5.0 / 6.0, 1.0 / 6.0)
COEF, XPEN, YPEN, ZPEN = 0, 16, 40, 58


def fetch(tiles, start, target):
    lane = lax.broadcasted_iota(jnp.int32, tiles[0].shape, 1)
    tile, offset = start // 128, start % 128
    shift = (target - offset) % 128
    first = pltpu.roll(tiles[tile], shift, 1) if shift else tiles[tile]
    if offset + NV <= 128:
        return first
    second = pltpu.roll(tiles[tile + 1], shift, 1) if shift else tiles[tile + 1]
    return jnp.where(lane >= target + 128 - offset, second, first)


def paired(even, odd, start):
    lane = lax.broadcasted_iota(jnp.int32, even[0].shape, 1)
    return jnp.where(lane < 64, fetch(even, start, 0), fetch(odd, start, 64))


def lane_tiles(values):
    wide = values.astype(jnp.float32)
    return [wide[:, 128 * t : 128 * t + 128] for t in range(wide.shape[1] // 128)]


def gram(left, right):
    return lax.dot_general(left, right, (((0,), (0,)), ((), ())), preferred_element_type=jnp.float32)


def assemble_kernel(deflation, gradients, table, main, own_x, own_y, roots_x, roots_y, nodes, sides, stack, second, total, roots, low_z, other_z):
    rooted = jnp.sqrt(jnp.transpose(table[...]))[:24]
    half = lax.broadcasted_iota(jnp.int32, (24, 128), 1) < 64

    def spread(even, odd):
        left = jnp.broadcast_to(rooted[:, even : even + 1], (24, 128))
        right = jnp.broadcast_to(rooted[:, odd : odd + 1], (24, 128))
        return jnp.where(half, left, right)

    for i in range(4):
        for x in range(2):
            roots[0, i, x] = spread(COEF + 8 * x + 2 * i, COEF + 8 * x + 2 * i + 1)
            roots[1, i, x] = spread(XPEN + 16 * x + 2 * i, XPEN + 16 * x + 2 * i + 1)
            roots[2, i, x] = spread(XPEN + 8 + 2 * i, XPEN + 8 + 2 * i + 1)
            roots[3, i, x] = spread(YPEN + 9 * x + 2 * i + 1, YPEN + 9 * x + 2 * i + 2)
            roots[4, i, x] = spread(ZPEN + 8 * x + 2 * i, ZPEN + 8 * x + 2 * i + 1)
            roots[5, i, x] = jnp.where(half & (i == 0), jnp.broadcast_to(rooted[:, YPEN + 9 * x : YPEN + 9 * x + 1], (24, 128)), 0.0)
        roots_x[i] = roots[1, i, 0, :16]
    roots_y[...] = spread(YPEN, YPEN + 9)[:16]

    def relay(i, carry):
        for x in range(2):
            even = lane_tiles(deflation[x, 2 * i])
            odd = lane_tiles(deflation[x, 2 * i + 1])
            for n in range(64):
                a, b, c = n // 16, n // 4 % 4, n % 4
                both = paired(even, odd, NV * n)
                nodes[i, x, pl.ds(n, 16, stride=65), :] = both
                if b % 3 == 0:
                    sides[i, x, b // 3, pl.ds(4 * a + c, 16, stride=17), :] = both
        return carry

    lax.fori_loop(0, 4, relay, 0)
    total[...] = jnp.zeros_like(total)
    node = lax.broadcasted_iota(jnp.int32, (64, 128), 0)

    def edge(position):
        return jnp.where((position == 0) | (position == 3), LINE_WEIGHTS[0], LINE_WEIGHTS[1])

    weight = jnp.sqrt(edge(node // 16) * edge(node // 4 % 4) * edge(node % 4))
    first_half = lax.broadcasted_iota(jnp.int32, (16, 128), 1) < 64

    def fill(step, stack):
        s, i = step // 4, step % 4
        low = jnp.bfloat16

        def root(kind, x, z, rows):
            return jnp.broadcast_to(roots[kind, i, x, pl.ds(z, 1), :], (rows, 128))

        inner = []
        for zz in range(4):
            z = 4 * s + zz
            at = pl.ds(65 * z, 64)
            block = [nodes[i, x, at, :] for x in range(2)]
            z_rows = jnp.concatenate(block, axis=1).astype(low)
            product = jnp.dot(gradients[...], z_rows, preferred_element_type=jnp.float32)
            factor_z = jnp.concatenate([weight * root(0, x, z, 64) for x in range(2)], axis=1)
            for d in range(3):
                stack[192 * zz + 64 * d : 192 * zz + 64 * d + 64, :] = (product[64 * d : 64 * d + 64] * factor_z).astype(low)
            near = (block[0][:16] * root(1, 0, z, 16)).astype(low)
            far = (block[1][48:] * root(1, 1, z, 16)).astype(low)
            stack[768 + 16 * zz : 784 + 16 * zz, :] = jnp.concatenate([near, far], axis=1)
            here = pl.ds(17 * z, 16)
            there = pl.ds(pl.multiple_of(16 * z, 16), 16)
            own_x[i, there, :] = near
            inner.append((root(2, 0, z, 16) * (block[0][48:] - block[1][:16])).astype(low))
            lows, jumps = [], []
            after = jnp.minimum(i + 1, 3)
            for x in range(2):
                lower = sides[i, x, 0, here, :]
                swapped = pltpu.roll(lower, 64, 1)
                later = jnp.where(i < 3, pltpu.roll(sides[after, x, 0, here, :], 64, 1), 0.0)
                jumps.append((root(3, x, z, 16) * (sides[i, x, 1, here, :] - jnp.where(first_half, swapped, later))).astype(low))
                lows.append((root(5, x, z, 16) * lower).astype(low))
            stack[864 + 16 * zz : 880 + 16 * zz, :] = jnp.concatenate(jumps, axis=1)
            stack[928 + 16 * zz : 944 + 16 * zz, :] = jnp.concatenate(lows, axis=1)
            ups, firsts, befores = [], [], []
            for x in range(2):
                upper = nodes[i, x, pl.ds(65 * z + 3, 16, stride=4), :]
                if zz < 3:
                    upper = upper - nodes[i, x, pl.ds(65 * z + 65, 16, stride=4), :]
                ups.append((root(4, x, z + 1, 16) * upper).astype(low))
                if zz == 0:
                    firsts.append((root(4, x, z, 16) * nodes[i, x, pl.ds(65 * z, 16, stride=4), :]).astype(low))
                    before = nodes[i, x, pl.ds(65 * jnp.maximum(z - 1, 0) + 3, 16, stride=4), :]
                    befores.append(jnp.where(s > 0, root(4, x, z, 16) * before, 0.0).astype(low))
            stack[992 + 16 * zz : 1008 + 16 * zz, :] = jnp.concatenate(ups, axis=1)
            if zz == 0:
                stack[1056:1072, :] = jnp.concatenate(firsts, axis=1)
                row = pl.ds(pl.multiple_of(16 * i, 16), 16)
                low_z[s, row, :] = jnp.concatenate(firsts, axis=1)
                other_z[s, row, :] = jnp.concatenate(befores, axis=1)
        stack[832:848, :] = jnp.concatenate(inner[:2], axis=1)
        stack[848:864, :] = jnp.concatenate(inner[2:], axis=1)

    def add(step, stack):
        total[step // 4] += gram(stack[...], stack[...])

    second[...] = jnp.zeros_like(second)

    def pair(step, carry):
        add(jnp.maximum(2 * step - 1, 0), second)
        fill(2 * step, stack)
        add(2 * step, stack)
        fill(2 * step + 1, second)
        return carry

    lax.fori_loop(0, 8, pair, 0)
    add(15, second)

    def folded(square):
        return (
            square[:NV, :128]
            + pltpu.roll(square[64 : 64 + NV, :128], 64, 1)
            + square[128 : 128 + NV, 128:]
            + pltpu.roll(square[192 : 192 + NV, 128:], 64, 1)
        )

    for s in range(4):
        main[s, 0] = folded(total[s])
        below = -folded(gram(low_z[s], other_z[s]))
        main[s, 1] = below
        if s:
            main[s - 1, 2] = jnp.transpose(jnp.concatenate([below, jnp.zeros((80, 128), jnp.float32)], axis=0))[:NV]
    main[3, 2] = jnp.zeros((NV, 128), jnp.float32)
    for z in range(16):
        here = slice(16 * z, 16 * z + 16)
        there = slice(17 * z, 17 * z + 16)
        lower = [sides[0, x, 0, there, :] for x in range(2)]
        near = jnp.where(first_half, lower[0], pltpu.roll(lower[1], 64, 1))
        own_y[here, :] = (near * jnp.broadcast_to(roots_y[z : z + 1, :], (16, 128))).astype(jnp.bfloat16)


def assemble(deflation, gradients, table):
    vmem = pl.BlockSpec(memory_space=pltpu.VMEM)
    f32, low = jnp.float32, jnp.bfloat16
    return pl.pallas_call(
        assemble_kernel,
        out_shape=(
            jax.ShapeDtypeStruct((4, 3, NV, 128), f32),
            jax.ShapeDtypeStruct((4, 256, 128), low),
            jax.ShapeDtypeStruct((256, 128), low),
            jax.ShapeDtypeStruct((4, 16, 128), f32),
            jax.ShapeDtypeStruct((16, 128), f32),
        ),
        in_specs=[vmem] * 3,
        out_specs=(vmem,) * 5,
        scratch_shapes=[
            pltpu.VMEM((4, 2, 1040, 128), f32),
            pltpu.VMEM((4, 2, 2, 272, 128), f32),
            pltpu.VMEM((1072, 256), low),
            pltpu.VMEM((1072, 256), low),
            pltpu.VMEM((4, 256, 256), f32),
            pltpu.VMEM((6, 4, 2, 24, 128), f32),
            pltpu.VMEM((4, 64, 256), low),
            pltpu.VMEM((4, 64, 256), low),
        ],
        cost_estimate=pl.CostEstimate(flops=2_000_000_000, bytes_accessed=3_000_000, transcendentals=0),
        name="assemble",
    )(deflation, gradients, table)


def flipped(block):
    return jnp.transpose(jnp.concatenate([block, jnp.zeros((80, 128), jnp.float32)], axis=0))[:NV]


def lateral_kernel(order, meta, below_x, below_y, main, own_x, own_y, roots_x, roots_y, blocks, share, side, halo_x, halo_y):
    device = meta[0]
    low = jnp.bfloat16
    inside = lax.broadcasted_iota(jnp.int32, (NV, 128), 1) < NV

    def relay(i, carry):
        even = lane_tiles(below_x[2 * i])
        odd = lane_tiles(below_x[2 * i + 1])
        for m in range(16):
            halo_x[i, pl.ds(m, 16, stride=17), :] = paired(even, odd, NV * m) * roots_x[i]
        return carry

    lax.fori_loop(0, 4, relay, 0)
    even = lane_tiles(below_y[0])
    odd = lane_tiles(below_y[1])
    for m in range(16):
        n = 16 * (m // 4) + 12 + m % 4
        halo_y[pl.ds(m, 16, stride=17), :] = paired(even, odd, NV * n) * roots_y[...]

    def folded(square):
        return jnp.where(inside, -(square[:NV] + pltpu.roll(square[64 : 64 + NV], 64, 1)), 0.0)

    for s in range(SUB_DEV):
        at = slice(64 * s, 64 * s + 64)
        diag = jnp.where(inside, main[s, 0], 0.0)
        low_z = jnp.where(inside, main[s, 1], 0.0)
        mine = jnp.concatenate([own_x[i, at, :] for i in range(4)], axis=0)
        theirs = [halo_x[i, 17 * z : 17 * z + 16, :].astype(low) for i in range(4) for z in range(4 * s, 4 * s + 4)]
        low_x = folded(gram(mine, jnp.concatenate(theirs, axis=0)))
        theirs = [halo_y[17 * z : 17 * z + 16, :].astype(low) for z in range(4 * s, 4 * s + 4)]
        low_y = folded(gram(own_y[at, :], jnp.concatenate(theirs, axis=0)))
        blocks[s, 0] = diag
        blocks[s, 1] = low_x
        blocks[s, 2] = low_y
        blocks[s, 3] = low_z
        blocks[s, 4] = jnp.where(inside, main[s, 2], 0.0)
        here = device * SUB_DEV + s
        rank = order[here]
        turned_y = jnp.where(rank > order[jnp.maximum(here - SUB_DEV, 0)], low_y, flipped(low_y))
        turned_z = jnp.where(rank > order[jnp.maximum(here - 1, 0)], low_z, flipped(low_z))
        for kind, value in enumerate((diag, turned_y, turned_z)):
            row = (s % 2) * 3 + kind
            if s < 2:
                share[row] = value
            else:
                share[row] += pltpu.roll(value, 64, 1)
        if s < 2:
            side[s] = low_x
        else:
            side[s - 2] += pltpu.roll(low_x, 64, 1)


def lateral(order, meta, below_x, below_y, main, own_x, own_y, roots_x, roots_y):
    smem = pl.BlockSpec(memory_space=pltpu.SMEM)
    vmem = pl.BlockSpec(memory_space=pltpu.VMEM)
    f32 = jnp.float32
    return pl.pallas_call(
        lateral_kernel,
        out_shape=(
            jax.ShapeDtypeStruct((SUB_DEV, 5, NV, 128), f32),
            jax.ShapeDtypeStruct((6, NV, 128), f32),
            jax.ShapeDtypeStruct((2, NV, 128), f32),
        ),
        in_specs=[smem] * 2 + [vmem] * 7,
        out_specs=(vmem, vmem, vmem),
        scratch_shapes=[
            pltpu.VMEM((4, 272, 128), f32),
            pltpu.VMEM((272, 128), f32),
        ],
        name="lateral",
    )(order, meta, below_x, below_y, main, own_x, own_y, roots_x, roots_y)


def row_major(read, write):
    lane = lax.broadcasted_iota(jnp.int32, (8, 128), 1)
    for t in range(18):
        value = None
        for v in range(NV):
            shift = NV * v - 128 * t
            if shift <= -NV or shift >= 128:
                continue
            row = read(v)
            row = pltpu.roll(row, shift % 128, 1) if shift % 128 else row
            here = (lane >= shift) & (lane < shift + NV)
            value = jnp.where(here, row, 0.0 if value is None else value)
        write(t, value)


def flatten_kernel(order, meta, blocks, above, out, high_y, turned):
    device = meta[0]
    places = (0, 1, 3, 5, 6)
    for s in range(SUB_DEV):
        for kind in range(5):
            group = (SUB_DEV * kind + s) // 8
            turned[group, pl.ds((SUB_DEV * kind + s) % 8, NV, stride=8), :] = blocks[s, kind]
        packed_low = above[(s % 2) * 3 + 1]
        if s >= 2:
            packed_low = pltpu.roll(packed_low, 64, 1)
        packed_low = jnp.where(lax.broadcasted_iota(jnp.int32, (NV, 128), 1) < NV, packed_low, 0.0)
        here = device * SUB_DEV + s
        later = order[jnp.minimum(here + SUB_DEV, SUBS - 1)]
        upper = jnp.where(order[here] > later, packed_low, flipped(packed_low))
        high_y[s] = upper
        turned[2, pl.ds(SUB_DEV + s, NV, stride=8), :] = upper
    for group in range(3):
        low_place = places[2 * group]
        high_place = places[2 * group + 1] if group < 2 else 4

        def write(t, value):
            out[low_place, :, 128 * t : 128 * t + 128] = value[:4]
            out[high_place, :, 128 * t : 128 * t + 128] = value[4:]

        row_major(lambda v: turned[group, 8 * v : 8 * v + 8, :], write)


def flatten(order, meta, blocks, above):
    smem = pl.BlockSpec(memory_space=pltpu.SMEM)
    vmem = pl.BlockSpec(memory_space=pltpu.VMEM)
    return pl.pallas_call(
        flatten_kernel,
        out_shape=(
            jax.ShapeDtypeStruct((7, SUB_DEV, NV * NV), jnp.float32),
            jax.ShapeDtypeStruct((SUB_DEV, NV, 128), jnp.float32),
        ),
        in_specs=[smem] * 2 + [vmem] * 2,
        out_specs=(vmem, vmem),
        scratch_shapes=[pltpu.VMEM((3, NV * 8, 128), jnp.float32)],
        cost_estimate=pl.CostEstimate(flops=1_000_000, bytes_accessed=2_000_000, transcendentals=0),
        name="flatten",
    )(order, meta, blocks, above)


def eliminate(work, unit):
    groups = [work[8 * v : 8 * v + 8] for v in range(6)]
    sub = lax.broadcasted_iota(jnp.int32, (8, 128), 0)

    def row_of(value, k):
        return jnp.broadcast_to(value[k : k + 1, :], (8, 128))

    def column_of(value, k):
        return jnp.broadcast_to(value[:, k : k + 1], (8, 128))

    for g in range(6):
        head = groups[g]
        splat = [column_of(head, 64 + 8 * g + k) * unit for k in range(8)]
        below = [[column_of(groups[v], 64 + 8 * g + k) for k in range(8)] for v in range(g + 1, 6)]
        done = jnp.zeros((8, 128), jnp.float32)
        for k in range(0, 8, 2):
            x, y = splat[k], splat[k + 1]
            a, b, c = row_of(x, k), row_of(y, k), row_of(y, k + 1)
            inverse = 1.0 / (a * c - b * b)
            ratio = b / a
            top, low = row_of(head, k), row_of(head, k + 1)
            done = jnp.where(sub == k, top * lax.rsqrt(a), done)
            done = jnp.where(sub == k + 1, (low - ratio * top) * lax.rsqrt(c - ratio * b), done)

            def reduced(value, upper, lower):
                one = (c * upper - b * lower) * inverse
                two = (a * lower - b * upper) * inverse
                return jnp.where(sub == k, one, jnp.where(sub == k + 1, two, value - x * one - y * two))

            for m in range(k + 2, 8):
                splat[m] = reduced(splat[m], row_of(splat[m], k), row_of(splat[m], k + 1))
            head = reduced(head, top, low)
        rows = [row_of(head, k) for k in range(8)]
        for v in range(g + 1, 6):
            terms = [s * r for s, r in zip(below[v - g - 1], rows)]
            while len(terms) > 1:
                terms = [p + q for p, q in zip(terms[::2], terms[1::2])]
            groups[v] = groups[v] - terms[0]
        groups[g] = done
    return jnp.concatenate(groups, axis=0)


def halves(values):
    high = values.astype(jnp.bfloat16)
    low = (values - high.astype(jnp.float32)).astype(jnp.bfloat16)
    return high, low


def across(left, right):
    return lax.dot_general(left, right, (((1,), (1,)), ((), ())), preferred_element_type=jnp.float32)


ROWS = SUB_DEV * NV
BAND = 4


def factor_kernel(order, meta, own, right1, right2, right3, left1, left2, left3, below, above, rescue, blocks, high_y, flat_in, out, flat, grid, got, lhs, rhs, side, high_x, turned, slab, sems, side_sems):
    device = meta[0]
    lane = lax.broadcasted_iota(jnp.int32, (NV, 128), 1)

    def place(value, half, row, column, wanted):
        parity = column % 2
        moved = pltpu.roll(value, 64 * ((parity + half) % 2), 1)
        inside = (lane >= 64 * parity) & (lane < 64 * parity + NV)
        tile = jnp.where(wanted, column // 2, 7)
        at = pl.ds(pl.multiple_of(jnp.where(wanted, row, 0), 16), NV)
        pltpu.store(grid.at[tile, at, :], moved, mask=inside)

    def ordered(subdomain):
        return order[jnp.clip(subdomain, 0, SUBS - 1)]

    def neighbours(subdomain):
        column = (subdomain // SUB_DEV) % N_COL
        local = subdomain % SUB_DEV
        stride = N_COL * SUB_DEV
        return (
            (subdomain, subdomain >= 0),
            (subdomain - stride, subdomain >= stride),
            (subdomain + stride, (subdomain >= 0) & (subdomain < SUBS - stride)),
            (subdomain - SUB_DEV, (subdomain >= 0) & (column > 0)),
            (subdomain + SUB_DEV, (subdomain >= 0) & (column < N_COL - 1)),
            (subdomain - 1, (subdomain >= 0) & (local > 0)),
            (subdomain + 1, (subdomain >= 0) & (local < SUB_DEV - 1)),
        )

    relevant = jnp.int32(0)
    for l in range(SUB_DEV):
        for near, there in neighbours(device * SUB_DEV + l):
            relevant += (there & (ordered(near) < PB)).astype(jnp.int32)

    side_copy = pltpu.make_async_copy(above.at[pl.ds(18, 2)], side, side_sems.at[0])
    side_copy.start()

    @pl.when(relevant > 0)
    def _():
        near_sources = [right3, right2, right1, own, left1, left2, left3]
        for case in range(5):

            @pl.when(meta[1] == case)
            def _():
                for i in range(3):
                    pltpu.make_async_copy(near_sources[case + i], got.at[i], sems.at[i]).start()

        for case, source in ((5, below), (6, above), (7, rescue)):

            @pl.when(meta[1] == case)
            def _():
                for i in range(3):
                    pltpu.make_async_copy(source.at[pl.ds(6 * i, 6)], got.at[i], sems.at[i]).start()

        pltpu.make_async_copy(rescue.at[pl.ds(18, 6)], got.at[3], sems.at[3]).start()

    side_copy.wait()
    for s in range(SUB_DEV):
        packed_low = side[s % 2]
        if s >= 2:
            packed_low = pltpu.roll(packed_low, 64, 1)
        upper = flipped(jnp.where(lane < NV, packed_low, 0.0))
        high_x[s] = upper
        turned[pl.ds(s, NV, stride=8), :] = upper

    def write(t, value):
        slab[:, 128 * t : 128 * t + 128] = value[:4]

    row_major(lambda v: turned[8 * v : 8 * v + 8, :], write)
    flat_copy = pltpu.make_async_copy(slab, flat.at[2], side_sems.at[1])
    flat_copy.start()

    @pl.when(relevant == 0)
    def _():
        out[...] = jnp.zeros_like(out)

    @pl.when(relevant > 0)
    def _():
        grid[:6, : ROWS + PB * NV + BAND * NV, :] = jnp.zeros((6, ROWS + PB * NV + BAND * NV, 128), jnp.float32)
        rhs[...] = jnp.zeros_like(rhs)
        lhs[...] = jnp.zeros_like(lhs)
        for l in range(SUB_DEV):
            for kind, (near, there) in enumerate(neighbours(device * SUB_DEV + l)):
                column = ordered(near)
                value = (blocks.at[l, 0], blocks.at[l, 1], high_x.at[l], blocks.at[l, 2], high_y.at[l], blocks.at[l, 3], blocks.at[l, 4])[kind][...]
                place(value, 0, NV * l, column, there & (column < PB))
        for i in range(4):
            pltpu.make_async_copy(own, got.at[i], sems.at[i]).wait()
        reach = jnp.int32(0)
        for slot in range(12):
            i, l = slot // SUB_DEV, slot % SUB_DEV
            s = meta[4 + slot]
            p = ordered(s)
            near = neighbours(s)
            for kind, (t, there) in enumerate((near[0], near[3], near[5], near[1])):
                q = ordered(t)
                wanted = there & (p < PB) & (q < PB)
                reach = jnp.maximum(reach, jnp.where(wanted, jnp.abs(p - q), 0))
                if kind < 3:
                    value, half = got[i, (l % 2) * 3 + kind], l // 2
                else:
                    value, half = got[3, slot % 6], slot // 6
                place(value, half, ROWS + NV * jnp.maximum(p, q), jnp.minimum(p, q), wanted)

        rows48 = lax.broadcasted_iota(jnp.int32, (NV, 128), 0)

        unit = jnp.full((8, 128), jnp.where(device >= 0, 1.0, 0.0), jnp.float32)

        def step(band, k, deferred):
            tile = k // 2
            parity = k % 2
            depth = ROWS + band * NV
            window = pl.ds(pl.multiple_of(ROWS + k * NV, 16), NV + band * NV)
            later = pl.ds(pl.multiple_of(ROWS + (k + 1) * NV, 16), band * NV)
            at = pl.ds(pl.multiple_of(ROWS + k * NV, 16), NV)
            diag = pltpu.roll(grid[tile, at, :], 64 * (1 - parity), 1)
            deferred()
            work = jnp.where(lane < 64, (lane == rows48).astype(jnp.float32), jnp.where(lane < 64 + NV, diag, 0.0))
            inverse = jnp.where(lane < NV, eliminate(work, unit), 0.0)
            inverse = pltpu.roll(inverse, 64 * parity, 1)
            column = jnp.concatenate([grid[tile, :ROWS, :], grid[tile, window, :]], axis=0)
            gap = jnp.zeros((16, 128), jnp.float32)
            b_high, b_low = halves(jnp.concatenate([inverse, gap, inverse, gap], axis=0))
            c_high, c_low = halves(column)
            solved = across(jnp.concatenate([c_high, c_low], axis=1), jnp.concatenate([b_high, b_high], axis=1)) + across(c_high, b_low)
            corner = jnp.where((lane % 64) <= rows48, solved[ROWS : ROWS + NV], 0.0)
            chosen = lane // 64 == parity
            chosen_all = lax.broadcasted_iota(jnp.int32, (depth, 128), 1) // 64 == parity
            rest = jnp.concatenate([solved[:ROWS], solved[ROWS + NV :]], axis=0)
            kept = jnp.where(chosen_all, rest, jnp.concatenate([column[:ROWS], column[ROWS + NV :]], axis=0))
            grid[tile, :ROWS, :] = kept[:ROWS]
            grid[tile, later, :] = kept[ROWS:]
            grid[tile, at, :] = jnp.where(chosen, corner, column[ROWS : ROWS + NV])
            s_high, s_low = halves(rest)
            lhs[:depth, :128] = s_high
            lhs[:depth, 128:] = s_low
            left_half = lax.broadcasted_iota(jnp.int32, (band * NV, 128), 1) < 64
            mixed = jnp.where(left_half, s_high[ROWS:].astype(jnp.float32), s_low[ROWS:].astype(jnp.float32)).astype(jnp.bfloat16)
            rhs[pl.ds(pl.multiple_of(64 * k, 64), 64), :] = jnp.zeros((64, 128), jnp.bfloat16)
            for w in range(band):
                rhs[pl.ds(pl.multiple_of(64 * (k + 1 + w), 64), NV), :] = mixed[NV * w : NV * w + NV]

        def trail(band, k, t):
            depth = ROWS + band * NV
            later = pl.ds(pl.multiple_of(ROWS + (k + 1) * NV, 16), band * NV)
            other = rhs[pl.ds(pl.multiple_of(128 * t, 128), 128), :]
            change = across(lhs[:depth, :], jnp.concatenate([other, other], axis=1))
            grid[t, :ROWS, :] -= change[:ROWS]
            grid[t, later, :] -= change[ROWS:]

        @pl.when(reach <= BAND)
        def _():
            def body(k, carry):
                def deferred():
                    for j in range(1, 3):
                        trail(BAND, jnp.maximum(k - 1, 0), k // 2 + j)

                step(BAND, k, deferred)
                trail(BAND, k, (k + 1) // 2)
                return carry

            lax.fori_loop(0, PB, body, 0)

        @pl.when(reach > BAND)
        def _():
            start = ROWS + PB * NV + BAND * NV
            grid[:6, start:, :] = jnp.zeros((6, grid.shape[1] - start, 128), jnp.float32)

            def body(k, carry):
                step(PB - 1, k, lambda: None)

                def inner(t, c):
                    trail(PB - 1, k, t)
                    return c

                lax.fori_loop((k + 1) // 2, 6, inner, 0)
                return carry

            lax.fori_loop(0, PB, body, 0)

        for l in range(SUB_DEV):
            p = ordered(device * SUB_DEV + l)
            inside = p < PB
            start = jnp.where(inside, ROWS + NV * p, NV * l)
            at = pl.ds(pl.multiple_of(start, 16), NV)
            pieces = []
            for j in range(PB):
                piece = grid[j // 2, at, :][:, 64 * (j % 2) : 64 * (j % 2) + NV]
                pieces.append(jnp.where(inside & (j > p), 0.0, piece))
            out[l] = jnp.concatenate(pieces, axis=1)

    flat_copy.wait()


def factor(order, meta, shares, below, above, rescue, blocks, high_y, flat):
    smem = pl.BlockSpec(memory_space=pltpu.SMEM)
    hbm = pl.BlockSpec(memory_space=pl.ANY)
    vmem = pl.BlockSpec(memory_space=pltpu.VMEM)
    return pl.pallas_call(
        factor_kernel,
        out_shape=(
            jax.ShapeDtypeStruct((SUB_DEV, NV, PB * NV), jnp.float32),
            jax.ShapeDtypeStruct(flat.shape, jnp.float32),
        ),
        in_specs=[smem] * 2 + [hbm] * 10 + [vmem] * 2 + [hbm],
        out_specs=(vmem, hbm),
        input_output_aliases={14: 1},
        scratch_shapes=[
            pltpu.VMEM((8, ROWS + PB * NV + PB * NV, 128), jnp.float32),
            pltpu.VMEM((4, 6, NV, 128), jnp.float32),
            pltpu.VMEM((ROWS + (PB - 1) * NV, 256), jnp.bfloat16),
            pltpu.VMEM(((2 * PB + 2) * 64, 128), jnp.bfloat16),
            pltpu.VMEM((2, NV, 128), jnp.float32),
            pltpu.VMEM((SUB_DEV, NV, 128), jnp.float32),
            pltpu.VMEM((NV * 8, 128), jnp.float32),
            pltpu.VMEM((SUB_DEV, NV * NV), jnp.float32),
            pltpu.SemaphoreType.DMA((4,)),
            pltpu.SemaphoreType.DMA((2,)),
        ],
        name="factor",
    )(order, meta, *shares, below, above, rescue, blocks, high_y, flat)


def shifted(value, amount):
    size = N_ROW * N_COL
    return lax.ppermute(value, ("row", "col"), [(i, (i + amount) % size) for i in range(size)])


def packed(blocks):
    wide = jnp.pad(blocks, ((0, 0), (0, 0), (0, 64 - NV)))
    return jnp.concatenate([wide[:6], wide[6:]], axis=2)


def everywhere(value):
    size = N_ROW * N_COL
    step = 1
    while step < size:
        value = value + lax.ppermute(value, ("row", "col"), [(i, i ^ step) for i in range(size)])
        step *= 2
    return value


def exchange(device, order, meta_lateral, blocks, share, side):
    subdomain = jnp.arange(SUBS, dtype=jnp.int32)
    first = jnp.sum(jnp.where(order == 0, subdomain // SUB_DEV, 0))
    size = N_ROW * N_COL
    distance = (subdomain // SUB_DEV - first + size // 2) % size - size // 2
    inside = order < PB
    least = jnp.min(jnp.where(inside, distance, size))
    most = jnp.max(jnp.where(inside, distance, -size))
    near = (most - least) <= 2
    base = (first + least) % size
    mine = device * SUB_DEV + jnp.arange(SUB_DEV, dtype=jnp.int32)
    my_order = lax.dynamic_slice(order, (device * SUB_DEV,), (SUB_DEV,))

    right1 = shifted(share, 1)
    left1 = shifted(share, -1)
    right2 = shifted(right1, 1)
    left2 = shifted(left1, -1)
    offset = (base - device + size // 2) % size - size // 2
    window = jnp.where(
        offset == 0,
        jnp.stack([share, left1, left2]),
        jnp.where(offset == -1, jnp.stack([right1, share, left1]), jnp.stack([right2, right1, share])),
    )
    payload = jnp.concatenate([window.reshape(18, NV, 128), side], axis=0)
    below = shifted(payload, N_COL)
    above = shifted(payload, -N_COL)
    flat, high_y = flatten(order, meta_lateral, blocks, left1)
    right3 = shifted(right2, 1)
    left3 = shifted(left2, -1)
    from_below = (offset + N_COL + 2) % size <= 2
    from_above = (offset - N_COL + 2) % size <= 2
    beside = (offset >= -3) & (offset <= 1)
    pick = jnp.where(beside, offset + 3, jnp.where(from_below, 5, jnp.where(from_above, 6, 0)))
    pick = jnp.where(near, pick, 7)

    def local_path(_):
        listed = (base * SUB_DEV + jnp.arange(12, dtype=jnp.int32)) % SUBS
        return (jnp.zeros((24, NV, 128), jnp.float32), listed)

    def global_path(_):
        slots = jnp.arange(12, dtype=jnp.int32)
        hit = (order[None, :] == slots[:, None]) & (slots[:, None] < PB)
        listed = jnp.where(slots < PB, jnp.sum(jnp.where(hit, subdomain[None, :], 0), axis=1), -1)
        mask = ((my_order[None, :] == slots[:, None]) & (slots[:, None] < PB)).astype(jnp.float32)
        def oriented(block, offset):
            other = lax.dynamic_slice(jnp.concatenate([order[:128], order]), (128 + device * SUB_DEV - offset,), (SUB_DEV,))
            return jnp.where((my_order > other)[:, None, None], block, jnp.swapaxes(block, 1, 2))

        kinds = jnp.stack(
            [
                blocks[:, 0, :, :NV],
                oriented(blocks[:, 2, :, :NV], SUB_DEV),
                oriented(blocks[:, 3, :, :NV], 1),
                oriented(blocks[:, 1, :, :NV], N_COL * SUB_DEV),
            ],
            axis=1,
        )
        placed = jnp.einsum("ps,skvw->pkvw", mask, kinds, precision=lax.Precision.HIGHEST)
        whole = everywhere(
            jnp.stack([packed(placed[4 * i : 4 * i + 4, :3].reshape(12, NV, NV)) for i in range(3)] + [packed(placed[:, 3])])
        )
        return (whole.reshape(24, NV, 128), listed)

    rescue, listed = lax.cond(near, local_path, global_path, None)
    meta = jnp.concatenate([jnp.stack([device, pick, jnp.int32(0), jnp.int32(0)]), listed]).astype(jnp.int32)
    shares = (share, right1, right2, right3, left1, left2, left3)
    panel, flat = factor(order, meta, shares, below, above, rescue, blocks, high_y, flat)
    return (jnp.transpose(flat, (1, 0, 2)), panel)


def from_next(value, axis, amount):
    size = lax.axis_size(axis)
    pairs = [(i, i + amount) for i in range(size) if 0 <= i + amount < size]
    return lax.ppermute(value, axis, pairs)


def shards(deflation, coefficient, gradients, x_penalty, y_penalty, z_penalty, coarse_order):
    device = (lax.axis_index("row") * N_COL + lax.axis_index("col")).astype(jnp.int32)
    below_x = from_next(deflation[1, :, :, 48 * NV :], "row", 1)
    below_y = from_next(deflation[:, 7], "col", 1)
    flat = jnp.concatenate([coefficient.reshape(16, 16), x_penalty.reshape(24, 16), y_penalty.reshape(18, 16)], axis=0)
    table = jnp.concatenate([jnp.pad(flat, ((0, 0), (0, 112))), jnp.pad(z_penalty.reshape(16, 17), ((0, 54), (0, 111)))], axis=0)
    main, own_x, own_y, roots_x, roots_y = assemble(deflation, gradients.reshape(192, 64), table)
    meta = jnp.full((8,), device, jnp.int32)
    blocks, share, side = lateral(coarse_order, meta, below_x, below_y, main, own_x, own_y, roots_x, roots_y)
    return exchange(device, coarse_order, meta, blocks, share, side)


def solution(mesh):
    in_specs = (
        P("row", "col", None, None),
        P("row", "col", None),
        P(),
        P("row", "col", None),
        P("row", "col", None),
        P("row", "col", None),
        P(),
    )
    out_specs = (P(("row", "col"), None, None), P(("row", "col"), None, None))
    return jax.shard_map(shards, mesh=mesh, in_specs=in_specs, out_specs=out_specs, check_vma=False)
```

```python
import jax
import jax.numpy as jnp
from jax import lax
from jax.experimental import pallas as pl
from jax.experimental.pallas import tpu as pltpu
from jax.sharding import PartitionSpec as P

NV = 48
SUB_DEV = 4
PB = 11
SUBS = 1024
N_ROW = 8
N_COL = 32


LINE_WEIGHTS = (1.0 / 6.0, 5.0 / 6.0, 5.0 / 6.0, 1.0 / 6.0)
COEF, XPEN, YPEN, ZPEN = 0, 16, 40, 58


def fetch(tiles, start, target):
    lane = lax.broadcasted_iota(jnp.int32, tiles[0].shape, 1)
    tile, offset = start // 128, start % 128
    shift = (target - offset) % 128
    first = pltpu.roll(tiles[tile], shift, 1) if shift else tiles[tile]
    if offset + NV <= 128:
        return first
    second = pltpu.roll(tiles[tile + 1], shift, 1) if shift else tiles[tile + 1]
    return jnp.where(lane >= target + 128 - offset, second, first)


def paired(even, odd, start):
    lane = lax.broadcasted_iota(jnp.int32, even[0].shape, 1)
    return jnp.where(lane < 64, fetch(even, start, 0), fetch(odd, start, 64))


def lane_tiles(values):
    wide = values.astype(jnp.float32)
    return [wide[:, 128 * t : 128 * t + 128] for t in range(wide.shape[1] // 128)]


def gram(left, right):
    return lax.dot_general(left, right, (((0,), (0,)), ((), ())), preferred_element_type=jnp.float32)


def assemble_kernel(deflation, gradients, coefficient, x_penalty, y_penalty, z_penalty, main, own_x, own_y, roots_x, roots_y, nodes, sides, stack, second, total, roots, low_z, other_z, table):
    table[...] = jnp.zeros_like(table)
    for x in range(2):
        table[COEF + 8 * x : COEF + 8 * x + 8, :16] = coefficient[x]
        table[ZPEN + 8 * x : ZPEN + 8 * x + 8, :17] = z_penalty[x]
    for g in range(3):
        table[XPEN + 8 * g : XPEN + 8 * g + 8, :16] = x_penalty[g]
    for g in range(9):
        table[YPEN + 2 * g : YPEN + 2 * g + 2, :16] = y_penalty[g]
    rooted = jnp.sqrt(jnp.transpose(table[...]))[:24]
    half = lax.broadcasted_iota(jnp.int32, (24, 128), 1) < 64

    def spread(even, odd):
        left = jnp.broadcast_to(rooted[:, even : even + 1], (24, 128))
        right = jnp.broadcast_to(rooted[:, odd : odd + 1], (24, 128))
        return jnp.where(half, left, right)

    for i in range(4):
        for x in range(2):
            roots[0, i, x] = spread(COEF + 8 * x + 2 * i, COEF + 8 * x + 2 * i + 1)
            roots[1, i, x] = spread(XPEN + 16 * x + 2 * i, XPEN + 16 * x + 2 * i + 1)
            roots[2, i, x] = spread(XPEN + 8 + 2 * i, XPEN + 8 + 2 * i + 1)
            roots[3, i, x] = spread(YPEN + 2 * (2 * i + 1) + x, YPEN + 2 * (2 * i + 2) + x)
            roots[4, i, x] = spread(ZPEN + 8 * x + 2 * i, ZPEN + 8 * x + 2 * i + 1)
            roots[5, i, x] = jnp.where(half & (i == 0), jnp.broadcast_to(rooted[:, YPEN + x : YPEN + x + 1], (24, 128)), 0.0)
        roots_x[i] = roots[1, i, 0, :16]
    roots_y[...] = spread(YPEN, YPEN + 1)[:16]

    def relay(i, carry):
        for x in range(2):
            even = lane_tiles(deflation[x, 2 * i])
            odd = lane_tiles(deflation[x, 2 * i + 1])
            for n in range(64):
                a, b, c = n // 16, n // 4 % 4, n % 4
                both = paired(even, odd, NV * n)
                nodes[i, x, pl.ds(n, 16, stride=65), :] = both
                if b % 3 == 0:
                    sides[i, x, b // 3, pl.ds(4 * a + c, 16, stride=17), :] = both
        return carry

    lax.fori_loop(0, 4, relay, 0)
    total[...] = jnp.zeros_like(total)
    node = lax.broadcasted_iota(jnp.int32, (64, 128), 0)

    def edge(position):
        return jnp.where((position == 0) | (position == 3), LINE_WEIGHTS[0], LINE_WEIGHTS[1])

    weight = jnp.sqrt(edge(node // 16) * edge(node // 4 % 4) * edge(node % 4))
    first_half = lax.broadcasted_iota(jnp.int32, (16, 128), 1) < 64

    def fill(step, stack):
        s, i = step // 4, step % 4
        low = jnp.bfloat16

        def root(kind, x, z, rows):
            return jnp.broadcast_to(roots[kind, i, x, pl.ds(z, 1), :], (rows, 128))

        inner = []
        for zz in range(4):
            z = 4 * s + zz
            at = pl.ds(65 * z, 64)
            block = [nodes[i, x, at, :] for x in range(2)]
            z_rows = jnp.concatenate(block, axis=1).astype(low)
            product = jnp.dot(gradients[...], z_rows, preferred_element_type=jnp.float32)
            factor_z = jnp.concatenate([weight * root(0, x, z, 64) for x in range(2)], axis=1)
            for d in range(3):
                stack[192 * zz + 64 * d : 192 * zz + 64 * d + 64, :] = (product[64 * d : 64 * d + 64] * factor_z).astype(low)
            near = (block[0][:16] * root(1, 0, z, 16)).astype(low)
            far = (block[1][48:] * root(1, 1, z, 16)).astype(low)
            stack[768 + 16 * zz : 784 + 16 * zz, :] = jnp.concatenate([near, far], axis=1)
            here = pl.ds(17 * z, 16)
            there = pl.ds(pl.multiple_of(16 * z, 16), 16)
            own_x[i, there, :] = near
            inner.append((root(2, 0, z, 16) * (block[0][48:] - block[1][:16])).astype(low))
            lows, jumps = [], []
            after = jnp.minimum(i + 1, 3)
            for x in range(2):
                lower = sides[i, x, 0, here, :]
                swapped = pltpu.roll(lower, 64, 1)
                later = jnp.where(i < 3, pltpu.roll(sides[after, x, 0, here, :], 64, 1), 0.0)
                jumps.append((root(3, x, z, 16) * (sides[i, x, 1, here, :] - jnp.where(first_half, swapped, later))).astype(low))
                lows.append((root(5, x, z, 16) * lower).astype(low))
            stack[864 + 16 * zz : 880 + 16 * zz, :] = jnp.concatenate(jumps, axis=1)
            stack[928 + 16 * zz : 944 + 16 * zz, :] = jnp.concatenate(lows, axis=1)
            ups, firsts, befores = [], [], []
            for x in range(2):
                upper = nodes[i, x, pl.ds(65 * z + 3, 16, stride=4), :]
                if zz < 3:
                    upper = upper - nodes[i, x, pl.ds(65 * z + 65, 16, stride=4), :]
                ups.append((root(4, x, z + 1, 16) * upper).astype(low))
                if zz == 0:
                    firsts.append((root(4, x, z, 16) * nodes[i, x, pl.ds(65 * z, 16, stride=4), :]).astype(low))
                    before = nodes[i, x, pl.ds(65 * jnp.maximum(z - 1, 0) + 3, 16, stride=4), :]
                    befores.append(jnp.where(s > 0, root(4, x, z, 16) * before, 0.0).astype(low))
            stack[992 + 16 * zz : 1008 + 16 * zz, :] = jnp.concatenate(ups, axis=1)
            if zz == 0:
                stack[1056:1072, :] = jnp.concatenate(firsts, axis=1)
                row = pl.ds(pl.multiple_of(16 * i, 16), 16)
                low_z[s, row, :] = jnp.concatenate(firsts, axis=1)
                other_z[s, row, :] = jnp.concatenate(befores, axis=1)
        stack[832:848, :] = jnp.concatenate(inner[:2], axis=1)
        stack[848:864, :] = jnp.concatenate(inner[2:], axis=1)

    def add(step, stack):
        total[step // 4] += gram(stack[...], stack[...])

    second[...] = jnp.zeros_like(second)

    def pair(step, carry):
        add(jnp.maximum(2 * step - 1, 0), second)
        fill(2 * step, stack)
        add(2 * step, stack)
        fill(2 * step + 1, second)
        return carry

    lax.fori_loop(0, 8, pair, 0)
    add(15, second)

    def folded(square):
        return (
            square[:NV, :128]
            + pltpu.roll(square[64 : 64 + NV, :128], 64, 1)
            + square[128 : 128 + NV, 128:]
            + pltpu.roll(square[192 : 192 + NV, 128:], 64, 1)
        )

    for s in range(4):
        main[s, 0] = folded(total[s])
        below = -folded(gram(low_z[s], other_z[s]))
        main[s, 1] = below
        if s:
            main[s - 1, 2] = jnp.transpose(jnp.concatenate([below, jnp.zeros((80, 128), jnp.float32)], axis=0))[:NV]
    main[3, 2] = jnp.zeros((NV, 128), jnp.float32)
    for z in range(16):
        here = slice(16 * z, 16 * z + 16)
        there = slice(17 * z, 17 * z + 16)
        lower = [sides[0, x, 0, there, :] for x in range(2)]
        near = jnp.where(first_half, lower[0], pltpu.roll(lower[1], 64, 1))
        own_y[here, :] = (near * jnp.broadcast_to(roots_y[z : z + 1, :], (16, 128))).astype(jnp.bfloat16)


def assemble(deflation, gradients, coefficient, x_penalty, y_penalty, z_penalty):
    vmem = pl.BlockSpec(memory_space=pltpu.VMEM)
    f32, low = jnp.float32, jnp.bfloat16
    return pl.pallas_call(
        assemble_kernel,
        out_shape=(
            jax.ShapeDtypeStruct((4, 3, NV, 128), f32),
            jax.ShapeDtypeStruct((4, 256, 128), low),
            jax.ShapeDtypeStruct((256, 128), low),
            jax.ShapeDtypeStruct((4, 16, 128), f32),
            jax.ShapeDtypeStruct((16, 128), f32),
        ),
        in_specs=[vmem] * 6,
        out_specs=(vmem,) * 5,
        scratch_shapes=[
            pltpu.VMEM((4, 2, 1040, 128), f32),
            pltpu.VMEM((4, 2, 2, 272, 128), f32),
            pltpu.VMEM((1072, 256), low),
            pltpu.VMEM((1072, 256), low),
            pltpu.VMEM((4, 256, 256), f32),
            pltpu.VMEM((6, 4, 2, 24, 128), f32),
            pltpu.VMEM((4, 64, 256), low),
            pltpu.VMEM((4, 64, 256), low),
            pltpu.VMEM((128, 128), f32),
        ],
        cost_estimate=pl.CostEstimate(flops=2_000_000_000, bytes_accessed=3_000_000, transcendentals=0),
        name="assemble",
    )(deflation, gradients, coefficient, x_penalty, y_penalty, z_penalty)


def flipped(block):
    return jnp.transpose(jnp.concatenate([block, jnp.zeros((80, 128), jnp.float32)], axis=0))[:NV]


def lateral_kernel(order, meta, below_x, below_y, main, own_x, own_y, roots_x, roots_y, blocks, share, side, halo_x, halo_y):
    device = meta[0]
    low = jnp.bfloat16
    inside = lax.broadcasted_iota(jnp.int32, (NV, 128), 1) < NV

    def relay(i, carry):
        even = lane_tiles(below_x[2 * i])
        odd = lane_tiles(below_x[2 * i + 1])
        for m in range(16):
            halo_x[i, pl.ds(m, 16, stride=17), :] = paired(even, odd, NV * m) * roots_x[i]
        return carry

    lax.fori_loop(0, 4, relay, 0)
    even = lane_tiles(below_y[0])
    odd = lane_tiles(below_y[1])
    for m in range(16):
        n = 16 * (m // 4) + 12 + m % 4
        halo_y[pl.ds(m, 16, stride=17), :] = paired(even, odd, NV * n) * roots_y[...]

    def folded(square):
        return jnp.where(inside, -(square[:NV] + pltpu.roll(square[64 : 64 + NV], 64, 1)), 0.0)

    for s in range(SUB_DEV):
        at = slice(64 * s, 64 * s + 64)
        diag = jnp.where(inside, main[s, 0], 0.0)
        low_z = jnp.where(inside, main[s, 1], 0.0)
        mine = jnp.concatenate([own_x[i, at, :] for i in range(4)], axis=0)
        theirs = [halo_x[i, 17 * z : 17 * z + 16, :].astype(low) for i in range(4) for z in range(4 * s, 4 * s + 4)]
        low_x = folded(gram(mine, jnp.concatenate(theirs, axis=0)))
        theirs = [halo_y[17 * z : 17 * z + 16, :].astype(low) for z in range(4 * s, 4 * s + 4)]
        low_y = folded(gram(own_y[at, :], jnp.concatenate(theirs, axis=0)))
        blocks[s, 0] = diag
        blocks[s, 1] = low_x
        blocks[s, 2] = low_y
        blocks[s, 3] = low_z
        blocks[s, 4] = jnp.where(inside, main[s, 2], 0.0)
        here = device * SUB_DEV + s
        rank = order[here]
        turned_y = jnp.where(rank > order[jnp.maximum(here - SUB_DEV, 0)], low_y, flipped(low_y))
        turned_z = jnp.where(rank > order[jnp.maximum(here - 1, 0)], low_z, flipped(low_z))
        for kind, value in enumerate((diag, turned_y, turned_z)):
            row = (s % 2) * 3 + kind
            if s < 2:
                share[row] = value
            else:
                share[row] += pltpu.roll(value, 64, 1)
        if s < 2:
            side[s] = low_x
        else:
            side[s - 2] += pltpu.roll(low_x, 64, 1)


def lateral(order, meta, below_x, below_y, main, own_x, own_y, roots_x, roots_y):
    smem = pl.BlockSpec(memory_space=pltpu.SMEM)
    vmem = pl.BlockSpec(memory_space=pltpu.VMEM)
    f32 = jnp.float32
    return pl.pallas_call(
        lateral_kernel,
        out_shape=(
            jax.ShapeDtypeStruct((SUB_DEV, 5, NV, 128), f32),
            jax.ShapeDtypeStruct((6, NV, 128), f32),
            jax.ShapeDtypeStruct((2, NV, 128), f32),
        ),
        in_specs=[smem] * 2 + [vmem] * 7,
        out_specs=(vmem, vmem, vmem),
        scratch_shapes=[
            pltpu.VMEM((4, 272, 128), f32),
            pltpu.VMEM((272, 128), f32),
        ],
        name="lateral",
    )(order, meta, below_x, below_y, main, own_x, own_y, roots_x, roots_y)


def row_major(read, write):
    lane = lax.broadcasted_iota(jnp.int32, (8, 128), 1)
    for t in range(18):
        value = None
        for v in range(NV):
            shift = NV * v - 128 * t
            if shift <= -NV or shift >= 128:
                continue
            row = read(v)
            row = pltpu.roll(row, shift % 128, 1) if shift % 128 else row
            here = (lane >= shift) & (lane < shift + NV)
            value = jnp.where(here, row, 0.0 if value is None else value)
        write(t, value)


def flatten_kernel(order, meta, blocks, above, out, high_y, turned):
    device = meta[0]
    places = (0, 1, 3, 5, 6)
    for s in range(SUB_DEV):
        for kind in range(5):
            group = (SUB_DEV * kind + s) // 8
            turned[group, pl.ds((SUB_DEV * kind + s) % 8, NV, stride=8), :] = blocks[s, kind]
        packed_low = above[(s % 2) * 3 + 1]
        if s >= 2:
            packed_low = pltpu.roll(packed_low, 64, 1)
        packed_low = jnp.where(lax.broadcasted_iota(jnp.int32, (NV, 128), 1) < NV, packed_low, 0.0)
        here = device * SUB_DEV + s
        later = order[jnp.minimum(here + SUB_DEV, SUBS - 1)]
        upper = jnp.where(order[here] > later, packed_low, flipped(packed_low))
        high_y[s] = upper
        turned[2, pl.ds(SUB_DEV + s, NV, stride=8), :] = upper
    for group in range(3):
        low_place = places[2 * group]
        high_place = places[2 * group + 1] if group < 2 else 4

        def write(t, value):
            out[low_place, :, 128 * t : 128 * t + 128] = value[:4]
            out[high_place, :, 128 * t : 128 * t + 128] = value[4:]

        row_major(lambda v: turned[group, 8 * v : 8 * v + 8, :], write)


def flatten(order, meta, blocks, above):
    smem = pl.BlockSpec(memory_space=pltpu.SMEM)
    vmem = pl.BlockSpec(memory_space=pltpu.VMEM)
    return pl.pallas_call(
        flatten_kernel,
        out_shape=(
            jax.ShapeDtypeStruct((7, SUB_DEV, NV * NV), jnp.float32),
            jax.ShapeDtypeStruct((SUB_DEV, NV, 128), jnp.float32),
        ),
        in_specs=[smem] * 2 + [vmem] * 2,
        out_specs=(vmem, vmem),
        scratch_shapes=[pltpu.VMEM((3, NV * 8, 128), jnp.float32)],
        cost_estimate=pl.CostEstimate(flops=1_000_000, bytes_accessed=2_000_000, transcendentals=0),
        name="flatten",
    )(order, meta, blocks, above)


def eliminate(work, unit):
    groups = [work[8 * v : 8 * v + 8] for v in range(6)]
    sub = lax.broadcasted_iota(jnp.int32, (8, 128), 0)

    def row_of(value, k):
        return jnp.broadcast_to(value[k : k + 1, :], (8, 128))

    def column_of(value, k):
        return jnp.broadcast_to(value[:, k : k + 1], (8, 128))

    for g in range(6):
        head = groups[g]
        splat = [column_of(head, 64 + 8 * g + k) * unit for k in range(8)]
        below = [[column_of(groups[v], 64 + 8 * g + k) for k in range(8)] for v in range(g + 1, 6)]
        done = jnp.zeros((8, 128), jnp.float32)
        for k in range(0, 8, 2):
            x, y = splat[k], splat[k + 1]
            a, b, c = row_of(x, k), row_of(y, k), row_of(y, k + 1)
            inverse = 1.0 / (a * c - b * b)
            ratio = b / a
            top, low = row_of(head, k), row_of(head, k + 1)
            done = jnp.where(sub == k, top * lax.rsqrt(a), done)
            done = jnp.where(sub == k + 1, (low - ratio * top) * lax.rsqrt(c - ratio * b), done)

            def reduced(value, upper, lower):
                one = (c * upper - b * lower) * inverse
                two = (a * lower - b * upper) * inverse
                return jnp.where(sub == k, one, jnp.where(sub == k + 1, two, value - x * one - y * two))

            for m in range(k + 2, 8):
                splat[m] = reduced(splat[m], row_of(splat[m], k), row_of(splat[m], k + 1))
            head = reduced(head, top, low)
        rows = [row_of(head, k) for k in range(8)]
        for v in range(g + 1, 6):
            terms = [s * r for s, r in zip(below[v - g - 1], rows)]
            while len(terms) > 1:
                terms = [p + q for p, q in zip(terms[::2], terms[1::2])]
            groups[v] = groups[v] - terms[0]
        groups[g] = done
    return jnp.concatenate(groups, axis=0)


def halves(values):
    high = values.astype(jnp.bfloat16)
    low = (values - high.astype(jnp.float32)).astype(jnp.bfloat16)
    return high, low


def across(left, right):
    return lax.dot_general(left, right, (((1,), (1,)), ((), ())), preferred_element_type=jnp.float32)


ROWS = SUB_DEV * NV
BAND = 4


def factor_kernel(order, meta, own, right1, right2, right3, left1, left2, left3, below, above, rescue, blocks, high_y, flat_in, out, flat, grid, got, lhs, rhs, binv, side, high_x, turned, slab, sems, side_sems):
    device = meta[0]
    lane = lax.broadcasted_iota(jnp.int32, (NV, 128), 1)

    def place(value, half, row, column, wanted):
        parity = column % 2
        moved = pltpu.roll(value, 64 * ((parity + half) % 2), 1)
        inside = (lane >= 64 * parity) & (lane < 64 * parity + NV)
        tile = jnp.where(wanted, column // 2, 7)
        at = pl.ds(pl.multiple_of(jnp.where(wanted, row, 0), 16), NV)
        pltpu.store(grid.at[tile, at, :], moved, mask=inside)

    def ordered(subdomain):
        return order[jnp.clip(subdomain, 0, SUBS - 1)]

    def neighbours(subdomain):
        column = (subdomain // SUB_DEV) % N_COL
        local = subdomain % SUB_DEV
        stride = N_COL * SUB_DEV
        return (
            (subdomain, subdomain >= 0),
            (subdomain - stride, subdomain >= stride),
            (subdomain + stride, (subdomain >= 0) & (subdomain < SUBS - stride)),
            (subdomain - SUB_DEV, (subdomain >= 0) & (column > 0)),
            (subdomain + SUB_DEV, (subdomain >= 0) & (column < N_COL - 1)),
            (subdomain - 1, (subdomain >= 0) & (local > 0)),
            (subdomain + 1, (subdomain >= 0) & (local < SUB_DEV - 1)),
        )

    relevant = jnp.int32(0)
    for l in range(SUB_DEV):
        for near, there in neighbours(device * SUB_DEV + l):
            relevant += (there & (ordered(near) < PB)).astype(jnp.int32)

    side_copy = pltpu.make_async_copy(above.at[pl.ds(18, 2)], side, side_sems.at[0])
    side_copy.start()

    @pl.when(relevant > 0)
    def _():
        near_sources = [right3, right2, right1, own, left1, left2, left3]
        for case in range(5):

            @pl.when(meta[1] == case)
            def _():
                for i in range(3):
                    pltpu.make_async_copy(near_sources[case + i], got.at[i], sems.at[i]).start()

        for case, source in ((5, below), (6, above), (7, rescue)):

            @pl.when(meta[1] == case)
            def _():
                for i in range(3):
                    pltpu.make_async_copy(source.at[pl.ds(6 * i, 6)], got.at[i], sems.at[i]).start()

        pltpu.make_async_copy(rescue.at[pl.ds(18, 6)], got.at[3], sems.at[3]).start()

    side_copy.wait()
    for s in range(SUB_DEV):
        packed_low = side[s % 2]
        if s >= 2:
            packed_low = pltpu.roll(packed_low, 64, 1)
        upper = flipped(jnp.where(lane < NV, packed_low, 0.0))
        high_x[s] = upper
        turned[pl.ds(s, NV, stride=8), :] = upper

    def write(t, value):
        slab[:, 128 * t : 128 * t + 128] = value[:4]

    row_major(lambda v: turned[8 * v : 8 * v + 8, :], write)
    flat_copy = pltpu.make_async_copy(slab, flat.at[2], side_sems.at[1])
    flat_copy.start()

    @pl.when(relevant == 0)
    def _():
        out[...] = jnp.zeros_like(out)

    @pl.when(relevant > 0)
    def _():
        grid[:6, : ROWS + PB * NV + BAND * NV, :] = jnp.zeros((6, ROWS + PB * NV + BAND * NV, 128), jnp.float32)
        rhs[...] = jnp.zeros_like(rhs)
        lhs[...] = jnp.zeros_like(lhs)
        for l in range(SUB_DEV):
            for kind, (near, there) in enumerate(neighbours(device * SUB_DEV + l)):
                column = ordered(near)
                value = (blocks.at[l, 0], blocks.at[l, 1], high_x.at[l], blocks.at[l, 2], high_y.at[l], blocks.at[l, 3], blocks.at[l, 4])[kind][...]
                place(value, 0, NV * l, column, there & (column < PB))
        for i in range(4):
            pltpu.make_async_copy(own, got.at[i], sems.at[i]).wait()
        reach = jnp.int32(0)
        for slot in range(12):
            i, l = slot // SUB_DEV, slot % SUB_DEV
            s = meta[4 + slot]
            p = ordered(s)
            near = neighbours(s)
            for kind, (t, there) in enumerate((near[0], near[3], near[5], near[1])):
                q = ordered(t)
                wanted = there & (p < PB) & (q < PB)
                reach = jnp.maximum(reach, jnp.where(wanted, jnp.abs(p - q), 0))
                if kind < 3:
                    value, half = got[i, (l % 2) * 3 + kind], l // 2
                else:
                    value, half = got[3, slot % 6], slot // 6
                place(value, half, ROWS + NV * jnp.maximum(p, q), jnp.minimum(p, q), wanted)

        rows48 = lax.broadcasted_iota(jnp.int32, (NV, 128), 0)

        unit = jnp.full((8, 128), jnp.where(device >= 0, 1.0, 0.0), jnp.float32)

        gap = jnp.zeros((16, 128), jnp.bfloat16)

        def diagonal(k):
            at = pl.ds(pl.multiple_of(ROWS + k * NV, 16), NV)
            return pltpu.roll(grid[k // 2, at, :], 64 * (1 - k % 2), 1)

        def invert(k, diag):
            work = jnp.where(lane < 64, (lane == rows48).astype(jnp.float32), jnp.where(lane < 64 + NV, diag, 0.0))
            inverse = jnp.where(lane < NV, eliminate(work, unit), 0.0)
            high, low = halves(pltpu.roll(inverse, 64 * (k % 2), 1))
            high = jnp.concatenate([high, gap, high, gap], axis=0)
            low = jnp.concatenate([low, gap, low, gap], axis=0)
            binv[0] = high
            binv[1] = low
            return high, low

        def solve(values, high, low):
            c_high, c_low = halves(values)
            return across(jnp.concatenate([c_high, c_low], axis=1), jnp.concatenate([high, high], axis=1)) + across(c_high, low)

        def mix(high, low):
            left_half = lax.broadcasted_iota(jnp.int32, high.shape, 1) < 64
            return jnp.where(left_half, high.astype(jnp.float32), low.astype(jnp.float32)).astype(jnp.bfloat16)

        def urgent(k, high, low):
            at = pl.ds(pl.multiple_of(ROWS + (k + 1) * NV, 16), NV)
            s_high, s_low = halves(solve(grid[k // 2, at, :], high, low))
            mixed = mix(s_high, s_low)
            nothing = jnp.zeros_like(mixed)
            even = (k + 1) % 2 == 0
            other = jnp.concatenate([jnp.where(even, mixed, nothing), gap, jnp.where(even, nothing, mixed), gap], axis=0)
            grid[(k + 1) // 2, at, :] -= across(jnp.concatenate([s_high, s_low], axis=1), jnp.concatenate([other, other], axis=1))

        def finish(band, k, live):
            tile = k // 2
            depth = ROWS + band * NV
            window = pl.ds(pl.multiple_of(ROWS + k * NV, 16), NV + band * NV)
            later = pl.ds(pl.multiple_of(ROWS + (k + 1) * NV, 16), band * NV)
            at = pl.ds(pl.multiple_of(ROWS + k * NV, 16), NV)
            column = jnp.concatenate([grid[tile, :ROWS, :], grid[tile, window, :]], axis=0)
            solved = solve(column, binv[0], binv[1])
            corner = jnp.where((lane % 64) <= rows48, solved[ROWS : ROWS + NV], 0.0)
            parity = jnp.where(live, k % 2, 2)
            rest = jnp.concatenate([solved[:ROWS], solved[ROWS + NV :]], axis=0)
            chosen = lax.broadcasted_iota(jnp.int32, (depth, 128), 1) // 64 == parity
            kept = jnp.where(chosen, rest, jnp.concatenate([column[:ROWS], column[ROWS + NV :]], axis=0))
            grid[tile, :ROWS, :] = kept[:ROWS]
            grid[tile, later, :] = kept[ROWS:]
            grid[tile, at, :] = jnp.where(lane // 64 == parity, corner, column[ROWS : ROWS + NV])
            s_high, s_low = halves(rest)
            lhs[:depth, :128] = s_high
            lhs[:depth, 128:] = s_low
            mixed = mix(s_high[ROWS:], s_low[ROWS:])
            rhs[pl.ds(pl.multiple_of(64 * k, 64), 64), :] = jnp.zeros((64, 128), jnp.bfloat16)
            for w in range(band):
                rhs[pl.ds(pl.multiple_of(64 * (k + 1 + w), 64), NV), :] = mixed[NV * w : NV * w + NV]

        def trail(band, k, t, skip):
            depth = ROWS + band * NV
            later = pl.ds(pl.multiple_of(ROWS + (k + 1 + skip) * NV, 16), (band - skip) * NV)
            other = rhs[pl.ds(pl.multiple_of(128 * t, 128), 128), :]
            other = jnp.concatenate([other, other], axis=1)
            grid[t, :ROWS, :] -= across(lhs[:ROWS, :], other)
            grid[t, later, :] -= across(lhs[ROWS + skip * NV : depth, :], other)

        @pl.when(reach <= BAND)
        def _():
            binv[...] = jnp.zeros_like(binv)

            def body(k, carry):
                diag = diagonal(k)
                last = jnp.maximum(k - 1, 0)
                finish(BAND, last, k > 0)
                for j in range(3):
                    trail(BAND, last, k // 2 + j, 1 if j == 0 else 0)
                high, low = invert(k, diag)
                urgent(k, high, low)
                return carry

            lax.fori_loop(0, PB, body, 0)
            finish(BAND, PB - 1, True)

        @pl.when(reach > BAND)
        def _():
            start = ROWS + PB * NV + BAND * NV
            grid[:6, start:, :] = jnp.zeros((6, grid.shape[1] - start, 128), jnp.float32)

            def body(k, carry):
                invert(k, diagonal(k))
                finish(PB - 1, k, True)

                def inner(t, c):
                    trail(PB - 1, k, t, 0)
                    return c

                lax.fori_loop((k + 1) // 2, 6, inner, 0)
                return carry

            lax.fori_loop(0, PB, body, 0)

        for l in range(SUB_DEV):
            p = ordered(device * SUB_DEV + l)
            inside = p < PB
            start = jnp.where(inside, ROWS + NV * p, NV * l)
            at = pl.ds(pl.multiple_of(start, 16), NV)
            pieces = []
            for j in range(PB):
                piece = grid[j // 2, at, :][:, 64 * (j % 2) : 64 * (j % 2) + NV]
                pieces.append(jnp.where(inside & (j > p), 0.0, piece))
            out[l] = jnp.concatenate(pieces, axis=1)

    flat_copy.wait()


def factor(order, meta, shares, below, above, rescue, blocks, high_y, flat):
    smem = pl.BlockSpec(memory_space=pltpu.SMEM)
    hbm = pl.BlockSpec(memory_space=pl.ANY)
    vmem = pl.BlockSpec(memory_space=pltpu.VMEM)
    return pl.pallas_call(
        factor_kernel,
        out_shape=(
            jax.ShapeDtypeStruct((SUB_DEV, NV, PB * NV), jnp.float32),
            jax.ShapeDtypeStruct(flat.shape, jnp.float32),
        ),
        in_specs=[smem] * 2 + [hbm] * 10 + [vmem] * 2 + [hbm],
        out_specs=(vmem, hbm),
        input_output_aliases={14: 1},
        scratch_shapes=[
            pltpu.VMEM((8, ROWS + PB * NV + PB * NV, 128), jnp.float32),
            pltpu.VMEM((4, 6, NV, 128), jnp.float32),
            pltpu.VMEM((ROWS + (PB - 1) * NV, 256), jnp.bfloat16),
            pltpu.VMEM(((2 * PB + 2) * 64, 128), jnp.bfloat16),
            pltpu.VMEM((2, 128, 128), jnp.bfloat16),
            pltpu.VMEM((2, NV, 128), jnp.float32),
            pltpu.VMEM((SUB_DEV, NV, 128), jnp.float32),
            pltpu.VMEM((NV * 8, 128), jnp.float32),
            pltpu.VMEM((SUB_DEV, NV * NV), jnp.float32),
            pltpu.SemaphoreType.DMA((4,)),
            pltpu.SemaphoreType.DMA((2,)),
        ],
        name="factor",
    )(order, meta, *shares, below, above, rescue, blocks, high_y, flat)


def shifted(value, amount):
    size = N_ROW * N_COL
    return lax.ppermute(value, ("row", "col"), [(i, (i + amount) % size) for i in range(size)])


def packed(blocks):
    wide = jnp.pad(blocks, ((0, 0), (0, 0), (0, 64 - NV)))
    return jnp.concatenate([wide[:6], wide[6:]], axis=2)


def everywhere(value):
    size = N_ROW * N_COL
    step = 1
    while step < size:
        value = value + lax.ppermute(value, ("row", "col"), [(i, i ^ step) for i in range(size)])
        step *= 2
    return value


def exchange(device, order, meta_lateral, blocks, share, side):
    subdomain = jnp.arange(SUBS, dtype=jnp.int32)
    first = jnp.sum(jnp.where(order == 0, subdomain // SUB_DEV, 0))
    size = N_ROW * N_COL
    distance = (subdomain // SUB_DEV - first + size // 2) % size - size // 2
    inside = order < PB
    least = jnp.min(jnp.where(inside, distance, size))
    most = jnp.max(jnp.where(inside, distance, -size))
    near = (most - least) <= 2
    base = (first + least) % size
    mine = device * SUB_DEV + jnp.arange(SUB_DEV, dtype=jnp.int32)
    my_order = lax.dynamic_slice(order, (device * SUB_DEV,), (SUB_DEV,))

    right1 = shifted(share, 1)
    left1 = shifted(share, -1)
    right2 = shifted(share, 2)
    left2 = shifted(share, -2)
    offset = (base - device + size // 2) % size - size // 2
    window = jnp.where(
        offset == 0,
        jnp.stack([share, left1, left2]),
        jnp.where(offset == -1, jnp.stack([right1, share, left1]), jnp.stack([right2, right1, share])),
    )
    payload = jnp.concatenate([window.reshape(18, NV, 128), side], axis=0)
    below = shifted(payload, N_COL)
    above = shifted(payload, -N_COL)
    flat, high_y = flatten(order, meta_lateral, blocks, left1)
    right3 = shifted(right2, 1)
    left3 = shifted(left2, -1)
    from_below = (offset + N_COL + 2) % size <= 2
    from_above = (offset - N_COL + 2) % size <= 2
    beside = (offset >= -3) & (offset <= 1)
    pick = jnp.where(beside, offset + 3, jnp.where(from_below, 5, jnp.where(from_above, 6, 0)))
    pick = jnp.where(near, pick, 7)

    def local_path(_):
        listed = (base * SUB_DEV + jnp.arange(12, dtype=jnp.int32)) % SUBS
        return (jnp.zeros((24, NV, 128), jnp.float32), listed)

    def global_path(_):
        slots = jnp.arange(12, dtype=jnp.int32)
        hit = (order[None, :] == slots[:, None]) & (slots[:, None] < PB)
        listed = jnp.where(slots < PB, jnp.sum(jnp.where(hit, subdomain[None, :], 0), axis=1), -1)
        mask = ((my_order[None, :] == slots[:, None]) & (slots[:, None] < PB)).astype(jnp.float32)
        def oriented(block, offset):
            other = lax.dynamic_slice(jnp.concatenate([order[:128], order]), (128 + device * SUB_DEV - offset,), (SUB_DEV,))
            return jnp.where((my_order > other)[:, None, None], block, jnp.swapaxes(block, 1, 2))

        kinds = jnp.stack(
            [
                blocks[:, 0, :, :NV],
                oriented(blocks[:, 2, :, :NV], SUB_DEV),
                oriented(blocks[:, 3, :, :NV], 1),
                oriented(blocks[:, 1, :, :NV], N_COL * SUB_DEV),
            ],
            axis=1,
        )
        placed = jnp.einsum("ps,skvw->pkvw", mask, kinds, precision=lax.Precision.HIGHEST)
        whole = everywhere(
            jnp.stack([packed(placed[4 * i : 4 * i + 4, :3].reshape(12, NV, NV)) for i in range(3)] + [packed(placed[:, 3])])
        )
        return (whole.reshape(24, NV, 128), listed)

    rescue, listed = lax.cond(near, local_path, global_path, None)
    meta = jnp.concatenate([jnp.stack([device, pick, jnp.int32(0), jnp.int32(0)]), listed]).astype(jnp.int32)
    shares = (share, right1, right2, right3, left1, left2, left3)
    panel, flat = factor(order, meta, shares, below, above, rescue, blocks, high_y, flat)
    return (jnp.transpose(flat, (1, 0, 2)), panel)


def from_next(value, axis, amount):
    size = lax.axis_size(axis)
    pairs = [(i, i + amount) for i in range(size) if 0 <= i + amount < size]
    return lax.ppermute(value, axis, pairs)


def shards(deflation, coefficient, gradients, x_penalty, y_penalty, z_penalty, coarse_order):
    device = (lax.axis_index("row") * N_COL + lax.axis_index("col")).astype(jnp.int32)
    below_x = from_next(deflation[1, :, :, 48 * NV :], "row", 1)
    below_y = from_next(deflation[:, 7], "col", 1)
    main, own_x, own_y, roots_x, roots_y = assemble(
        deflation, gradients.reshape(192, 64), coefficient, x_penalty, jnp.transpose(y_penalty, (1, 0, 2)), z_penalty
    )
    meta = jnp.full((8,), device, jnp.int32)
    blocks, share, side = lateral(coarse_order, meta, below_x, below_y, main, own_x, own_y, roots_x, roots_y)
    return exchange(device, coarse_order, meta, blocks, share, side)


def solution(mesh):
    in_specs = (
        P("row", "col", None, None),
        P("row", "col", None),
        P(),
        P("row", "col", None),
        P("row", "col", None),
        P("row", "col", None),
        P(),
    )
    out_specs = (P(("row", "col"), None, None), P(("row", "col"), None, None))
    return jax.shard_map(shards, mesh=mesh, in_specs=in_specs, out_specs=out_specs, check_vma=False)
```

```python
import jax
import jax.numpy as jnp
from jax import lax
from jax.experimental import pallas as pl
from jax.experimental.pallas import tpu as pltpu
from jax.sharding import PartitionSpec as P

NV = 48
SUB_DEV = 4
PB = 11
SUBS = 1024
N_ROW = 8
N_COL = 32


LINE_WEIGHTS = (1.0 / 6.0, 5.0 / 6.0, 5.0 / 6.0, 1.0 / 6.0)
COEF, XPEN, YPEN, ZPEN = 0, 16, 40, 58


def fetch(tiles, start, target):
    lane = lax.broadcasted_iota(jnp.int32, tiles[0].shape, 1)
    tile, offset = start // 128, start % 128
    shift = (target - offset) % 128
    first = pltpu.roll(tiles[tile], shift, 1) if shift else tiles[tile]
    if offset + NV <= 128:
        return first
    second = pltpu.roll(tiles[tile + 1], shift, 1) if shift else tiles[tile + 1]
    return jnp.where(lane >= target + 128 - offset, second, first)


def paired(even, odd, start):
    lane = lax.broadcasted_iota(jnp.int32, even[0].shape, 1)
    return jnp.where(lane < 64, fetch(even, start, 0), fetch(odd, start, 64))


def lane_tiles(values):
    wide = values.astype(jnp.float32)
    return [wide[:, 128 * t : 128 * t + 128] for t in range(wide.shape[1] // 128)]


def gram(left, right):
    return lax.dot_general(left, right, (((0,), (0,)), ((), ())), preferred_element_type=jnp.float32)


def assemble_kernel(deflation, gradients, coefficient, x_penalty, y_penalty, z_penalty, main, own_x, own_y, roots_x, roots_y, nodes, sides, stack, second, total, roots, low_z, other_z, table):
    table[...] = jnp.zeros_like(table)
    for x in range(2):
        table[COEF + 8 * x : COEF + 8 * x + 8, :16] = coefficient[x]
        table[ZPEN + 8 * x : ZPEN + 8 * x + 8, :17] = z_penalty[x]
    for g in range(3):
        table[XPEN + 8 * g : XPEN + 8 * g + 8, :16] = x_penalty[g]
    for g in range(9):
        table[YPEN + 2 * g : YPEN + 2 * g + 2, :16] = y_penalty[g]
    rooted = jnp.sqrt(jnp.transpose(table[...]))[:24]
    half = lax.broadcasted_iota(jnp.int32, (24, 128), 1) < 64

    def spread(even, odd):
        left = jnp.broadcast_to(rooted[:, even : even + 1], (24, 128))
        right = jnp.broadcast_to(rooted[:, odd : odd + 1], (24, 128))
        return jnp.where(half, left, right)

    for i in range(4):
        for x in range(2):
            roots[0, i, x] = spread(COEF + 8 * x + 2 * i, COEF + 8 * x + 2 * i + 1)
            roots[1, i, x] = spread(XPEN + 16 * x + 2 * i, XPEN + 16 * x + 2 * i + 1)
            roots[2, i, x] = spread(XPEN + 8 + 2 * i, XPEN + 8 + 2 * i + 1)
            roots[3, i, x] = spread(YPEN + 2 * (2 * i + 1) + x, YPEN + 2 * (2 * i + 2) + x)
            roots[4, i, x] = spread(ZPEN + 8 * x + 2 * i, ZPEN + 8 * x + 2 * i + 1)
            roots[5, i, x] = jnp.where(half & (i == 0), jnp.broadcast_to(rooted[:, YPEN + x : YPEN + x + 1], (24, 128)), 0.0)
        roots_x[i] = roots[1, i, 0, :16]
    roots_y[...] = spread(YPEN, YPEN + 1)[:16]

    def relay(i, carry):
        for x in range(2):
            even = lane_tiles(deflation[x, 2 * i])
            odd = lane_tiles(deflation[x, 2 * i + 1])
            for n in range(64):
                a, b, c = n // 16, n // 4 % 4, n % 4
                both = paired(even, odd, NV * n)
                nodes[i, x, pl.ds(n, 16, stride=65), :] = both
                if b % 3 == 0:
                    sides[i, x, b // 3, pl.ds(4 * a + c, 16, stride=17), :] = both
        return carry

    lax.fori_loop(0, 4, relay, 0)
    total[...] = jnp.zeros_like(total)
    node = lax.broadcasted_iota(jnp.int32, (64, 128), 0)

    def edge(position):
        return jnp.where((position == 0) | (position == 3), LINE_WEIGHTS[0], LINE_WEIGHTS[1])

    weight = jnp.sqrt(edge(node // 16) * edge(node // 4 % 4) * edge(node % 4))
    first_half = lax.broadcasted_iota(jnp.int32, (16, 128), 1) < 64

    def fill(step, stack):
        s, i = step // 4, step % 4
        low = jnp.bfloat16

        def root(kind, x, z, rows):
            return jnp.broadcast_to(roots[kind, i, x, pl.ds(z, 1), :], (rows, 128))

        inner = []
        for zz in range(4):
            z = 4 * s + zz
            at = pl.ds(65 * z, 64)
            block = [nodes[i, x, at, :] for x in range(2)]
            z_rows = jnp.concatenate(block, axis=1).astype(low)
            product = jnp.dot(gradients[...], z_rows, preferred_element_type=jnp.float32)
            factor_z = jnp.concatenate([weight * root(0, x, z, 64) for x in range(2)], axis=1)
            for d in range(3):
                stack[192 * zz + 64 * d : 192 * zz + 64 * d + 64, :] = (product[64 * d : 64 * d + 64] * factor_z).astype(low)
            near = (block[0][:16] * root(1, 0, z, 16)).astype(low)
            far = (block[1][48:] * root(1, 1, z, 16)).astype(low)
            stack[768 + 16 * zz : 784 + 16 * zz, :] = jnp.concatenate([near, far], axis=1)
            here = pl.ds(17 * z, 16)
            there = pl.ds(pl.multiple_of(16 * z, 16), 16)
            own_x[i, there, :] = near
            inner.append((root(2, 0, z, 16) * (block[0][48:] - block[1][:16])).astype(low))
            lows, jumps = [], []
            after = jnp.minimum(i + 1, 3)
            for x in range(2):
                lower = sides[i, x, 0, here, :]
                swapped = pltpu.roll(lower, 64, 1)
                later = jnp.where(i < 3, pltpu.roll(sides[after, x, 0, here, :], 64, 1), 0.0)
                jumps.append((root(3, x, z, 16) * (sides[i, x, 1, here, :] - jnp.where(first_half, swapped, later))).astype(low))
                lows.append((root(5, x, z, 16) * lower).astype(low))
            stack[864 + 16 * zz : 880 + 16 * zz, :] = jnp.concatenate(jumps, axis=1)
            stack[928 + 16 * zz : 944 + 16 * zz, :] = jnp.concatenate(lows, axis=1)
            ups, firsts, befores = [], [], []
            for x in range(2):
                upper = nodes[i, x, pl.ds(65 * z + 3, 16, stride=4), :]
                if zz < 3:
                    upper = upper - nodes[i, x, pl.ds(65 * z + 65, 16, stride=4), :]
                ups.append((root(4, x, z + 1, 16) * upper).astype(low))
                if zz == 0:
                    firsts.append((root(4, x, z, 16) * nodes[i, x, pl.ds(65 * z, 16, stride=4), :]).astype(low))
                    before = nodes[i, x, pl.ds(65 * jnp.maximum(z - 1, 0) + 3, 16, stride=4), :]
                    befores.append(jnp.where(s > 0, root(4, x, z, 16) * before, 0.0).astype(low))
            stack[992 + 16 * zz : 1008 + 16 * zz, :] = jnp.concatenate(ups, axis=1)
            if zz == 0:
                stack[1056:1072, :] = jnp.concatenate(firsts, axis=1)
                row = pl.ds(pl.multiple_of(16 * i, 16), 16)
                low_z[s, row, :] = jnp.concatenate(firsts, axis=1)
                other_z[s, row, :] = jnp.concatenate(befores, axis=1)
        stack[832:848, :] = jnp.concatenate(inner[:2], axis=1)
        stack[848:864, :] = jnp.concatenate(inner[2:], axis=1)

    def add(step, stack):
        total[step // 4] += gram(stack[...], stack[...])

    second[...] = jnp.zeros_like(second)

    def pair(step, carry):
        add(jnp.maximum(2 * step - 1, 0), second)
        fill(2 * step, stack)
        add(2 * step, stack)
        fill(2 * step + 1, second)
        return carry

    lax.fori_loop(0, 8, pair, 0)
    add(15, second)

    def folded(square):
        return (
            square[:NV, :128]
            + pltpu.roll(square[64 : 64 + NV, :128], 64, 1)
            + square[128 : 128 + NV, 128:]
            + pltpu.roll(square[192 : 192 + NV, 128:], 64, 1)
        )

    for s in range(4):
        main[s, 0] = folded(total[s])
        below = -folded(gram(low_z[s], other_z[s]))
        main[s, 1] = below
        if s:
            main[s - 1, 2] = jnp.transpose(jnp.concatenate([below, jnp.zeros((80, 128), jnp.float32)], axis=0))[:NV]
    main[3, 2] = jnp.zeros((NV, 128), jnp.float32)
    for z in range(16):
        here = slice(16 * z, 16 * z + 16)
        there = slice(17 * z, 17 * z + 16)
        lower = [sides[0, x, 0, there, :] for x in range(2)]
        near = jnp.where(first_half, lower[0], pltpu.roll(lower[1], 64, 1))
        own_y[here, :] = (near * jnp.broadcast_to(roots_y[z : z + 1, :], (16, 128))).astype(jnp.bfloat16)


def assemble(deflation, gradients, coefficient, x_penalty, y_penalty, z_penalty):
    vmem = pl.BlockSpec(memory_space=pltpu.VMEM)
    f32, low = jnp.float32, jnp.bfloat16
    return pl.pallas_call(
        assemble_kernel,
        out_shape=(
            jax.ShapeDtypeStruct((4, 3, NV, 128), f32),
            jax.ShapeDtypeStruct((4, 256, 128), low),
            jax.ShapeDtypeStruct((256, 128), low),
            jax.ShapeDtypeStruct((4, 16, 128), f32),
            jax.ShapeDtypeStruct((16, 128), f32),
        ),
        in_specs=[vmem] * 6,
        out_specs=(vmem,) * 5,
        scratch_shapes=[
            pltpu.VMEM((4, 2, 1040, 128), f32),
            pltpu.VMEM((4, 2, 2, 272, 128), f32),
            pltpu.VMEM((1072, 256), low),
            pltpu.VMEM((1072, 256), low),
            pltpu.VMEM((4, 256, 256), f32),
            pltpu.VMEM((6, 4, 2, 24, 128), f32),
            pltpu.VMEM((4, 64, 256), low),
            pltpu.VMEM((4, 64, 256), low),
            pltpu.VMEM((128, 128), f32),
        ],
        cost_estimate=pl.CostEstimate(flops=2_000_000_000, bytes_accessed=3_000_000, transcendentals=0),
        name="assemble",
    )(deflation, gradients, coefficient, x_penalty, y_penalty, z_penalty)


def device_index():
    return (lax.axis_index("row") * N_COL + lax.axis_index("col")).astype(jnp.int32)


def flipped(block):
    return jnp.transpose(jnp.concatenate([block, jnp.zeros((80, 128), jnp.float32)], axis=0))[:NV]


def lateral_kernel(order, below_x, below_y, main, own_x, own_y, roots_x, roots_y, blocks, share, side, halo_x, halo_y):
    device = device_index()
    low = jnp.bfloat16
    inside = lax.broadcasted_iota(jnp.int32, (NV, 128), 1) < NV

    def relay(i, carry):
        even = lane_tiles(below_x[2 * i])
        odd = lane_tiles(below_x[2 * i + 1])
        for m in range(16):
            halo_x[i, pl.ds(m, 16, stride=17), :] = paired(even, odd, NV * m) * roots_x[i]
        return carry

    lax.fori_loop(0, 4, relay, 0)
    even = lane_tiles(below_y[0])
    odd = lane_tiles(below_y[1])
    for m in range(16):
        n = 16 * (m // 4) + 12 + m % 4
        halo_y[pl.ds(m, 16, stride=17), :] = paired(even, odd, NV * n) * roots_y[...]

    def folded(square):
        return jnp.where(inside, -(square[:NV] + pltpu.roll(square[64 : 64 + NV], 64, 1)), 0.0)

    diags, low_ys, low_zs = [], [], []
    for s in range(SUB_DEV):
        at = slice(64 * s, 64 * s + 64)
        diag = jnp.where(inside, main[s, 0], 0.0)
        low_z = jnp.where(inside, main[s, 1], 0.0)
        mine = jnp.concatenate([own_x[i, at, :] for i in range(4)], axis=0)
        theirs = [halo_x[i, 17 * z : 17 * z + 16, :].astype(low) for i in range(4) for z in range(4 * s, 4 * s + 4)]
        low_x = folded(gram(mine, jnp.concatenate(theirs, axis=0)))
        theirs = [halo_y[17 * z : 17 * z + 16, :].astype(low) for z in range(4 * s, 4 * s + 4)]
        low_y = folded(gram(own_y[at, :], jnp.concatenate(theirs, axis=0)))
        blocks[s, 0] = diag
        blocks[s, 1] = low_x
        blocks[s, 2] = low_y
        blocks[s, 3] = low_z
        blocks[s, 4] = jnp.where(inside, main[s, 2], 0.0)
        here = device * SUB_DEV + s
        rank = order[here]
        turned_y = jnp.where(rank > order[jnp.maximum(here - SUB_DEV, 0)], low_y, flipped(low_y))
        turned_z = jnp.where(rank > order[jnp.maximum(here - 1, 0)], low_z, flipped(low_z))
        diags.append(diag)
        low_ys.append(turned_y)
        low_zs.append(turned_z)
        if s < 2:
            side[s] = low_x
        else:
            side[s - 2] += pltpu.roll(low_x, 64, 1)
    lane = lax.broadcasted_iota(jnp.int32, (NV, 128), 1)
    row = lax.broadcasted_iota(jnp.int32, (NV, 128), 0)

    def both(lower, upper):
        last = jnp.sum(jnp.where(lane == row, upper, 0.0), axis=1, keepdims=True)
        return jnp.where(lane <= row, lower, upper) + jnp.where(lane == NV, jnp.broadcast_to(last, (NV, 128)), 0.0)

    def piece(start, target):
        moved = pltpu.roll(low_zs[3], (target - start) % 128, 1)
        return jnp.where((lane >= target) & (lane < target + 16), moved, 0.0)

    share[0] = both(diags[0], diags[1]) + pltpu.roll(both(diags[2], diags[3]), 64, 1)
    share[1] = low_ys[0] + pltpu.roll(low_ys[2], 64, 1) + piece(0, 48) + piece(16, 112)
    share[2] = low_ys[1] + pltpu.roll(low_ys[3], 64, 1) + piece(32, 48)
    share[3] = low_zs[1] + pltpu.roll(low_zs[2], 64, 1)


def lateral(order, below_x, below_y, main, own_x, own_y, roots_x, roots_y):
    smem = pl.BlockSpec(memory_space=pltpu.SMEM)
    vmem = pl.BlockSpec(memory_space=pltpu.VMEM)
    f32 = jnp.float32
    return pl.pallas_call(
        lateral_kernel,
        out_shape=(
            jax.ShapeDtypeStruct((SUB_DEV, 5, NV, 128), f32),
            jax.ShapeDtypeStruct((4, NV, 128), f32),
            jax.ShapeDtypeStruct((2, NV, 128), f32),
        ),
        in_specs=[smem] + [vmem] * 7,
        out_specs=(vmem, vmem, vmem),
        scratch_shapes=[
            pltpu.VMEM((4, 272, 128), f32),
            pltpu.VMEM((272, 128), f32),
        ],
        name="lateral",
    )(order, below_x, below_y, main, own_x, own_y, roots_x, roots_y)


def row_major(read, write):
    lane = lax.broadcasted_iota(jnp.int32, (8, 128), 1)
    for t in range(18):
        value = None
        for v in range(NV):
            shift = NV * v - 128 * t
            if shift <= -NV or shift >= 128:
                continue
            row = read(v)
            row = pltpu.roll(row, shift % 128, 1) if shift % 128 else row
            here = (lane >= shift) & (lane < shift + NV)
            value = jnp.where(here, row, 0.0 if value is None else value)
        write(t, value)


def flatten_kernel(order, blocks, above, out, high_y, turned):
    device = device_index()
    places = (0, 1, 3, 5, 6)
    for s in range(SUB_DEV):
        for kind in range(5):
            group = (SUB_DEV * kind + s) // 8
            turned[group, pl.ds((SUB_DEV * kind + s) % 8, NV, stride=8), :] = blocks[s, kind]
        packed_low = above[1 + s % 2]
        if s >= 2:
            packed_low = pltpu.roll(packed_low, 64, 1)
        packed_low = jnp.where(lax.broadcasted_iota(jnp.int32, (NV, 128), 1) < NV, packed_low, 0.0)
        here = device * SUB_DEV + s
        later = order[jnp.minimum(here + SUB_DEV, SUBS - 1)]
        upper = jnp.where(order[here] > later, packed_low, flipped(packed_low))
        high_y[s] = upper
        turned[2, pl.ds(SUB_DEV + s, NV, stride=8), :] = upper
    for group in range(3):
        low_place = places[2 * group]
        high_place = places[2 * group + 1] if group < 2 else 4

        def write(t, value):
            out[low_place, :, 128 * t : 128 * t + 128] = value[:4]
            out[high_place, :, 128 * t : 128 * t + 128] = value[4:]

        row_major(lambda v: turned[group, 8 * v : 8 * v + 8, :], write)


def flatten(order, blocks, above):
    smem = pl.BlockSpec(memory_space=pltpu.SMEM)
    vmem = pl.BlockSpec(memory_space=pltpu.VMEM)
    return pl.pallas_call(
        flatten_kernel,
        out_shape=(
            jax.ShapeDtypeStruct((7, SUB_DEV, NV * NV), jnp.float32),
            jax.ShapeDtypeStruct((SUB_DEV, NV, 128), jnp.float32),
        ),
        in_specs=[smem] + [vmem] * 2,
        out_specs=(vmem, vmem),
        scratch_shapes=[pltpu.VMEM((3, NV * 8, 128), jnp.float32)],
        cost_estimate=pl.CostEstimate(flops=1_000_000, bytes_accessed=2_000_000, transcendentals=0),
        name="flatten",
    )(order, blocks, above)


def eliminate(work, unit):
    groups = [work[8 * v : 8 * v + 8] for v in range(6)]
    sub = lax.broadcasted_iota(jnp.int32, (8, 128), 0)

    def row_of(value, k):
        return jnp.broadcast_to(value[k : k + 1, :], (8, 128))

    def column_of(value, k):
        return jnp.broadcast_to(value[:, k : k + 1], (8, 128))

    for g in range(6):
        head = groups[g]
        splat = [column_of(head, 64 + 8 * g + k) * unit for k in range(8)]
        below = [[column_of(groups[v], 64 + 8 * g + k) for k in range(8)] for v in range(g + 1, 6)]
        done = jnp.zeros((8, 128), jnp.float32)
        for k in range(0, 8, 2):
            x, y = splat[k], splat[k + 1]
            a, b, c = row_of(x, k), row_of(y, k), row_of(y, k + 1)
            inverse = 1.0 / (a * c - b * b)
            ratio = b / a
            top, low = row_of(head, k), row_of(head, k + 1)
            done = jnp.where(sub == k, top * lax.rsqrt(a), done)
            done = jnp.where(sub == k + 1, (low - ratio * top) * lax.rsqrt(c - ratio * b), done)

            def reduced(value, upper, lower):
                one = (c * upper - b * lower) * inverse
                two = (a * lower - b * upper) * inverse
                return jnp.where(sub == k, one, jnp.where(sub == k + 1, two, value - x * one - y * two))

            for m in range(k + 2, 8):
                splat[m] = reduced(splat[m], row_of(splat[m], k), row_of(splat[m], k + 1))
            head = reduced(head, top, low)
        rows = [row_of(head, k) for k in range(8)]
        for v in range(g + 1, 6):
            terms = [s * r for s, r in zip(below[v - g - 1], rows)]
            while len(terms) > 1:
                terms = [p + q for p, q in zip(terms[::2], terms[1::2])]
            groups[v] = groups[v] - terms[0]
        groups[g] = done
    return jnp.concatenate(groups, axis=0)


def halves(values):
    high = values.astype(jnp.bfloat16)
    low = (values - high.astype(jnp.float32)).astype(jnp.bfloat16)
    return high, low


def across(left, right):
    return lax.dot_general(left, right, (((1,), (1,)), ((), ())), preferred_element_type=jnp.float32)


ROWS = SUB_DEV * NV
BAND = 4


def factor_kernel(order, meta, own, right1, right2, right3, left1, left2, left3, below, above, rescue, blocks, high_y, flat_in, out, flat, grid, got, dense, lhs, rhs, binv, side, high_x, turned, slab, sems, side_sems):
    device = meta[0]
    lane = lax.broadcasted_iota(jnp.int32, (NV, 128), 1)

    def place(value, half, row, column, wanted):
        parity = column % 2
        moved = pltpu.roll(value, 64 * ((parity + half) % 2), 1)
        inside = (lane >= 64 * parity) & (lane < 64 * parity + NV)
        tile = jnp.where(wanted, column // 2, 7)
        at = pl.ds(pl.multiple_of(jnp.where(wanted, row, 0), 16), NV)
        pltpu.store(grid.at[tile, at, :], moved, mask=inside)

    def ordered(subdomain):
        return order[jnp.clip(subdomain, 0, SUBS - 1)]

    def neighbours(subdomain):
        column = (subdomain // SUB_DEV) % N_COL
        local = subdomain % SUB_DEV
        stride = N_COL * SUB_DEV
        return (
            (subdomain, subdomain >= 0),
            (subdomain - stride, subdomain >= stride),
            (subdomain + stride, (subdomain >= 0) & (subdomain < SUBS - stride)),
            (subdomain - SUB_DEV, (subdomain >= 0) & (column > 0)),
            (subdomain + SUB_DEV, (subdomain >= 0) & (column < N_COL - 1)),
            (subdomain - 1, (subdomain >= 0) & (local > 0)),
            (subdomain + 1, (subdomain >= 0) & (local < SUB_DEV - 1)),
        )

    relevant = jnp.int32(0)
    for l in range(SUB_DEV):
        for near, there in neighbours(device * SUB_DEV + l):
            relevant += (there & (ordered(near) < PB)).astype(jnp.int32)

    side_copy = pltpu.make_async_copy(above.at[pl.ds(12, 2)], side, side_sems.at[0])
    side_copy.start()

    @pl.when(relevant > 0)
    def _():
        near_sources = [right3, right2, right1, own, left1, left2, left3]
        for case in range(5):

            @pl.when(meta[1] == case)
            def _():
                for i in range(3):
                    pltpu.make_async_copy(near_sources[case + i], dense.at[i], sems.at[i]).start()

        for case, source in ((5, below), (6, above)):

            @pl.when(meta[1] == case)
            def _():
                for i in range(3):
                    pltpu.make_async_copy(source.at[pl.ds(4 * i, 4)], dense.at[i], sems.at[i]).start()

        @pl.when(meta[1] == 7)
        def _():
            for i in range(3):
                pltpu.make_async_copy(rescue.at[pl.ds(6 * i, 6)], got.at[i], sems.at[i]).start()

        pltpu.make_async_copy(rescue.at[pl.ds(18, 6)], got.at[3], sems.at[3]).start()

    side_copy.wait()
    for s in range(SUB_DEV):
        packed_low = side[s % 2]
        if s >= 2:
            packed_low = pltpu.roll(packed_low, 64, 1)
        upper = flipped(jnp.where(lane < NV, packed_low, 0.0))
        high_x[s] = upper
        turned[pl.ds(s, NV, stride=8), :] = upper

    def write(t, value):
        slab[:, 128 * t : 128 * t + 128] = value[:4]

    row_major(lambda v: turned[8 * v : 8 * v + 8, :], write)
    flat_copy = pltpu.make_async_copy(slab, flat.at[2], side_sems.at[1])
    flat_copy.start()

    @pl.when(relevant == 0)
    def _():
        out[...] = jnp.zeros_like(out)

    @pl.when(relevant > 0)
    def _():
        grid[:6, : ROWS + PB * NV + BAND * NV, :] = jnp.zeros((6, ROWS + PB * NV + BAND * NV, 128), jnp.float32)
        rhs[...] = jnp.zeros_like(rhs)
        lhs[...] = jnp.zeros_like(lhs)
        for l in range(SUB_DEV):
            for kind, (near, there) in enumerate(neighbours(device * SUB_DEV + l)):
                column = ordered(near)
                value = (blocks.at[l, 0], blocks.at[l, 1], high_x.at[l], blocks.at[l, 2], high_y.at[l], blocks.at[l, 3], blocks.at[l, 4])[kind][...]
                place(value, 0, NV * l, column, there & (column < PB))
        pltpu.make_async_copy(rescue.at[pl.ds(18, 6)], got.at[3], sems.at[3]).wait()

        @pl.when(meta[1] == 7)
        def _():
            for i in range(3):
                pltpu.make_async_copy(rescue.at[pl.ds(6 * i, 6)], got.at[i], sems.at[i]).wait()

        @pl.when(meta[1] < 7)
        def _():
            row = lax.broadcasted_iota(jnp.int32, (NV, 128), 0)
            left = lane < 64
            for i in range(3):
                pltpu.make_async_copy(own, dense.at[i], sems.at[i]).wait()
                pairs = dense[i, 0]
                whole = []
                for half in range(2):
                    slot = pltpu.roll(pairs, 64, 1) if half else pairs
                    last = jnp.broadcast_to(slot[:, NV : NV + 1], (NV, 128))
                    turned_slot = flipped(jnp.where(lane < NV, slot, 0.0))
                    whole.append(jnp.where(lane <= row, slot, turned_slot))
                    whole.append(jnp.where(lane == row, last, jnp.where(lane < row, turned_slot, slot)))
                got[i, 0] = jnp.where(left, whole[0], pltpu.roll(whole[2], 64, 1))
                got[i, 3] = jnp.where(left, whole[1], pltpu.roll(whole[3], 64, 1))
                got[i, 1] = dense[i, 1]
                got[i, 4] = dense[i, 2]
                z_pair = dense[i, 3]
                z_last = jnp.where(
                    lane < 80,
                    pltpu.roll(dense[i, 1], 16, 1),
                    jnp.where(lane < 96, pltpu.roll(dense[i, 1], 96, 1), pltpu.roll(dense[i, 2], 48, 1)),
                )
                got[i, 2] = z_pair
                got[i, 5] = jnp.where(left, z_pair, z_last)
        reach = jnp.int32(0)
        for slot in range(12):
            i, l = slot // SUB_DEV, slot % SUB_DEV
            s = meta[4 + slot]
            p = ordered(s)
            near = neighbours(s)
            for kind, (t, there) in enumerate((near[0], near[3], near[5], near[1])):
                q = ordered(t)
                wanted = there & (p < PB) & (q < PB)
                reach = jnp.maximum(reach, jnp.where(wanted, jnp.abs(p - q), 0))
                if kind < 3:
                    value, half = got[i, (l % 2) * 3 + kind], l // 2
                else:
                    value, half = got[3, slot % 6], slot // 6
                place(value, half, ROWS + NV * jnp.maximum(p, q), jnp.minimum(p, q), wanted)

        rows48 = lax.broadcasted_iota(jnp.int32, (NV, 128), 0)

        unit = jnp.full((8, 128), jnp.where(device >= 0, 1.0, 0.0), jnp.float32)

        gap = jnp.zeros((16, 128), jnp.bfloat16)

        def diagonal(k):
            at = pl.ds(pl.multiple_of(ROWS + k * NV, 16), NV)
            return pltpu.roll(grid[k // 2, at, :], 64 * (1 - k % 2), 1)

        def invert(k, diag):
            work = jnp.where(lane < 64, (lane == rows48).astype(jnp.float32), jnp.where(lane < 64 + NV, diag, 0.0))
            inverse = jnp.where(lane < NV, eliminate(work, unit), 0.0)
            high, low = halves(pltpu.roll(inverse, 64 * (k % 2), 1))
            high = jnp.concatenate([high, gap, high, gap], axis=0)
            low = jnp.concatenate([low, gap, low, gap], axis=0)
            binv[0] = high
            binv[1] = low
            return high, low

        def solve(values, high, low):
            c_high, c_low = halves(values)
            return across(jnp.concatenate([c_high, c_low], axis=1), jnp.concatenate([high, high], axis=1)) + across(c_high, low)

        def mix(high, low):
            left_half = lax.broadcasted_iota(jnp.int32, high.shape, 1) < 64
            return jnp.where(left_half, high.astype(jnp.float32), low.astype(jnp.float32)).astype(jnp.bfloat16)

        def urgent(k, high, low):
            at = pl.ds(pl.multiple_of(ROWS + (k + 1) * NV, 16), NV)
            s_high, s_low = halves(solve(grid[k // 2, at, :], high, low))
            mixed = mix(s_high, s_low)
            nothing = jnp.zeros_like(mixed)
            even = (k + 1) % 2 == 0
            other = jnp.concatenate([jnp.where(even, mixed, nothing), gap, jnp.where(even, nothing, mixed), gap], axis=0)
            grid[(k + 1) // 2, at, :] -= across(jnp.concatenate([s_high, s_low], axis=1), jnp.concatenate([other, other], axis=1))

        def finish(band, k, live):
            tile = k // 2
            depth = ROWS + band * NV
            window = pl.ds(pl.multiple_of(ROWS + k * NV, 16), NV + band * NV)
            later = pl.ds(pl.multiple_of(ROWS + (k + 1) * NV, 16), band * NV)
            at = pl.ds(pl.multiple_of(ROWS + k * NV, 16), NV)
            column = jnp.concatenate([grid[tile, :ROWS, :], grid[tile, window, :]], axis=0)
            solved = solve(column, binv[0], binv[1])
            corner = jnp.where((lane % 64) <= rows48, solved[ROWS : ROWS + NV], 0.0)
            parity = jnp.where(live, k % 2, 2)
            rest = jnp.concatenate([solved[:ROWS], solved[ROWS + NV :]], axis=0)
            chosen = lax.broadcasted_iota(jnp.int32, (depth, 128), 1) // 64 == parity
            kept = jnp.where(chosen, rest, jnp.concatenate([column[:ROWS], column[ROWS + NV :]], axis=0))
            grid[tile, :ROWS, :] = kept[:ROWS]
            grid[tile, later, :] = kept[ROWS:]
            grid[tile, at, :] = jnp.where(lane // 64 == parity, corner, column[ROWS : ROWS + NV])
            s_high, s_low = halves(rest)
            lhs[:depth, :128] = s_high
            lhs[:depth, 128:] = s_low
            mixed = mix(s_high[ROWS:], s_low[ROWS:])
            rhs[pl.ds(pl.multiple_of(64 * k, 64), 64), :] = jnp.zeros((64, 128), jnp.bfloat16)
            for w in range(band):
                rhs[pl.ds(pl.multiple_of(64 * (k + 1 + w), 64), NV), :] = mixed[NV * w : NV * w + NV]

        def trail(band, k, t, skip):
            depth = ROWS + band * NV
            later = pl.ds(pl.multiple_of(ROWS + (k + 1 + skip) * NV, 16), (band - skip) * NV)
            other = rhs[pl.ds(pl.multiple_of(128 * t, 128), 128), :]
            other = jnp.concatenate([other, other], axis=1)
            grid[t, :ROWS, :] -= across(lhs[:ROWS, :], other)
            grid[t, later, :] -= across(lhs[ROWS + skip * NV : depth, :], other)

        @pl.when(reach <= BAND)
        def _():
            binv[...] = jnp.zeros_like(binv)

            def body(k, carry):
                diag = diagonal(k)
                last = jnp.maximum(k - 1, 0)
                finish(BAND, last, k > 0)
                for j in range(3):
                    trail(BAND, last, k // 2 + j, 1 if j == 0 else 0)
                high, low = invert(k, diag)
                urgent(k, high, low)
                return carry

            lax.fori_loop(0, PB, body, 0)
            finish(BAND, PB - 1, True)

        @pl.when(reach > BAND)
        def _():
            start = ROWS + PB * NV + BAND * NV
            grid[:6, start:, :] = jnp.zeros((6, grid.shape[1] - start, 128), jnp.float32)

            def body(k, carry):
                invert(k, diagonal(k))
                finish(PB - 1, k, True)

                def inner(t, c):
                    trail(PB - 1, k, t, 0)
                    return c

                lax.fori_loop((k + 1) // 2, 6, inner, 0)
                return carry

            lax.fori_loop(0, PB, body, 0)

        for l in range(SUB_DEV):
            p = ordered(device * SUB_DEV + l)
            inside = p < PB
            start = jnp.where(inside, ROWS + NV * p, NV * l)
            at = pl.ds(pl.multiple_of(start, 16), NV)
            pieces = []
            for j in range(PB):
                piece = grid[j // 2, at, :][:, 64 * (j % 2) : 64 * (j % 2) + NV]
                pieces.append(jnp.where(inside & (j > p), 0.0, piece))
            out[l] = jnp.concatenate(pieces, axis=1)

    flat_copy.wait()


def factor(order, meta, shares, below, above, rescue, blocks, high_y, flat):
    smem = pl.BlockSpec(memory_space=pltpu.SMEM)
    hbm = pl.BlockSpec(memory_space=pl.ANY)
    vmem = pl.BlockSpec(memory_space=pltpu.VMEM)
    return pl.pallas_call(
        factor_kernel,
        out_shape=(
            jax.ShapeDtypeStruct((SUB_DEV, NV, PB * NV), jnp.float32),
            jax.ShapeDtypeStruct(flat.shape, jnp.float32),
        ),
        in_specs=[smem] * 2 + [hbm] * 10 + [vmem] * 2 + [hbm],
        out_specs=(vmem, hbm),
        input_output_aliases={14: 1},
        scratch_shapes=[
            pltpu.VMEM((8, ROWS + PB * NV + PB * NV, 128), jnp.float32),
            pltpu.VMEM((4, 6, NV, 128), jnp.float32),
            pltpu.VMEM((3, 4, NV, 128), jnp.float32),
            pltpu.VMEM((ROWS + (PB - 1) * NV, 256), jnp.bfloat16),
            pltpu.VMEM(((2 * PB + 2) * 64, 128), jnp.bfloat16),
            pltpu.VMEM((2, 128, 128), jnp.bfloat16),
            pltpu.VMEM((2, NV, 128), jnp.float32),
            pltpu.VMEM((SUB_DEV, NV, 128), jnp.float32),
            pltpu.VMEM((NV * 8, 128), jnp.float32),
            pltpu.VMEM((SUB_DEV, NV * NV), jnp.float32),
            pltpu.SemaphoreType.DMA((4,)),
            pltpu.SemaphoreType.DMA((2,)),
        ],
        name="factor",
    )(order, meta, *shares, below, above, rescue, blocks, high_y, flat)


def shifted(value, amount):
    size = N_ROW * N_COL
    return lax.ppermute(value, ("row", "col"), [(i, (i + amount) % size) for i in range(size)])


def packed(blocks):
    wide = jnp.pad(blocks, ((0, 0), (0, 0), (0, 64 - NV)))
    return jnp.concatenate([wide[:6], wide[6:]], axis=2)


def everywhere(value):
    size = N_ROW * N_COL
    step = 1
    while step < size:
        value = value + lax.ppermute(value, ("row", "col"), [(i, i ^ step) for i in range(size)])
        step *= 2
    return value


def choose_kernel(spot, right2, right1, share, left1, left2, side, out):
    out[12:14] = side[...]
    for case, sources in enumerate(((share, left1, left2), (right1, share, left1), (right2, right1, share))):

        @pl.when(spot[0] == case)
        def _():
            for i, source in enumerate(sources):
                out[4 * i : 4 * i + 4] = source[...]


def choose(spot, right2, right1, share, left1, left2, side):
    vmem = pl.BlockSpec(memory_space=pltpu.VMEM)
    return pl.pallas_call(
        choose_kernel,
        out_shape=jax.ShapeDtypeStruct((14, NV, 128), jnp.float32),
        in_specs=[pl.BlockSpec(memory_space=pltpu.SMEM)] + [vmem] * 6,
        out_specs=vmem,
        name="choose",
    )(spot, right2, right1, share, left1, left2, side)


def exchange(device, order, blocks, share, side):
    subdomain = jnp.arange(SUBS, dtype=jnp.int32)
    first = jnp.sum(jnp.where(order == 0, subdomain // SUB_DEV, 0))
    size = N_ROW * N_COL
    distance = (subdomain // SUB_DEV - first + size // 2) % size - size // 2
    inside = order < PB
    least = jnp.min(jnp.where(inside, distance, size))
    most = jnp.max(jnp.where(inside, distance, -size))
    near = (most - least) <= 2
    base = (first + least) % size
    mine = device * SUB_DEV + jnp.arange(SUB_DEV, dtype=jnp.int32)
    my_order = lax.dynamic_slice(order, (device * SUB_DEV,), (SUB_DEV,))

    right1 = shifted(share, 1)
    left1 = shifted(share, -1)
    right2 = shifted(share, 2)
    left2 = shifted(share, -2)
    offset = (base - device + size // 2) % size - size // 2
    spot = jnp.where(offset == 0, 0, jnp.where(offset == -1, 1, 2)).astype(jnp.int32).reshape(1)
    payload = choose(spot, right2, right1, share, left1, left2, side)
    below = shifted(payload, N_COL)
    above = shifted(payload, -N_COL)
    flat, high_y = flatten(order, blocks, left1)
    right3 = shifted(right2, 1)
    left3 = shifted(left2, -1)
    from_below = (offset + N_COL + 2) % size <= 2
    from_above = (offset - N_COL + 2) % size <= 2
    beside = (offset >= -3) & (offset <= 1)
    pick = jnp.where(beside, offset + 3, jnp.where(from_below, 5, jnp.where(from_above, 6, 0)))
    pick = jnp.where(near, pick, 7)

    def local_path(_):
        listed = (base * SUB_DEV + jnp.arange(12, dtype=jnp.int32)) % SUBS
        return (jnp.zeros((24, NV, 128), jnp.float32), listed)

    def global_path(_):
        slots = jnp.arange(12, dtype=jnp.int32)
        hit = (order[None, :] == slots[:, None]) & (slots[:, None] < PB)
        listed = jnp.where(slots < PB, jnp.sum(jnp.where(hit, subdomain[None, :], 0), axis=1), -1)
        mask = ((my_order[None, :] == slots[:, None]) & (slots[:, None] < PB)).astype(jnp.float32)
        def oriented(block, offset):
            other = lax.dynamic_slice(jnp.concatenate([order[:128], order]), (128 + device * SUB_DEV - offset,), (SUB_DEV,))
            return jnp.where((my_order > other)[:, None, None], block, jnp.swapaxes(block, 1, 2))

        kinds = jnp.stack(
            [
                blocks[:, 0, :, :NV],
                oriented(blocks[:, 2, :, :NV], SUB_DEV),
                oriented(blocks[:, 3, :, :NV], 1),
                oriented(blocks[:, 1, :, :NV], N_COL * SUB_DEV),
            ],
            axis=1,
        )
        placed = jnp.einsum("ps,skvw->pkvw", mask, kinds, precision=lax.Precision.HIGHEST)
        whole = everywhere(
            jnp.stack([packed(placed[4 * i : 4 * i + 4, :3].reshape(12, NV, NV)) for i in range(3)] + [packed(placed[:, 3])])
        )
        return (whole.reshape(24, NV, 128), listed)

    rescue, listed = lax.cond(near, local_path, global_path, None)
    meta = jnp.concatenate([jnp.stack([device, pick, jnp.int32(0), jnp.int32(0)]), listed]).astype(jnp.int32)
    shares = (share, right1, right2, right3, left1, left2, left3)
    panel, flat = factor(order, meta, shares, below, above, rescue, blocks, high_y, flat)
    return (jnp.transpose(flat, (1, 0, 2)), panel)


def from_next(value, axis, amount):
    size = lax.axis_size(axis)
    pairs = [(i, i + amount) for i in range(size) if 0 <= i + amount < size]
    return lax.ppermute(value, axis, pairs)


def shards(deflation, coefficient, gradients, x_penalty, y_penalty, z_penalty, coarse_order):
    device = device_index()
    below_x = from_next(deflation[1, :, :, 48 * NV :], "row", 1)
    below_y = from_next(deflation[:, 7], "col", 1)
    main, own_x, own_y, roots_x, roots_y = assemble(
        deflation, gradients.reshape(192, 64), coefficient, x_penalty, jnp.transpose(y_penalty, (1, 0, 2)), z_penalty
    )
    blocks, share, side = lateral(coarse_order, below_x, below_y, main, own_x, own_y, roots_x, roots_y)
    return exchange(device, coarse_order, blocks, share, side)


def solution(mesh):
    in_specs = (
        P("row", "col", None, None),
        P("row", "col", None),
        P(),
        P("row", "col", None),
        P("row", "col", None),
        P("row", "col", None),
        P(),
    )
    out_specs = (P(("row", "col"), None, None), P(("row", "col"), None, None))
    return jax.shard_map(shards, mesh=mesh, in_specs=in_specs, out_specs=out_specs, check_vma=False)
```

```python
import jax
import jax.numpy as jnp
from jax import lax
from jax.experimental import pallas as pl
from jax.experimental.pallas import tpu as pltpu
from jax.sharding import PartitionSpec as P

NV = 48
SUB_DEV = 4
PB = 11
SUBS = 1024
N_ROW = 8
N_COL = 32


LINE_WEIGHTS = (1.0 / 6.0, 5.0 / 6.0, 5.0 / 6.0, 1.0 / 6.0)
COEF, XPEN, YPEN, ZPEN = 0, 16, 40, 58


def fetch(tiles, start, target):
    lane = lax.broadcasted_iota(jnp.int32, tiles[0].shape, 1)
    tile, offset = start // 128, start % 128
    shift = (target - offset) % 128
    first = pltpu.roll(tiles[tile], shift, 1) if shift else tiles[tile]
    if offset + NV <= 128:
        return first
    second = pltpu.roll(tiles[tile + 1], shift, 1) if shift else tiles[tile + 1]
    return jnp.where(lane >= target + 128 - offset, second, first)


def paired(even, odd, start):
    lane = lax.broadcasted_iota(jnp.int32, even[0].shape, 1)
    return jnp.where(lane < 64, fetch(even, start, 0), fetch(odd, start, 64))


def lane_tiles(values):
    wide = values.astype(jnp.float32)
    return [wide[:, 128 * t : 128 * t + 128] for t in range(wide.shape[1] // 128)]


def gram(left, right):
    return lax.dot_general(left, right, (((0,), (0,)), ((), ())), preferred_element_type=jnp.float32)


def assemble_kernel(deflation, gradients, coefficient, x_penalty, y_penalty, z_penalty, main, own_x, own_y, roots_x, roots_y, nodes, sides, stack, second, total, roots, low_z, other_z, table):
    table[...] = jnp.zeros_like(table)
    for x in range(2):
        table[COEF + 8 * x : COEF + 8 * x + 8, :16] = coefficient[x]
        table[ZPEN + 8 * x : ZPEN + 8 * x + 8, :17] = z_penalty[x]
    for g in range(3):
        table[XPEN + 8 * g : XPEN + 8 * g + 8, :16] = x_penalty[g]
    for g in range(9):
        table[YPEN + 2 * g : YPEN + 2 * g + 2, :16] = y_penalty[g]
    rooted = jnp.sqrt(jnp.transpose(table[...]))[:24]
    half = lax.broadcasted_iota(jnp.int32, (24, 128), 1) < 64

    def spread(even, odd):
        left = jnp.broadcast_to(rooted[:, even : even + 1], (24, 128))
        right = jnp.broadcast_to(rooted[:, odd : odd + 1], (24, 128))
        return jnp.where(half, left, right)

    for i in range(4):
        for x in range(2):
            roots[0, i, x] = spread(COEF + 8 * x + 2 * i, COEF + 8 * x + 2 * i + 1)
            roots[1, i, x] = spread(XPEN + 16 * x + 2 * i, XPEN + 16 * x + 2 * i + 1)
            roots[2, i, x] = spread(XPEN + 8 + 2 * i, XPEN + 8 + 2 * i + 1)
            roots[3, i, x] = spread(YPEN + 2 * (2 * i + 1) + x, YPEN + 2 * (2 * i + 2) + x)
            roots[4, i, x] = spread(ZPEN + 8 * x + 2 * i, ZPEN + 8 * x + 2 * i + 1)
            roots[5, i, x] = jnp.where(half & (i == 0), jnp.broadcast_to(rooted[:, YPEN + x : YPEN + x + 1], (24, 128)), 0.0)
        roots_x[i] = roots[1, i, 0, :16]
    roots_y[...] = spread(YPEN, YPEN + 1)[:16]

    def relay(i, carry):
        for x in range(2):
            even = lane_tiles(deflation[x, 2 * i])
            odd = lane_tiles(deflation[x, 2 * i + 1])
            for n in range(64):
                a, b, c = n // 16, n // 4 % 4, n % 4
                both = paired(even, odd, NV * n)
                nodes[i, x, pl.ds(n, 16, stride=65), :] = both
                if b % 3 == 0:
                    sides[i, x, b // 3, pl.ds(4 * a + c, 16, stride=17), :] = both
        return carry

    lax.fori_loop(0, 4, relay, 0)
    total[...] = jnp.zeros_like(total)
    node = lax.broadcasted_iota(jnp.int32, (64, 128), 0)

    def edge(position):
        return jnp.where((position == 0) | (position == 3), LINE_WEIGHTS[0], LINE_WEIGHTS[1])

    weight = jnp.sqrt(edge(node // 16) * edge(node // 4 % 4) * edge(node % 4))
    first_half = lax.broadcasted_iota(jnp.int32, (16, 128), 1) < 64

    def fill(step, stack):
        s, i = step // 4, step % 4
        low = jnp.bfloat16

        def root(kind, x, z, rows):
            return jnp.broadcast_to(roots[kind, i, x, pl.ds(z, 1), :], (rows, 128))

        inner = []
        for zz in range(4):
            z = 4 * s + zz
            at = pl.ds(65 * z, 64)
            block = [nodes[i, x, at, :] for x in range(2)]
            z_rows = jnp.concatenate(block, axis=1).astype(low)
            product = jnp.dot(gradients[...], z_rows, preferred_element_type=jnp.float32)
            factor_z = jnp.concatenate([weight * root(0, x, z, 64) for x in range(2)], axis=1)
            for d in range(3):
                stack[192 * zz + 64 * d : 192 * zz + 64 * d + 64, :] = (product[64 * d : 64 * d + 64] * factor_z).astype(low)
            near = (block[0][:16] * root(1, 0, z, 16)).astype(low)
            far = (block[1][48:] * root(1, 1, z, 16)).astype(low)
            stack[768 + 16 * zz : 784 + 16 * zz, :] = jnp.concatenate([near, far], axis=1)
            here = pl.ds(17 * z, 16)
            there = pl.ds(pl.multiple_of(16 * z, 16), 16)
            own_x[i, there, :] = near
            inner.append((root(2, 0, z, 16) * (block[0][48:] - block[1][:16])).astype(low))
            lows, jumps = [], []
            after = jnp.minimum(i + 1, 3)
            for x in range(2):
                lower = sides[i, x, 0, here, :]
                swapped = pltpu.roll(lower, 64, 1)
                later = jnp.where(i < 3, pltpu.roll(sides[after, x, 0, here, :], 64, 1), 0.0)
                jumps.append((root(3, x, z, 16) * (sides[i, x, 1, here, :] - jnp.where(first_half, swapped, later))).astype(low))
                lows.append((root(5, x, z, 16) * lower).astype(low))
            stack[864 + 16 * zz : 880 + 16 * zz, :] = jnp.concatenate(jumps, axis=1)
            stack[928 + 16 * zz : 944 + 16 * zz, :] = jnp.concatenate(lows, axis=1)
            ups, firsts, befores = [], [], []
            for x in range(2):
                upper = nodes[i, x, pl.ds(65 * z + 3, 16, stride=4), :]
                if zz < 3:
                    upper = upper - nodes[i, x, pl.ds(65 * z + 65, 16, stride=4), :]
                ups.append((root(4, x, z + 1, 16) * upper).astype(low))
                if zz == 0:
                    firsts.append((root(4, x, z, 16) * nodes[i, x, pl.ds(65 * z, 16, stride=4), :]).astype(low))
                    before = nodes[i, x, pl.ds(65 * jnp.maximum(z - 1, 0) + 3, 16, stride=4), :]
                    befores.append(jnp.where(s > 0, root(4, x, z, 16) * before, 0.0).astype(low))
            stack[992 + 16 * zz : 1008 + 16 * zz, :] = jnp.concatenate(ups, axis=1)
            if zz == 0:
                stack[1056:1072, :] = jnp.concatenate(firsts, axis=1)
                row = pl.ds(pl.multiple_of(16 * i, 16), 16)
                low_z[s, row, :] = jnp.concatenate(firsts, axis=1)
                other_z[s, row, :] = jnp.concatenate(befores, axis=1)
        stack[832:848, :] = jnp.concatenate(inner[:2], axis=1)
        stack[848:864, :] = jnp.concatenate(inner[2:], axis=1)

    def add(step, stack):
        total[step // 4] += gram(stack[...], stack[...])

    second[...] = jnp.zeros_like(second)

    def pair(step, carry):
        add(jnp.maximum(2 * step - 1, 0), second)
        fill(2 * step, stack)
        add(2 * step, stack)
        fill(2 * step + 1, second)
        return carry

    lax.fori_loop(0, 8, pair, 0)
    add(15, second)

    def folded(square):
        return (
            square[:NV, :128]
            + pltpu.roll(square[64 : 64 + NV, :128], 64, 1)
            + square[128 : 128 + NV, 128:]
            + pltpu.roll(square[192 : 192 + NV, 128:], 64, 1)
        )

    for s in range(4):
        main[s, 0] = folded(total[s])
        below = -folded(gram(low_z[s], other_z[s]))
        main[s, 1] = below
        if s:
            main[s - 1, 2] = jnp.transpose(jnp.concatenate([below, jnp.zeros((80, 128), jnp.float32)], axis=0))[:NV]
    main[3, 2] = jnp.zeros((NV, 128), jnp.float32)
    for z in range(16):
        here = slice(16 * z, 16 * z + 16)
        there = slice(17 * z, 17 * z + 16)
        lower = [sides[0, x, 0, there, :] for x in range(2)]
        near = jnp.where(first_half, lower[0], pltpu.roll(lower[1], 64, 1))
        own_y[here, :] = (near * jnp.broadcast_to(roots_y[z : z + 1, :], (16, 128))).astype(jnp.bfloat16)


def assemble(deflation, gradients, coefficient, x_penalty, y_penalty, z_penalty):
    vmem = pl.BlockSpec(memory_space=pltpu.VMEM)
    f32, low = jnp.float32, jnp.bfloat16
    return pl.pallas_call(
        assemble_kernel,
        out_shape=(
            jax.ShapeDtypeStruct((4, 3, NV, 128), f32),
            jax.ShapeDtypeStruct((4, 256, 128), low),
            jax.ShapeDtypeStruct((256, 128), low),
            jax.ShapeDtypeStruct((4, 16, 128), f32),
            jax.ShapeDtypeStruct((16, 128), f32),
        ),
        in_specs=[vmem] * 6,
        out_specs=(vmem,) * 5,
        scratch_shapes=[
            pltpu.VMEM((4, 2, 1040, 128), f32),
            pltpu.VMEM((4, 2, 2, 272, 128), f32),
            pltpu.VMEM((1072, 256), low),
            pltpu.VMEM((1072, 256), low),
            pltpu.VMEM((4, 256, 256), f32),
            pltpu.VMEM((6, 4, 2, 24, 128), f32),
            pltpu.VMEM((4, 64, 256), low),
            pltpu.VMEM((4, 64, 256), low),
            pltpu.VMEM((128, 128), f32),
        ],
        cost_estimate=pl.CostEstimate(flops=2_000_000_000, bytes_accessed=3_000_000, transcendentals=0),
        name="assemble",
    )(deflation, gradients, coefficient, x_penalty, y_penalty, z_penalty)


def device_index():
    return (lax.axis_index("row") * N_COL + lax.axis_index("col")).astype(jnp.int32)


def flipped(block):
    return jnp.transpose(jnp.concatenate([block, jnp.zeros((80, 128), jnp.float32)], axis=0))[:NV]


def lateral_kernel(order, ranks, below_x, below_y, main, own_x, own_y, roots_x, roots_y, blocks, share, side, plan, halo_x, halo_y):
    device = device_index()
    size = N_ROW * N_COL
    rank_all = ranks[...]
    holder = (lax.broadcasted_iota(jnp.int32, (8, 128), 0) * 128 + lax.broadcasted_iota(jnp.int32, (8, 128), 1)) // SUB_DEV
    first = jnp.sum(jnp.where(rank_all == 0, holder.astype(jnp.float32), 0.0)).astype(jnp.int32)
    distance = (((holder - first + size // 2) & (size - 1)) - size // 2).astype(jnp.float32)
    least = jnp.min(jnp.where(rank_all < PB, distance, float(size))).astype(jnp.int32)
    most = jnp.max(jnp.where(rank_all < PB, distance, float(-size))).astype(jnp.int32)
    base = (first + least) & (size - 1)
    offset = ((base - device + size // 2) & (size - 1)) - size // 2
    near = (most - least) <= 2
    from_below = ((offset + N_COL + 2) & (size - 1)) <= 2
    from_above = ((offset - N_COL + 2) & (size - 1)) <= 2
    beside = (offset >= -3) & (offset <= 1)
    plan[0] = device
    plan[1] = jnp.where(near, jnp.where(beside, offset + 3, jnp.where(from_below, 5, jnp.where(from_above, 6, 0))), 7)
    plan[2] = near.astype(jnp.int32)
    plan[3] = jnp.where(offset == 0, 0, jnp.where(offset == -1, 1, 2))
    for slot in range(12):
        plan[4 + slot] = (base * SUB_DEV + slot) & (SUBS - 1)
    low = jnp.bfloat16
    inside = lax.broadcasted_iota(jnp.int32, (NV, 128), 1) < NV

    def relay(i, carry):
        even = lane_tiles(below_x[2 * i])
        odd = lane_tiles(below_x[2 * i + 1])
        for m in range(16):
            halo_x[i, pl.ds(m, 16, stride=17), :] = paired(even, odd, NV * m) * roots_x[i]
        return carry

    lax.fori_loop(0, 4, relay, 0)
    even = lane_tiles(below_y[0])
    odd = lane_tiles(below_y[1])
    for m in range(16):
        n = 16 * (m // 4) + 12 + m % 4
        halo_y[pl.ds(m, 16, stride=17), :] = paired(even, odd, NV * n) * roots_y[...]

    def folded(square):
        return jnp.where(inside, -(square[:NV] + pltpu.roll(square[64 : 64 + NV], 64, 1)), 0.0)

    diags, low_ys, low_zs = [], [], []
    for s in range(SUB_DEV):
        at = slice(64 * s, 64 * s + 64)
        diag = jnp.where(inside, main[s, 0], 0.0)
        low_z = jnp.where(inside, main[s, 1], 0.0)
        mine = jnp.concatenate([own_x[i, at, :] for i in range(4)], axis=0)
        theirs = [halo_x[i, 17 * z : 17 * z + 16, :].astype(low) for i in range(4) for z in range(4 * s, 4 * s + 4)]
        low_x = folded(gram(mine, jnp.concatenate(theirs, axis=0)))
        theirs = [halo_y[17 * z : 17 * z + 16, :].astype(low) for z in range(4 * s, 4 * s + 4)]
        low_y = folded(gram(own_y[at, :], jnp.concatenate(theirs, axis=0)))
        blocks[s, 0] = diag
        blocks[s, 1] = low_x
        blocks[s, 2] = low_y
        blocks[s, 3] = low_z
        blocks[s, 4] = jnp.where(inside, main[s, 2], 0.0)
        here = device * SUB_DEV + s
        rank = order[here]
        turned_y = jnp.where(rank > order[jnp.maximum(here - SUB_DEV, 0)], low_y, flipped(low_y))
        turned_z = jnp.where(rank > order[jnp.maximum(here - 1, 0)], low_z, flipped(low_z))
        diags.append(diag)
        low_ys.append(turned_y)
        low_zs.append(turned_z)
        if s < 2:
            side[s] = low_x
        else:
            side[s - 2] += pltpu.roll(low_x, 64, 1)
    lane = lax.broadcasted_iota(jnp.int32, (NV, 128), 1)
    row = lax.broadcasted_iota(jnp.int32, (NV, 128), 0)

    def both(lower, upper):
        last = jnp.sum(jnp.where(lane == row, upper, 0.0), axis=1, keepdims=True)
        return jnp.where(lane <= row, lower, upper) + jnp.where(lane == NV, jnp.broadcast_to(last, (NV, 128)), 0.0)

    def piece(start, target):
        moved = pltpu.roll(low_zs[3], (target - start) % 128, 1)
        return jnp.where((lane >= target) & (lane < target + 16), moved, 0.0)

    share[0] = both(diags[0], diags[1]) + pltpu.roll(both(diags[2], diags[3]), 64, 1)
    share[1] = low_ys[0] + pltpu.roll(low_ys[2], 64, 1) + piece(0, 48) + piece(16, 112)
    share[2] = low_ys[1] + pltpu.roll(low_ys[3], 64, 1) + piece(32, 48)
    share[3] = low_zs[1] + pltpu.roll(low_zs[2], 64, 1)


def lateral(order, ranks, below_x, below_y, main, own_x, own_y, roots_x, roots_y):
    smem = pl.BlockSpec(memory_space=pltpu.SMEM)
    vmem = pl.BlockSpec(memory_space=pltpu.VMEM)
    f32 = jnp.float32
    return pl.pallas_call(
        lateral_kernel,
        out_shape=(
            jax.ShapeDtypeStruct((SUB_DEV, 5, NV, 128), f32),
            jax.ShapeDtypeStruct((4, NV, 128), f32),
            jax.ShapeDtypeStruct((2, NV, 128), f32),
            jax.ShapeDtypeStruct((16,), jnp.int32),
        ),
        in_specs=[smem] + [vmem] * 8,
        out_specs=(vmem, vmem, vmem, smem),
        scratch_shapes=[
            pltpu.VMEM((4, 272, 128), f32),
            pltpu.VMEM((272, 128), f32),
        ],
        name="lateral",
    )(order, ranks, below_x, below_y, main, own_x, own_y, roots_x, roots_y)


def row_major(read, write):
    lane = lax.broadcasted_iota(jnp.int32, (8, 128), 1)
    for t in range(18):
        value = None
        for v in range(NV):
            shift = NV * v - 128 * t
            if shift <= -NV or shift >= 128:
                continue
            row = read(v)
            row = pltpu.roll(row, shift % 128, 1) if shift % 128 else row
            here = (lane >= shift) & (lane < shift + NV)
            value = jnp.where(here, row, 0.0 if value is None else value)
        write(t, value)


def flatten_kernel(order, blocks, above, out, high_y, turned):
    device = device_index()
    places = (0, 1, 3, 5, 6)
    for s in range(SUB_DEV):
        for kind in range(5):
            group = (SUB_DEV * kind + s) // 8
            turned[group, pl.ds((SUB_DEV * kind + s) % 8, NV, stride=8), :] = blocks[s, kind]
        packed_low = above[1 + s % 2]
        if s >= 2:
            packed_low = pltpu.roll(packed_low, 64, 1)
        packed_low = jnp.where(lax.broadcasted_iota(jnp.int32, (NV, 128), 1) < NV, packed_low, 0.0)
        here = device * SUB_DEV + s
        later = order[jnp.minimum(here + SUB_DEV, SUBS - 1)]
        upper = jnp.where(order[here] > later, packed_low, flipped(packed_low))
        high_y[s] = upper
        turned[2, pl.ds(SUB_DEV + s, NV, stride=8), :] = upper
    for group in range(3):
        low_place = places[2 * group]
        high_place = places[2 * group + 1] if group < 2 else 4

        def write(t, value):
            out[low_place, :, 128 * t : 128 * t + 128] = value[:4]
            out[high_place, :, 128 * t : 128 * t + 128] = value[4:]

        row_major(lambda v: turned[group, 8 * v : 8 * v + 8, :], write)


def flatten(order, blocks, above):
    smem = pl.BlockSpec(memory_space=pltpu.SMEM)
    vmem = pl.BlockSpec(memory_space=pltpu.VMEM)
    return pl.pallas_call(
        flatten_kernel,
        out_shape=(
            jax.ShapeDtypeStruct((7, SUB_DEV, NV * NV), jnp.float32),
            jax.ShapeDtypeStruct((SUB_DEV, NV, 128), jnp.float32),
        ),
        in_specs=[smem] + [vmem] * 2,
        out_specs=(vmem, vmem),
        scratch_shapes=[pltpu.VMEM((3, NV * 8, 128), jnp.float32)],
        cost_estimate=pl.CostEstimate(flops=1_000_000, bytes_accessed=2_000_000, transcendentals=0),
        name="flatten",
    )(order, blocks, above)


def eliminate(work, unit):
    groups = [work[8 * v : 8 * v + 8] for v in range(6)]
    sub = lax.broadcasted_iota(jnp.int32, (8, 128), 0)

    def row_of(value, k):
        return jnp.broadcast_to(value[k : k + 1, :], (8, 128))

    def column_of(value, k):
        return jnp.broadcast_to(value[:, k : k + 1], (8, 128))

    for g in range(6):
        head = groups[g]
        splat = [column_of(head, 64 + 8 * g + k) * unit for k in range(8)]
        below = [[column_of(groups[v], 64 + 8 * g + k) for k in range(8)] for v in range(g + 1, 6)]
        done = jnp.zeros((8, 128), jnp.float32)
        for k in range(0, 8, 2):
            x, y = splat[k], splat[k + 1]
            a, b, c = row_of(x, k), row_of(y, k), row_of(y, k + 1)
            inverse = 1.0 / (a * c - b * b)
            ratio = b / a
            top, low = row_of(head, k), row_of(head, k + 1)
            done = jnp.where(sub == k, top * lax.rsqrt(a), done)
            done = jnp.where(sub == k + 1, (low - ratio * top) * lax.rsqrt(c - ratio * b), done)

            def reduced(value, upper, lower):
                one = (c * upper - b * lower) * inverse
                two = (a * lower - b * upper) * inverse
                return jnp.where(sub == k, one, jnp.where(sub == k + 1, two, value - x * one - y * two))

            for m in range(k + 2, 8):
                splat[m] = reduced(splat[m], row_of(splat[m], k), row_of(splat[m], k + 1))
            head = reduced(head, top, low)
        rows = [row_of(head, k) for k in range(8)]
        for v in range(g + 1, 6):
            terms = [s * r for s, r in zip(below[v - g - 1], rows)]
            while len(terms) > 1:
                terms = [p + q for p, q in zip(terms[::2], terms[1::2])]
            groups[v] = groups[v] - terms[0]
        groups[g] = done
    return jnp.concatenate(groups, axis=0)


def halves(values):
    high = values.astype(jnp.bfloat16)
    low = (values - high.astype(jnp.float32)).astype(jnp.bfloat16)
    return high, low


def across(left, right):
    return lax.dot_general(left, right, (((1,), (1,)), ((), ())), preferred_element_type=jnp.float32)


ROWS = SUB_DEV * NV
BAND = 4


def factor_kernel(order, meta, own, right1, right2, right3, left1, left2, left3, below, above, rescue, blocks, high_y, flat_in, out, flat, grid, got, dense, lhs, rhs, binv, side, high_x, turned, slab, sems, side_sems):
    device = meta[0]
    lane = lax.broadcasted_iota(jnp.int32, (NV, 128), 1)

    def place(value, half, row, column, wanted):
        parity = column % 2
        moved = pltpu.roll(value, 64 * ((parity + half) % 2), 1)
        inside = (lane >= 64 * parity) & (lane < 64 * parity + NV)
        tile = jnp.where(wanted, column // 2, 7)
        at = pl.ds(pl.multiple_of(jnp.where(wanted, row, 0), 16), NV)
        pltpu.store(grid.at[tile, at, :], moved, mask=inside)

    def ordered(subdomain):
        return order[jnp.clip(subdomain, 0, SUBS - 1)]

    def neighbours(subdomain):
        column = (subdomain // SUB_DEV) % N_COL
        local = subdomain % SUB_DEV
        stride = N_COL * SUB_DEV
        return (
            (subdomain, subdomain >= 0),
            (subdomain - stride, subdomain >= stride),
            (subdomain + stride, (subdomain >= 0) & (subdomain < SUBS - stride)),
            (subdomain - SUB_DEV, (subdomain >= 0) & (column > 0)),
            (subdomain + SUB_DEV, (subdomain >= 0) & (column < N_COL - 1)),
            (subdomain - 1, (subdomain >= 0) & (local > 0)),
            (subdomain + 1, (subdomain >= 0) & (local < SUB_DEV - 1)),
        )

    relevant = jnp.int32(0)
    for l in range(SUB_DEV):
        for near, there in neighbours(device * SUB_DEV + l):
            relevant += (there & (ordered(near) < PB)).astype(jnp.int32)

    side_copy = pltpu.make_async_copy(above.at[pl.ds(12, 2)], side, side_sems.at[0])
    side_copy.start()

    @pl.when(relevant > 0)
    def _():
        near_sources = [right3, right2, right1, own, left1, left2, left3]
        for case in range(5):

            @pl.when(meta[1] == case)
            def _():
                for i in range(3):
                    pltpu.make_async_copy(near_sources[case + i], dense.at[i], sems.at[i]).start()

        for case, source in ((5, below), (6, above)):

            @pl.when(meta[1] == case)
            def _():
                for i in range(3):
                    pltpu.make_async_copy(source.at[pl.ds(4 * i, 4)], dense.at[i], sems.at[i]).start()

        @pl.when(meta[1] == 7)
        def _():
            for i in range(3):
                pltpu.make_async_copy(rescue.at[pl.ds(6 * i, 6)], got.at[i], sems.at[i]).start()

        pltpu.make_async_copy(rescue.at[pl.ds(18, 6)], got.at[3], sems.at[3]).start()

    side_copy.wait()
    for s in range(SUB_DEV):
        packed_low = side[s % 2]
        if s >= 2:
            packed_low = pltpu.roll(packed_low, 64, 1)
        upper = flipped(jnp.where(lane < NV, packed_low, 0.0))
        high_x[s] = upper
        turned[pl.ds(s, NV, stride=8), :] = upper

    def write(t, value):
        slab[:, 128 * t : 128 * t + 128] = value[:4]

    row_major(lambda v: turned[8 * v : 8 * v + 8, :], write)
    flat_copy = pltpu.make_async_copy(slab, flat.at[2], side_sems.at[1])
    flat_copy.start()

    @pl.when(relevant == 0)
    def _():
        out[...] = jnp.zeros_like(out)

    @pl.when(relevant > 0)
    def _():
        grid[:6, : ROWS + PB * NV + BAND * NV, :] = jnp.zeros((6, ROWS + PB * NV + BAND * NV, 128), jnp.float32)
        rhs[...] = jnp.zeros_like(rhs)
        lhs[...] = jnp.zeros_like(lhs)
        for l in range(SUB_DEV):
            for kind, (near, there) in enumerate(neighbours(device * SUB_DEV + l)):
                column = ordered(near)
                value = (blocks.at[l, 0], blocks.at[l, 1], high_x.at[l], blocks.at[l, 2], high_y.at[l], blocks.at[l, 3], blocks.at[l, 4])[kind][...]
                place(value, 0, NV * l, column, there & (column < PB))
        pltpu.make_async_copy(rescue.at[pl.ds(18, 6)], got.at[3], sems.at[3]).wait()

        @pl.when(meta[1] == 7)
        def _():
            for i in range(3):
                pltpu.make_async_copy(rescue.at[pl.ds(6 * i, 6)], got.at[i], sems.at[i]).wait()

        @pl.when(meta[1] < 7)
        def _():
            row = lax.broadcasted_iota(jnp.int32, (NV, 128), 0)
            left = lane < 64
            for i in range(3):
                pltpu.make_async_copy(own, dense.at[i], sems.at[i]).wait()
                pairs = dense[i, 0]
                whole = []
                for half in range(2):
                    slot = pltpu.roll(pairs, 64, 1) if half else pairs
                    last = jnp.broadcast_to(slot[:, NV : NV + 1], (NV, 128))
                    turned_slot = flipped(jnp.where(lane < NV, slot, 0.0))
                    whole.append(jnp.where(lane <= row, slot, turned_slot))
                    whole.append(jnp.where(lane == row, last, jnp.where(lane < row, turned_slot, slot)))
                got[i, 0] = jnp.where(left, whole[0], pltpu.roll(whole[2], 64, 1))
                got[i, 3] = jnp.where(left, whole[1], pltpu.roll(whole[3], 64, 1))
                got[i, 1] = dense[i, 1]
                got[i, 4] = dense[i, 2]
                z_pair = dense[i, 3]
                z_last = jnp.where(
                    lane < 80,
                    pltpu.roll(dense[i, 1], 16, 1),
                    jnp.where(lane < 96, pltpu.roll(dense[i, 1], 96, 1), pltpu.roll(dense[i, 2], 48, 1)),
                )
                got[i, 2] = z_pair
                got[i, 5] = jnp.where(left, z_pair, z_last)
        reach = jnp.int32(0)
        for slot in range(12):
            i, l = slot // SUB_DEV, slot % SUB_DEV
            s = meta[4 + slot]
            p = ordered(s)
            near = neighbours(s)
            for kind, (t, there) in enumerate((near[0], near[3], near[5], near[1])):
                q = ordered(t)
                wanted = there & (p < PB) & (q < PB)
                reach = jnp.maximum(reach, jnp.where(wanted, jnp.abs(p - q), 0))
                if kind < 3:
                    value, half = got[i, (l % 2) * 3 + kind], l // 2
                else:
                    value, half = got[3, slot % 6], slot // 6
                place(value, half, ROWS + NV * jnp.maximum(p, q), jnp.minimum(p, q), wanted)

        rows48 = lax.broadcasted_iota(jnp.int32, (NV, 128), 0)

        unit = jnp.full((8, 128), jnp.where(device >= 0, 1.0, 0.0), jnp.float32)

        gap = jnp.zeros((16, 128), jnp.bfloat16)

        def diagonal(k):
            at = pl.ds(pl.multiple_of(ROWS + k * NV, 16), NV)
            return pltpu.roll(grid[k // 2, at, :], 64 * (1 - k % 2), 1)

        def invert(k, diag):
            work = jnp.where(lane < 64, (lane == rows48).astype(jnp.float32), jnp.where(lane < 64 + NV, diag, 0.0))
            inverse = jnp.where(lane < NV, eliminate(work, unit), 0.0)
            high, low = halves(pltpu.roll(inverse, 64 * (k % 2), 1))
            binv[0] = jnp.concatenate([high, gap, high, gap], axis=0)
            binv[1] = jnp.concatenate([low, gap, low, gap], axis=0)
            high, low = halves(inverse)
            return jnp.concatenate([high, gap, high, gap], axis=0), jnp.concatenate([low, gap, low, gap], axis=0)

        def solve(values, high, low):
            c_high, c_low = halves(values)
            return across(jnp.concatenate([c_high, c_low], axis=1), jnp.concatenate([high, high], axis=1)) + across(c_high, low)

        def mix(high, low):
            left_half = lax.broadcasted_iota(jnp.int32, high.shape, 1) < 64
            return jnp.where(left_half, high.astype(jnp.float32), low.astype(jnp.float32)).astype(jnp.bfloat16)

        def urgent(k, high, low):
            at = pl.ds(pl.multiple_of(ROWS + (k + 1) * NV, 16), NV)
            ahead = pltpu.roll(grid[k // 2, at, :], 64 * (k % 2), 1)
            following = diagonal(k + 1)
            s_high, s_low = halves(solve(ahead, high, low))
            mixed = mix(s_high, s_low)
            other = jnp.concatenate([mixed, gap, mixed, gap], axis=0)
            change = across(jnp.concatenate([s_high, s_low], axis=1), jnp.concatenate([other, other], axis=1))
            mine = lane // 64 == (k + 1) % 2
            grid[(k + 1) // 2, at, :] -= jnp.where(mine, change, 0.0)
            return following - change

        def finish(band, k, live):
            tile = k // 2
            depth = ROWS + band * NV
            window = pl.ds(pl.multiple_of(ROWS + k * NV, 16), NV + band * NV)
            later = pl.ds(pl.multiple_of(ROWS + (k + 1) * NV, 16), band * NV)
            at = pl.ds(pl.multiple_of(ROWS + k * NV, 16), NV)
            column = jnp.concatenate([grid[tile, :ROWS, :], grid[tile, window, :]], axis=0)
            solved = solve(column, binv[0], binv[1])
            corner = jnp.where((lane % 64) <= rows48, solved[ROWS : ROWS + NV], 0.0)
            parity = jnp.where(live, k % 2, 2)
            rest = jnp.concatenate([solved[:ROWS], solved[ROWS + NV :]], axis=0)
            chosen = lax.broadcasted_iota(jnp.int32, (depth, 128), 1) // 64 == parity
            kept = jnp.where(chosen, rest, jnp.concatenate([column[:ROWS], column[ROWS + NV :]], axis=0))
            grid[tile, :ROWS, :] = kept[:ROWS]
            grid[tile, later, :] = kept[ROWS:]
            grid[tile, at, :] = jnp.where(lane // 64 == parity, corner, column[ROWS : ROWS + NV])
            s_high, s_low = halves(rest)
            lhs[:depth, :128] = s_high
            lhs[:depth, 128:] = s_low
            mixed = mix(s_high[ROWS:], s_low[ROWS:])
            rhs[pl.ds(pl.multiple_of(64 * k, 64), 64), :] = jnp.zeros((64, 128), jnp.bfloat16)
            for w in range(band):
                rhs[pl.ds(pl.multiple_of(64 * (k + 1 + w), 64), NV), :] = mixed[NV * w : NV * w + NV]

        def trail(band, k, t, skip):
            depth = ROWS + band * NV
            later = pl.ds(pl.multiple_of(ROWS + (k + 1 + skip) * NV, 16), (band - skip) * NV)
            other = rhs[pl.ds(pl.multiple_of(128 * t, 128), 128), :]
            other = jnp.concatenate([other, other], axis=1)
            grid[t, :ROWS, :] -= across(lhs[:ROWS, :], other)
            grid[t, later, :] -= across(lhs[ROWS + skip * NV : depth, :], other)

        @pl.when(reach <= BAND)
        def _():
            binv[...] = jnp.zeros_like(binv)

            def body(k, carry):
                diag = carry
                last = jnp.maximum(k - 1, 0)
                finish(BAND, last, k > 0)
                for j in range(3):
                    trail(BAND, last, k // 2 + j, 1 if j == 0 else 0)
                high, low = invert(k, diag)
                return urgent(k, high, low)

            lax.fori_loop(0, PB, body, diagonal(0))
            finish(BAND, PB - 1, True)

        @pl.when(reach > BAND)
        def _():
            start = ROWS + PB * NV + BAND * NV
            grid[:6, start:, :] = jnp.zeros((6, grid.shape[1] - start, 128), jnp.float32)

            def body(k, carry):
                invert(k, diagonal(k))
                finish(PB - 1, k, True)

                def inner(t, c):
                    trail(PB - 1, k, t, 0)
                    return c

                lax.fori_loop((k + 1) // 2, 6, inner, 0)
                return carry

            lax.fori_loop(0, PB, body, 0)

        for l in range(SUB_DEV):
            p = ordered(device * SUB_DEV + l)
            inside = p < PB
            start = jnp.where(inside, ROWS + NV * p, NV * l)
            at = pl.ds(pl.multiple_of(start, 16), NV)
            pieces = []
            for j in range(PB):
                piece = grid[j // 2, at, :][:, 64 * (j % 2) : 64 * (j % 2) + NV]
                pieces.append(jnp.where(inside & (j > p), 0.0, piece))
            out[l] = jnp.concatenate(pieces, axis=1)

    flat_copy.wait()


def factor(order, meta, shares, below, above, rescue, blocks, high_y, flat):
    smem = pl.BlockSpec(memory_space=pltpu.SMEM)
    hbm = pl.BlockSpec(memory_space=pl.ANY)
    vmem = pl.BlockSpec(memory_space=pltpu.VMEM)
    return pl.pallas_call(
        factor_kernel,
        out_shape=(
            jax.ShapeDtypeStruct((SUB_DEV, NV, PB * NV), jnp.float32),
            jax.ShapeDtypeStruct(flat.shape, jnp.float32),
        ),
        in_specs=[smem] * 2 + [hbm] * 10 + [vmem] * 2 + [hbm],
        out_specs=(vmem, hbm),
        input_output_aliases={14: 1},
        scratch_shapes=[
            pltpu.VMEM((8, ROWS + PB * NV + PB * NV, 128), jnp.float32),
            pltpu.VMEM((4, 6, NV, 128), jnp.float32),
            pltpu.VMEM((3, 4, NV, 128), jnp.float32),
            pltpu.VMEM((ROWS + (PB - 1) * NV, 256), jnp.bfloat16),
            pltpu.VMEM(((2 * PB + 2) * 64, 128), jnp.bfloat16),
            pltpu.VMEM((2, 128, 128), jnp.bfloat16),
            pltpu.VMEM((2, NV, 128), jnp.float32),
            pltpu.VMEM((SUB_DEV, NV, 128), jnp.float32),
            pltpu.VMEM((NV * 8, 128), jnp.float32),
            pltpu.VMEM((SUB_DEV, NV * NV), jnp.float32),
            pltpu.SemaphoreType.DMA((4,)),
            pltpu.SemaphoreType.DMA((2,)),
        ],
        name="factor",
    )(order, meta, *shares, below, above, rescue, blocks, high_y, flat)


def shifted(value, amount):
    size = N_ROW * N_COL
    return lax.ppermute(value, ("row", "col"), [(i, (i + amount) % size) for i in range(size)])


def packed(blocks):
    wide = jnp.pad(blocks, ((0, 0), (0, 0), (0, 64 - NV)))
    return jnp.concatenate([wide[:6], wide[6:]], axis=2)


def everywhere(value):
    size = N_ROW * N_COL
    step = 1
    while step < size:
        value = value + lax.ppermute(value, ("row", "col"), [(i, i ^ step) for i in range(size)])
        step *= 2
    return value


def choose_kernel(spot, right2, right1, share, left1, left2, side, out):
    out[12:14] = side[...]
    for case, sources in enumerate(((share, left1, left2), (right1, share, left1), (right2, right1, share))):

        @pl.when(spot[3] == case)
        def _():
            for i, source in enumerate(sources):
                out[4 * i : 4 * i + 4] = source[...]


def choose(spot, right2, right1, share, left1, left2, side):
    vmem = pl.BlockSpec(memory_space=pltpu.VMEM)
    return pl.pallas_call(
        choose_kernel,
        out_shape=jax.ShapeDtypeStruct((14, NV, 128), jnp.float32),
        in_specs=[pl.BlockSpec(memory_space=pltpu.SMEM)] + [vmem] * 6,
        out_specs=vmem,
        name="choose",
    )(spot, right2, right1, share, left1, left2, side)


def exchange(device, order, blocks, share, side, plan):
    subdomain = jnp.arange(SUBS, dtype=jnp.int32)
    my_order = lax.dynamic_slice(order, (device * SUB_DEV,), (SUB_DEV,))

    right1 = shifted(share, 1)
    left1 = shifted(share, -1)
    right2 = shifted(share, 2)
    left2 = shifted(share, -2)
    payload = choose(plan, right2, right1, share, left1, left2, side)
    below = shifted(payload, N_COL)
    above = shifted(payload, -N_COL)
    flat, high_y = flatten(order, blocks, left1)
    right3 = shifted(right2, 1)
    left3 = shifted(left2, -1)
    def local_path(_):
        return (jnp.zeros((24, NV, 128), jnp.float32), plan)

    def global_path(_):
        slots = jnp.arange(12, dtype=jnp.int32)
        hit = (order[None, :] == slots[:, None]) & (slots[:, None] < PB)
        listed = jnp.where(slots < PB, jnp.sum(jnp.where(hit, subdomain[None, :], 0), axis=1), -1)
        mask = ((my_order[None, :] == slots[:, None]) & (slots[:, None] < PB)).astype(jnp.float32)
        def oriented(block, offset):
            other = lax.dynamic_slice(jnp.concatenate([order[:128], order]), (128 + device * SUB_DEV - offset,), (SUB_DEV,))
            return jnp.where((my_order > other)[:, None, None], block, jnp.swapaxes(block, 1, 2))

        kinds = jnp.stack(
            [
                blocks[:, 0, :, :NV],
                oriented(blocks[:, 2, :, :NV], SUB_DEV),
                oriented(blocks[:, 3, :, :NV], 1),
                oriented(blocks[:, 1, :, :NV], N_COL * SUB_DEV),
            ],
            axis=1,
        )
        placed = jnp.einsum("ps,skvw->pkvw", mask, kinds, precision=lax.Precision.HIGHEST)
        whole = everywhere(
            jnp.stack([packed(placed[4 * i : 4 * i + 4, :3].reshape(12, NV, NV)) for i in range(3)] + [packed(placed[:, 3])])
        )
        return (whole.reshape(24, NV, 128), jnp.concatenate([plan[:4], listed]).astype(jnp.int32))

    rescue, meta = lax.cond(plan[2] > 0, local_path, global_path, None)
    shares = (share, right1, right2, right3, left1, left2, left3)
    panel, flat = factor(order, meta, shares, below, above, rescue, blocks, high_y, flat)
    return (jnp.transpose(flat, (1, 0, 2)), panel)


def from_next(value, axis, amount):
    size = lax.axis_size(axis)
    pairs = [(i, i + amount) for i in range(size) if 0 <= i + amount < size]
    return lax.ppermute(value, axis, pairs)


def shards(deflation, coefficient, gradients, x_penalty, y_penalty, z_penalty, coarse_order):
    device = device_index()
    below_x = from_next(deflation[1, :, :, 48 * NV :], "row", 1)
    below_y = from_next(deflation[:, 7], "col", 1)
    main, own_x, own_y, roots_x, roots_y = assemble(
        deflation, gradients.reshape(192, 64), coefficient, x_penalty, jnp.transpose(y_penalty, (1, 0, 2)), z_penalty
    )
    blocks, share, side, plan = lateral(coarse_order, coarse_order.reshape(8, 128), below_x, below_y, main, own_x, own_y, roots_x, roots_y)
    return exchange(device, coarse_order, blocks, share, side, plan)


def solution(mesh):
    in_specs = (
        P("row", "col", None, None),
        P("row", "col", None),
        P(),
        P("row", "col", None),
        P("row", "col", None),
        P("row", "col", None),
        P(),
    )
    out_specs = (P(("row", "col"), None, None), P(("row", "col"), None, None))
    return jax.shard_map(shards, mesh=mesh, in_specs=in_specs, out_specs=out_specs, check_vma=False)
```

```python
import jax
import jax.numpy as jnp
from jax import lax
from jax.experimental import pallas as pl
from jax.experimental.pallas import tpu as pltpu
from jax.sharding import PartitionSpec as P

NV = 48
SUB_DEV = 4
PB = 11
SUBS = 1024
N_ROW = 8
N_COL = 32


LINE_WEIGHTS = (1.0 / 6.0, 5.0 / 6.0, 5.0 / 6.0, 1.0 / 6.0)
COEF, XPEN, YPEN, ZPEN = 0, 16, 40, 58


def fetch(tiles, start, target):
    lane = lax.broadcasted_iota(jnp.int32, tiles[0].shape, 1)
    tile, offset = start // 128, start % 128
    shift = (target - offset) % 128
    first = pltpu.roll(tiles[tile], shift, 1) if shift else tiles[tile]
    if offset + NV <= 128:
        return first
    second = pltpu.roll(tiles[tile + 1], shift, 1) if shift else tiles[tile + 1]
    return jnp.where(lane >= target + 128 - offset, second, first)


def paired(even, odd, start):
    lane = lax.broadcasted_iota(jnp.int32, even[0].shape, 1)
    return jnp.where(lane < 64, fetch(even, start, 0), fetch(odd, start, 64))


def lane_tiles(values):
    wide = values.astype(jnp.float32)
    return [wide[:, 128 * t : 128 * t + 128] for t in range(wide.shape[1] // 128)]


def gram(left, right):
    return lax.dot_general(left, right, (((0,), (0,)), ((), ())), preferred_element_type=jnp.float32)


def assemble_kernel(deflation, gradients, coefficient, x_penalty, y_penalty, z_penalty, main, own_x, own_y, roots_x, roots_y, nodes, sides, stack, second, total, roots, low_z, other_z, table):
    table[...] = jnp.zeros_like(table)
    for x in range(2):
        table[COEF + 8 * x : COEF + 8 * x + 8, :16] = coefficient[x]
        table[ZPEN + 8 * x : ZPEN + 8 * x + 8, :17] = z_penalty[x]
    for g in range(3):
        table[XPEN + 8 * g : XPEN + 8 * g + 8, :16] = x_penalty[g]
    for g in range(9):
        table[YPEN + 2 * g : YPEN + 2 * g + 2, :16] = y_penalty[g]
    rooted = jnp.sqrt(jnp.transpose(table[...]))[:24]
    half = lax.broadcasted_iota(jnp.int32, (24, 128), 1) < 64

    def spread(even, odd):
        left = jnp.broadcast_to(rooted[:, even : even + 1], (24, 128))
        right = jnp.broadcast_to(rooted[:, odd : odd + 1], (24, 128))
        return jnp.where(half, left, right)

    for i in range(4):
        for x in range(2):
            roots[0, i, x] = spread(COEF + 8 * x + 2 * i, COEF + 8 * x + 2 * i + 1)
            roots[1, i, x] = spread(XPEN + 16 * x + 2 * i, XPEN + 16 * x + 2 * i + 1)
            roots[2, i, x] = spread(XPEN + 8 + 2 * i, XPEN + 8 + 2 * i + 1)
            roots[3, i, x] = spread(YPEN + 2 * (2 * i + 1) + x, YPEN + 2 * (2 * i + 2) + x)
            roots[4, i, x] = spread(ZPEN + 8 * x + 2 * i, ZPEN + 8 * x + 2 * i + 1)
            roots[5, i, x] = jnp.where(half & (i == 0), jnp.broadcast_to(rooted[:, YPEN + x : YPEN + x + 1], (24, 128)), 0.0)
        roots_x[i] = roots[1, i, 0, :16]
    roots_y[...] = spread(YPEN, YPEN + 1)[:16]

    def relay(i, carry):
        for x in range(2):
            even = lane_tiles(deflation[x, 2 * i])
            odd = lane_tiles(deflation[x, 2 * i + 1])
            for n in range(64):
                a, b, c = n // 16, n // 4 % 4, n % 4
                both = paired(even, odd, NV * n)
                nodes[i, x, pl.ds(n, 16, stride=65), :] = both
                if b % 3 == 0:
                    sides[i, x, b // 3, pl.ds(4 * a + c, 16, stride=17), :] = both
        return carry

    lax.fori_loop(0, 4, relay, 0)
    total[...] = jnp.zeros_like(total)
    node = lax.broadcasted_iota(jnp.int32, (64, 128), 0)

    def edge(position):
        return jnp.where((position == 0) | (position == 3), LINE_WEIGHTS[0], LINE_WEIGHTS[1])

    weight = jnp.sqrt(edge(node // 16) * edge(node // 4 % 4) * edge(node % 4))
    first_half = lax.broadcasted_iota(jnp.int32, (16, 128), 1) < 64

    def fill(step, stack):
        s, i = step // 4, step % 4
        low = jnp.bfloat16

        def root(kind, x, z, rows):
            return jnp.broadcast_to(roots[kind, i, x, pl.ds(z, 1), :], (rows, 128))

        inner = []
        for zz in range(4):
            z = 4 * s + zz
            at = pl.ds(65 * z, 64)
            block = [nodes[i, x, at, :] for x in range(2)]
            z_rows = jnp.concatenate(block, axis=1).astype(low)
            product = jnp.dot(gradients[...], z_rows, preferred_element_type=jnp.float32)
            factor_z = jnp.concatenate([weight * root(0, x, z, 64) for x in range(2)], axis=1)
            for d in range(3):
                stack[192 * zz + 64 * d : 192 * zz + 64 * d + 64, :] = (product[64 * d : 64 * d + 64] * factor_z).astype(low)
            near = (block[0][:16] * root(1, 0, z, 16)).astype(low)
            far = (block[1][48:] * root(1, 1, z, 16)).astype(low)
            stack[768 + 16 * zz : 784 + 16 * zz, :] = jnp.concatenate([near, far], axis=1)
            here = pl.ds(17 * z, 16)
            there = pl.ds(pl.multiple_of(16 * z, 16), 16)
            own_x[i, there, :] = near
            inner.append((root(2, 0, z, 16) * (block[0][48:] - block[1][:16])).astype(low))
            lows, jumps = [], []
            after = jnp.minimum(i + 1, 3)
            for x in range(2):
                lower = sides[i, x, 0, here, :]
                swapped = pltpu.roll(lower, 64, 1)
                later = jnp.where(i < 3, pltpu.roll(sides[after, x, 0, here, :], 64, 1), 0.0)
                jumps.append((root(3, x, z, 16) * (sides[i, x, 1, here, :] - jnp.where(first_half, swapped, later))).astype(low))
                lows.append((root(5, x, z, 16) * lower).astype(low))
            stack[864 + 16 * zz : 880 + 16 * zz, :] = jnp.concatenate(jumps, axis=1)
            stack[928 + 16 * zz : 944 + 16 * zz, :] = jnp.concatenate(lows, axis=1)
            ups, firsts, befores = [], [], []
            for x in range(2):
                upper = nodes[i, x, pl.ds(65 * z + 3, 16, stride=4), :]
                if zz < 3:
                    upper = upper - nodes[i, x, pl.ds(65 * z + 65, 16, stride=4), :]
                ups.append((root(4, x, z + 1, 16) * upper).astype(low))
                if zz == 0:
                    firsts.append((root(4, x, z, 16) * nodes[i, x, pl.ds(65 * z, 16, stride=4), :]).astype(low))
                    before = nodes[i, x, pl.ds(65 * jnp.maximum(z - 1, 0) + 3, 16, stride=4), :]
                    befores.append(jnp.where(s > 0, root(4, x, z, 16) * before, 0.0).astype(low))
            stack[992 + 16 * zz : 1008 + 16 * zz, :] = jnp.concatenate(ups, axis=1)
            if zz == 0:
                stack[1056:1072, :] = jnp.concatenate(firsts, axis=1)
                row = pl.ds(pl.multiple_of(16 * i, 16), 16)
                low_z[s, row, :] = jnp.concatenate(firsts, axis=1)
                other_z[s, row, :] = jnp.concatenate(befores, axis=1)
        stack[832:848, :] = jnp.concatenate(inner[:2], axis=1)
        stack[848:864, :] = jnp.concatenate(inner[2:], axis=1)

    def add(step, stack):
        total[step // 4] += gram(stack[...], stack[...])

    second[...] = jnp.zeros_like(second)

    def pair(step, carry):
        add(jnp.maximum(2 * step - 1, 0), second)
        fill(2 * step, stack)
        add(2 * step, stack)
        fill(2 * step + 1, second)
        return carry

    lax.fori_loop(0, 8, pair, 0)
    add(15, second)

    def folded(square):
        return (
            square[:NV, :128]
            + pltpu.roll(square[64 : 64 + NV, :128], 64, 1)
            + square[128 : 128 + NV, 128:]
            + pltpu.roll(square[192 : 192 + NV, 128:], 64, 1)
        )

    for s in range(4):
        main[s, 0] = folded(total[s])
        below = -folded(gram(low_z[s], other_z[s]))
        main[s, 1] = below
        if s:
            main[s - 1, 2] = jnp.transpose(jnp.concatenate([below, jnp.zeros((80, 128), jnp.float32)], axis=0))[:NV]
    main[3, 2] = jnp.zeros((NV, 128), jnp.float32)
    for z in range(16):
        here = slice(16 * z, 16 * z + 16)
        there = slice(17 * z, 17 * z + 16)
        lower = [sides[0, x, 0, there, :] for x in range(2)]
        near = jnp.where(first_half, lower[0], pltpu.roll(lower[1], 64, 1))
        own_y[here, :] = (near * jnp.broadcast_to(roots_y[z : z + 1, :], (16, 128))).astype(jnp.bfloat16)


def assemble(deflation, gradients, coefficient, x_penalty, y_penalty, z_penalty):
    vmem = pl.BlockSpec(memory_space=pltpu.VMEM)
    f32, low = jnp.float32, jnp.bfloat16
    return pl.pallas_call(
        assemble_kernel,
        out_shape=(
            jax.ShapeDtypeStruct((4, 3, NV, 128), f32),
            jax.ShapeDtypeStruct((4, 256, 128), low),
            jax.ShapeDtypeStruct((256, 128), low),
            jax.ShapeDtypeStruct((4, 16, 128), f32),
            jax.ShapeDtypeStruct((16, 128), f32),
        ),
        in_specs=[vmem] * 6,
        out_specs=(vmem,) * 5,
        scratch_shapes=[
            pltpu.VMEM((4, 2, 1040, 128), f32),
            pltpu.VMEM((4, 2, 2, 272, 128), f32),
            pltpu.VMEM((1072, 256), low),
            pltpu.VMEM((1072, 256), low),
            pltpu.VMEM((4, 256, 256), f32),
            pltpu.VMEM((6, 4, 2, 24, 128), f32),
            pltpu.VMEM((4, 64, 256), low),
            pltpu.VMEM((4, 64, 256), low),
            pltpu.VMEM((128, 128), f32),
        ],
        cost_estimate=pl.CostEstimate(flops=2_000_000_000, bytes_accessed=3_000_000, transcendentals=0),
        name="assemble",
    )(deflation, gradients, coefficient, x_penalty, y_penalty, z_penalty)


def device_index():
    return (lax.axis_index("row") * N_COL + lax.axis_index("col")).astype(jnp.int32)


def flipped(block):
    return jnp.transpose(jnp.concatenate([block, jnp.zeros((80, 128), jnp.float32)], axis=0))[:NV]


def lateral_kernel(order, ranks, below_x, below_y, main, own_x, own_y, roots_x, roots_y, blocks, share, side, plan, halo_x, halo_y):
    device = device_index()
    size = N_ROW * N_COL
    rank_all = ranks[...]
    holder = (lax.broadcasted_iota(jnp.int32, (8, 128), 0) * 128 + lax.broadcasted_iota(jnp.int32, (8, 128), 1)) // SUB_DEV
    first = jnp.sum(jnp.where(rank_all == 0, holder.astype(jnp.float32), 0.0)).astype(jnp.int32)
    distance = (((holder - first + size // 2) & (size - 1)) - size // 2).astype(jnp.float32)
    least = jnp.min(jnp.where(rank_all < PB, distance, float(size))).astype(jnp.int32)
    most = jnp.max(jnp.where(rank_all < PB, distance, float(-size))).astype(jnp.int32)
    base = (first + least) & (size - 1)
    offset = ((base - device + size // 2) & (size - 1)) - size // 2
    near = (most - least) <= 2
    from_below = ((offset + N_COL + 2) & (size - 1)) <= 2
    from_above = ((offset - N_COL + 2) & (size - 1)) <= 2
    beside = (offset >= -3) & (offset <= 1)
    plan[0] = device
    plan[1] = jnp.where(near, jnp.where(beside, offset + 3, jnp.where(from_below, 5, jnp.where(from_above, 6, 0))), 7)
    plan[2] = near.astype(jnp.int32)
    plan[3] = jnp.where(offset == 0, 0, jnp.where(offset == -1, 1, 2))
    for slot in range(12):
        plan[4 + slot] = (base * SUB_DEV + slot) & (SUBS - 1)
    low = jnp.bfloat16
    inside = lax.broadcasted_iota(jnp.int32, (NV, 128), 1) < NV

    def relay(i, carry):
        even = lane_tiles(below_x[2 * i])
        odd = lane_tiles(below_x[2 * i + 1])
        for m in range(16):
            halo_x[i, pl.ds(m, 16, stride=17), :] = paired(even, odd, NV * m) * roots_x[i]
        return carry

    lax.fori_loop(0, 4, relay, 0)
    even = lane_tiles(below_y[0])
    odd = lane_tiles(below_y[1])
    for m in range(16):
        n = 16 * (m // 4) + 12 + m % 4
        halo_y[pl.ds(m, 16, stride=17), :] = paired(even, odd, NV * n) * roots_y[...]

    def folded(square):
        return jnp.where(inside, -(square[:NV] + pltpu.roll(square[64 : 64 + NV], 64, 1)), 0.0)

    diags, low_ys, low_zs = [], [], []
    for s in range(SUB_DEV):
        at = slice(64 * s, 64 * s + 64)
        diag = jnp.where(inside, main[s, 0], 0.0)
        low_z = jnp.where(inside, main[s, 1], 0.0)
        mine = jnp.concatenate([own_x[i, at, :] for i in range(4)], axis=0)
        theirs = [halo_x[i, 17 * z : 17 * z + 16, :].astype(low) for i in range(4) for z in range(4 * s, 4 * s + 4)]
        low_x = folded(gram(mine, jnp.concatenate(theirs, axis=0)))
        theirs = [halo_y[17 * z : 17 * z + 16, :].astype(low) for z in range(4 * s, 4 * s + 4)]
        low_y = folded(gram(own_y[at, :], jnp.concatenate(theirs, axis=0)))
        blocks[s, 0] = diag
        blocks[s, 1] = low_x
        blocks[s, 2] = low_y
        blocks[s, 3] = low_z
        blocks[s, 4] = jnp.where(inside, main[s, 2], 0.0)
        here = device * SUB_DEV + s
        rank = order[here]
        turned_y = jnp.where(rank > order[jnp.maximum(here - SUB_DEV, 0)], low_y, flipped(low_y))
        turned_z = jnp.where(rank > order[jnp.maximum(here - 1, 0)], low_z, flipped(low_z))
        diags.append(diag)
        low_ys.append(turned_y)
        low_zs.append(turned_z)
        if s < 2:
            side[s] = low_x
        else:
            side[s - 2] += pltpu.roll(low_x, 64, 1)
    lane = lax.broadcasted_iota(jnp.int32, (NV, 128), 1)
    row = lax.broadcasted_iota(jnp.int32, (NV, 128), 0)

    def both(lower, upper):
        last = jnp.sum(jnp.where(lane == row, upper, 0.0), axis=1, keepdims=True)
        return jnp.where(lane <= row, lower, upper) + jnp.where(lane == NV, jnp.broadcast_to(last, (NV, 128)), 0.0)

    def piece(start, target):
        moved = pltpu.roll(low_zs[3], (target - start) % 128, 1)
        return jnp.where((lane >= target) & (lane < target + 16), moved, 0.0)

    share[0] = both(diags[0], diags[1]) + pltpu.roll(both(diags[2], diags[3]), 64, 1)
    share[1] = low_ys[0] + pltpu.roll(low_ys[2], 64, 1) + piece(0, 48) + piece(16, 112)
    share[2] = low_ys[1] + pltpu.roll(low_ys[3], 64, 1) + piece(32, 48)
    share[3] = low_zs[1] + pltpu.roll(low_zs[2], 64, 1)


def lateral(order, ranks, below_x, below_y, main, own_x, own_y, roots_x, roots_y):
    smem = pl.BlockSpec(memory_space=pltpu.SMEM)
    vmem = pl.BlockSpec(memory_space=pltpu.VMEM)
    f32 = jnp.float32
    return pl.pallas_call(
        lateral_kernel,
        out_shape=(
            jax.ShapeDtypeStruct((SUB_DEV, 5, NV, 128), f32),
            jax.ShapeDtypeStruct((4, NV, 128), f32),
            jax.ShapeDtypeStruct((2, NV, 128), f32),
            jax.ShapeDtypeStruct((16,), jnp.int32),
        ),
        in_specs=[smem] + [vmem] * 8,
        out_specs=(vmem, vmem, vmem, smem),
        scratch_shapes=[
            pltpu.VMEM((4, 272, 128), f32),
            pltpu.VMEM((272, 128), f32),
        ],
        name="lateral",
    )(order, ranks, below_x, below_y, main, own_x, own_y, roots_x, roots_y)


def row_major(read, write):
    lane = lax.broadcasted_iota(jnp.int32, (8, 128), 1)
    for t in range(18):
        value = None
        for v in range(NV):
            shift = NV * v - 128 * t
            if shift <= -NV or shift >= 128:
                continue
            row = read(v)
            row = pltpu.roll(row, shift % 128, 1) if shift % 128 else row
            here = (lane >= shift) & (lane < shift + NV)
            value = jnp.where(here, row, 0.0 if value is None else value)
        write(t, value)


def flatten_kernel(order, blocks, above, out, high_y, turned):
    device = device_index()
    places = (0, 1, 3, 5, 6)
    for s in range(SUB_DEV):
        for kind in range(5):
            group = (SUB_DEV * kind + s) // 8
            turned[group, pl.ds((SUB_DEV * kind + s) % 8, NV, stride=8), :] = blocks[s, kind]
        packed_low = above[1 + s % 2]
        if s >= 2:
            packed_low = pltpu.roll(packed_low, 64, 1)
        packed_low = jnp.where(lax.broadcasted_iota(jnp.int32, (NV, 128), 1) < NV, packed_low, 0.0)
        here = device * SUB_DEV + s
        later = order[jnp.minimum(here + SUB_DEV, SUBS - 1)]
        upper = jnp.where(order[here] > later, packed_low, flipped(packed_low))
        high_y[s] = upper
        turned[2, pl.ds(SUB_DEV + s, NV, stride=8), :] = upper
    for group in range(3):
        low_place = places[2 * group]
        high_place = places[2 * group + 1] if group < 2 else 4

        def write(t, value):
            out[low_place, :, 128 * t : 128 * t + 128] = value[:4]
            out[high_place, :, 128 * t : 128 * t + 128] = value[4:]

        row_major(lambda v: turned[group, 8 * v : 8 * v + 8, :], write)


def flatten(order, blocks, above):
    smem = pl.BlockSpec(memory_space=pltpu.SMEM)
    vmem = pl.BlockSpec(memory_space=pltpu.VMEM)
    return pl.pallas_call(
        flatten_kernel,
        out_shape=(
            jax.ShapeDtypeStruct((7, SUB_DEV, NV * NV), jnp.float32),
            jax.ShapeDtypeStruct((SUB_DEV, NV, 128), jnp.float32),
        ),
        in_specs=[smem] + [vmem] * 2,
        out_specs=(vmem, vmem),
        scratch_shapes=[pltpu.VMEM((3, NV * 8, 128), jnp.float32)],
        cost_estimate=pl.CostEstimate(flops=1_000_000, bytes_accessed=2_000_000, transcendentals=0),
        name="flatten",
    )(order, blocks, above)


def eliminate(work, unit):
    groups = [work[8 * v : 8 * v + 8] for v in range(6)]
    sub = lax.broadcasted_iota(jnp.int32, (8, 128), 0)

    def row_of(value, k):
        return jnp.broadcast_to(value[k : k + 1, :], (8, 128))

    def column_of(value, k):
        return jnp.broadcast_to(value[:, k : k + 1], (8, 128))

    for g in range(6):
        head = groups[g]
        splat = [column_of(head, 64 + 8 * g + k) * unit for k in range(8)]
        below = [[column_of(groups[v], 64 + 8 * g + k) for k in range(8)] for v in range(g + 1, 6)]
        done = jnp.zeros((8, 128), jnp.float32)
        for k in range(0, 8, 2):
            x, y = splat[k], splat[k + 1]
            a, b, c = row_of(x, k), row_of(y, k), row_of(y, k + 1)
            inverse = 1.0 / (a * c - b * b)
            ratio = b / a
            top, low = row_of(head, k), row_of(head, k + 1)
            done = jnp.where(sub == k, top * lax.rsqrt(a), done)
            done = jnp.where(sub == k + 1, (low - ratio * top) * lax.rsqrt(c - ratio * b), done)

            def reduced(value, upper, lower):
                one = (c * upper - b * lower) * inverse
                two = (a * lower - b * upper) * inverse
                return jnp.where(sub == k, one, jnp.where(sub == k + 1, two, value - x * one - y * two))

            for m in range(k + 2, 8):
                splat[m] = reduced(splat[m], row_of(splat[m], k), row_of(splat[m], k + 1))
            head = reduced(head, top, low)
        rows = [row_of(head, k) for k in range(8)]
        for v in range(g + 1, 6):
            terms = [s * r for s, r in zip(below[v - g - 1], rows)]
            while len(terms) > 1:
                terms = [p + q for p, q in zip(terms[::2], terms[1::2])]
            groups[v] = groups[v] - terms[0]
        groups[g] = done
    return jnp.concatenate(groups, axis=0)


def halves(values):
    high = values.astype(jnp.bfloat16)
    low = (values - high.astype(jnp.float32)).astype(jnp.bfloat16)
    return high, low


def across(left, right):
    return lax.dot_general(left, right, (((1,), (1,)), ((), ())), preferred_element_type=jnp.float32)


ROWS = SUB_DEV * NV
BAND = 4


def factor_kernel(order, meta, own, right1, right2, right3, left1, left2, left3, below, above, rescue, blocks, high_y, flat_in, out, flat, grid, got, dense, lhs, rhs, binv, side, high_x, turned, slab, sems, side_sems):
    device = meta[0]
    lane = lax.broadcasted_iota(jnp.int32, (NV, 128), 1)

    def place(value, half, row, column, wanted):
        parity = column % 2
        moved = pltpu.roll(value, 64 * ((parity + half) % 2), 1)
        inside = (lane >= 64 * parity) & (lane < 64 * parity + NV)
        tile = jnp.where(wanted, column // 2, 7)
        at = pl.ds(pl.multiple_of(jnp.where(wanted, row, 0), 16), NV)
        pltpu.store(grid.at[tile, at, :], moved, mask=inside)

    def ordered(subdomain):
        return order[jnp.clip(subdomain, 0, SUBS - 1)]

    def neighbours(subdomain):
        column = (subdomain // SUB_DEV) % N_COL
        local = subdomain % SUB_DEV
        stride = N_COL * SUB_DEV
        return (
            (subdomain, subdomain >= 0),
            (subdomain - stride, subdomain >= stride),
            (subdomain + stride, (subdomain >= 0) & (subdomain < SUBS - stride)),
            (subdomain - SUB_DEV, (subdomain >= 0) & (column > 0)),
            (subdomain + SUB_DEV, (subdomain >= 0) & (column < N_COL - 1)),
            (subdomain - 1, (subdomain >= 0) & (local > 0)),
            (subdomain + 1, (subdomain >= 0) & (local < SUB_DEV - 1)),
        )

    relevant = jnp.int32(0)
    for l in range(SUB_DEV):
        for near, there in neighbours(device * SUB_DEV + l):
            relevant += (there & (ordered(near) < PB)).astype(jnp.int32)

    side_copy = pltpu.make_async_copy(above.at[pl.ds(12, 2)], side, side_sems.at[0])
    side_copy.start()

    @pl.when(relevant > 0)
    def _():
        near_sources = [right3, right2, right1, own, left1, left2, left3]
        for case in range(5):

            @pl.when(meta[1] == case)
            def _():
                for i in range(3):
                    pltpu.make_async_copy(near_sources[case + i], dense.at[i], sems.at[i]).start()

        for case, source in ((5, below), (6, above)):

            @pl.when(meta[1] == case)
            def _():
                for i in range(3):
                    pltpu.make_async_copy(source.at[pl.ds(4 * i, 4)], dense.at[i], sems.at[i]).start()

        @pl.when(meta[1] == 7)
        def _():
            for i in range(3):
                pltpu.make_async_copy(rescue.at[pl.ds(6 * i, 6)], got.at[i], sems.at[i]).start()

        pltpu.make_async_copy(rescue.at[pl.ds(18, 6)], got.at[3], sems.at[3]).start()

    side_copy.wait()
    for s in range(SUB_DEV):
        packed_low = side[s % 2]
        if s >= 2:
            packed_low = pltpu.roll(packed_low, 64, 1)
        upper = flipped(jnp.where(lane < NV, packed_low, 0.0))
        high_x[s] = upper
        turned[pl.ds(s, NV, stride=8), :] = upper

    def write(t, value):
        slab[:, 128 * t : 128 * t + 128] = value[:4]

    row_major(lambda v: turned[8 * v : 8 * v + 8, :], write)
    flat_copy = pltpu.make_async_copy(slab, flat.at[2], side_sems.at[1])
    flat_copy.start()

    @pl.when(relevant == 0)
    def _():
        out[...] = jnp.zeros_like(out)

    @pl.when(relevant > 0)
    def _():
        grid[:6, : ROWS + PB * NV + BAND * NV, :] = jnp.zeros((6, ROWS + PB * NV + BAND * NV, 128), jnp.float32)
        rhs[...] = jnp.zeros_like(rhs)
        lhs[...] = jnp.zeros_like(lhs)
        for l in range(SUB_DEV):
            for kind, (near, there) in enumerate(neighbours(device * SUB_DEV + l)):
                column = ordered(near)
                value = (blocks.at[l, 0], blocks.at[l, 1], high_x.at[l], blocks.at[l, 2], high_y.at[l], blocks.at[l, 3], blocks.at[l, 4])[kind][...]
                place(value, 0, NV * l, column, there & (column < PB))
        pltpu.make_async_copy(rescue.at[pl.ds(18, 6)], got.at[3], sems.at[3]).wait()

        @pl.when(meta[1] == 7)
        def _():
            for i in range(3):
                pltpu.make_async_copy(rescue.at[pl.ds(6 * i, 6)], got.at[i], sems.at[i]).wait()

        @pl.when(meta[1] < 7)
        def _():
            row = lax.broadcasted_iota(jnp.int32, (NV, 128), 0)
            left = lane < 64
            for i in range(3):
                pltpu.make_async_copy(own, dense.at[i], sems.at[i]).wait()
                pairs = dense[i, 0]
                whole = []
                for half in range(2):
                    slot = pltpu.roll(pairs, 64, 1) if half else pairs
                    last = jnp.broadcast_to(slot[:, NV : NV + 1], (NV, 128))
                    turned_slot = flipped(jnp.where(lane < NV, slot, 0.0))
                    whole.append(jnp.where(lane <= row, slot, turned_slot))
                    whole.append(jnp.where(lane == row, last, jnp.where(lane < row, turned_slot, slot)))
                got[i, 0] = jnp.where(left, whole[0], pltpu.roll(whole[2], 64, 1))
                got[i, 3] = jnp.where(left, whole[1], pltpu.roll(whole[3], 64, 1))
                got[i, 1] = dense[i, 1]
                got[i, 4] = dense[i, 2]
                z_pair = dense[i, 3]
                z_last = jnp.where(
                    lane < 80,
                    pltpu.roll(dense[i, 1], 16, 1),
                    jnp.where(lane < 96, pltpu.roll(dense[i, 1], 96, 1), pltpu.roll(dense[i, 2], 48, 1)),
                )
                got[i, 2] = z_pair
                got[i, 5] = jnp.where(left, z_pair, z_last)
        reach = jnp.int32(0)
        for slot in range(12):
            i, l = slot // SUB_DEV, slot % SUB_DEV
            s = meta[4 + slot]
            p = ordered(s)
            near = neighbours(s)
            for kind, (t, there) in enumerate((near[0], near[3], near[5], near[1])):
                q = ordered(t)
                wanted = there & (p < PB) & (q < PB)
                reach = jnp.maximum(reach, jnp.where(wanted, jnp.abs(p - q), 0))
                if kind < 3:
                    place(got[i, (l % 2) * 3 + kind], l // 2, ROWS + NV * jnp.maximum(p, q), jnp.minimum(p, q), wanted)

        @pl.when(meta[1] == 7)
        def _():
            for slot in range(12):
                s = meta[4 + slot]
                p = ordered(s)
                t, there = neighbours(s)[1]
                q = ordered(t)
                place(got[3, slot % 6], slot // 6, ROWS + NV * jnp.maximum(p, q), jnp.minimum(p, q), there & (p < PB) & (q < PB))

        rows48 = lax.broadcasted_iota(jnp.int32, (NV, 128), 0)

        unit = jnp.full((8, 128), jnp.where(device >= 0, 1.0, 0.0), jnp.float32)

        gap = jnp.zeros((16, 128), jnp.bfloat16)

        def diagonal(k):
            at = pl.ds(pl.multiple_of(ROWS + k * NV, 16), NV)
            return pltpu.roll(grid[k // 2, at, :], 64 * (1 - k % 2), 1)

        def invert(k, diag):
            work = jnp.where(lane < 64, (lane == rows48).astype(jnp.float32), jnp.where(lane < 64 + NV, diag, 0.0))
            inverse = jnp.where(lane < NV, eliminate(work, unit), 0.0)
            high, low = halves(pltpu.roll(inverse, 64 * (k % 2), 1))
            binv[0] = jnp.concatenate([high, gap, high, gap], axis=0)
            binv[1] = jnp.concatenate([low, gap, low, gap], axis=0)
            high, low = halves(inverse)
            return jnp.concatenate([high, gap, high, gap], axis=0), jnp.concatenate([low, gap, low, gap], axis=0)

        def solve(values, high, low):
            c_high, c_low = halves(values)
            return across(jnp.concatenate([c_high, c_low], axis=1), jnp.concatenate([high, high], axis=1)) + across(c_high, low)

        def mix(high, low):
            left_half = lax.broadcasted_iota(jnp.int32, high.shape, 1) < 64
            return jnp.where(left_half, high.astype(jnp.float32), low.astype(jnp.float32)).astype(jnp.bfloat16)

        def urgent(k, high, low):
            at = pl.ds(pl.multiple_of(ROWS + (k + 1) * NV, 16), NV)
            ahead = pltpu.roll(grid[k // 2, at, :], 64 * (k % 2), 1)
            following = diagonal(k + 1)
            s_high, s_low = halves(solve(ahead, high, low))
            mixed = mix(s_high, s_low)
            other = jnp.concatenate([mixed, gap, mixed, gap], axis=0)
            change = across(jnp.concatenate([s_high, s_low], axis=1), jnp.concatenate([other, other], axis=1))
            mine = lane // 64 == (k + 1) % 2
            grid[(k + 1) // 2, at, :] -= jnp.where(mine, change, 0.0)
            return following - change

        def finish(band, k, live):
            tile = k // 2
            depth = ROWS + band * NV
            window = pl.ds(pl.multiple_of(ROWS + k * NV, 16), NV + band * NV)
            later = pl.ds(pl.multiple_of(ROWS + (k + 1) * NV, 16), band * NV)
            at = pl.ds(pl.multiple_of(ROWS + k * NV, 16), NV)
            column = jnp.concatenate([grid[tile, :ROWS, :], grid[tile, window, :]], axis=0)
            solved = solve(column, binv[0], binv[1])
            corner = jnp.where((lane % 64) <= rows48, solved[ROWS : ROWS + NV], 0.0)
            parity = jnp.where(live, k % 2, 2)
            rest = jnp.concatenate([solved[:ROWS], solved[ROWS + NV :]], axis=0)
            chosen = lax.broadcasted_iota(jnp.int32, (depth, 128), 1) // 64 == parity
            kept = jnp.where(chosen, rest, jnp.concatenate([column[:ROWS], column[ROWS + NV :]], axis=0))
            grid[tile, :ROWS, :] = kept[:ROWS]
            grid[tile, later, :] = kept[ROWS:]
            grid[tile, at, :] = jnp.where(lane // 64 == parity, corner, column[ROWS : ROWS + NV])
            s_high, s_low = halves(rest)
            lhs[:depth, :128] = s_high
            lhs[:depth, 128:] = s_low
            mixed = mix(s_high[ROWS:], s_low[ROWS:])
            rhs[pl.ds(pl.multiple_of(64 * k, 64), 64), :] = jnp.zeros((64, 128), jnp.bfloat16)
            for w in range(band):
                rhs[pl.ds(pl.multiple_of(64 * (k + 1 + w), 64), NV), :] = mixed[NV * w : NV * w + NV]

        def trail(band, k, t, skip):
            depth = ROWS + band * NV
            later = pl.ds(pl.multiple_of(ROWS + (k + 1 + skip) * NV, 16), (band - skip) * NV)
            other = rhs[pl.ds(pl.multiple_of(128 * t, 128), 128), :]
            other = jnp.concatenate([other, other], axis=1)
            grid[t, :ROWS, :] -= across(lhs[:ROWS, :], other)
            grid[t, later, :] -= across(lhs[ROWS + skip * NV : depth, :], other)

        @pl.when(reach <= BAND)
        def _():
            binv[...] = jnp.zeros_like(binv)

            def body(k, carry):
                diag = carry
                last = jnp.maximum(k - 1, 0)
                finish(BAND, last, k > 0)
                for j in range(3):
                    trail(BAND, last, k // 2 + j, 1 if j == 0 else 0)
                high, low = invert(k, diag)
                return urgent(k, high, low)

            lax.fori_loop(0, PB, body, diagonal(0))
            finish(BAND, PB - 1, True)

        @pl.when(reach > BAND)
        def _():
            start = ROWS + PB * NV + BAND * NV
            grid[:6, start:, :] = jnp.zeros((6, grid.shape[1] - start, 128), jnp.float32)

            def body(k, carry):
                invert(k, diagonal(k))
                finish(PB - 1, k, True)

                def inner(t, c):
                    trail(PB - 1, k, t, 0)
                    return c

                lax.fori_loop((k + 1) // 2, 6, inner, 0)
                return carry

            lax.fori_loop(0, PB, body, 0)

        for l in range(SUB_DEV):
            p = ordered(device * SUB_DEV + l)
            inside = p < PB
            start = jnp.where(inside, ROWS + NV * p, NV * l)
            at = pl.ds(pl.multiple_of(start, 16), NV)
            pieces = []
            for j in range(PB):
                piece = grid[j // 2, at, :][:, 64 * (j % 2) : 64 * (j % 2) + NV]
                pieces.append(jnp.where(inside & (j > p), 0.0, piece))
            out[l] = jnp.concatenate(pieces, axis=1)

    flat_copy.wait()


def factor(order, meta, shares, below, above, rescue, blocks, high_y, flat):
    smem = pl.BlockSpec(memory_space=pltpu.SMEM)
    hbm = pl.BlockSpec(memory_space=pl.ANY)
    vmem = pl.BlockSpec(memory_space=pltpu.VMEM)
    return pl.pallas_call(
        factor_kernel,
        out_shape=(
            jax.ShapeDtypeStruct((SUB_DEV, NV, PB * NV), jnp.float32),
            jax.ShapeDtypeStruct(flat.shape, jnp.float32),
        ),
        in_specs=[smem] * 2 + [hbm] * 10 + [vmem] * 2 + [hbm],
        out_specs=(vmem, hbm),
        input_output_aliases={14: 1},
        scratch_shapes=[
            pltpu.VMEM((8, ROWS + PB * NV + PB * NV, 128), jnp.float32),
            pltpu.VMEM((4, 6, NV, 128), jnp.float32),
            pltpu.VMEM((3, 4, NV, 128), jnp.float32),
            pltpu.VMEM((ROWS + (PB - 1) * NV, 256), jnp.bfloat16),
            pltpu.VMEM(((2 * PB + 2) * 64, 128), jnp.bfloat16),
            pltpu.VMEM((2, 128, 128), jnp.bfloat16),
            pltpu.VMEM((2, NV, 128), jnp.float32),
            pltpu.VMEM((SUB_DEV, NV, 128), jnp.float32),
            pltpu.VMEM((NV * 8, 128), jnp.float32),
            pltpu.VMEM((SUB_DEV, NV * NV), jnp.float32),
            pltpu.SemaphoreType.DMA((4,)),
            pltpu.SemaphoreType.DMA((2,)),
        ],
        name="factor",
    )(order, meta, *shares, below, above, rescue, blocks, high_y, flat)


def shifted(value, amount):
    size = N_ROW * N_COL
    return lax.ppermute(value, ("row", "col"), [(i, (i + amount) % size) for i in range(size)])


def packed(blocks):
    wide = jnp.pad(blocks, ((0, 0), (0, 0), (0, 64 - NV)))
    return jnp.concatenate([wide[:6], wide[6:]], axis=2)


def everywhere(value):
    size = N_ROW * N_COL
    step = 1
    while step < size:
        value = value + lax.ppermute(value, ("row", "col"), [(i, i ^ step) for i in range(size)])
        step *= 2
    return value


def choose_kernel(spot, right2, right1, share, left1, left2, side, out):
    out[12:14] = side[...]
    for case, sources in enumerate(((share, left1, left2), (right1, share, left1), (right2, right1, share))):

        @pl.when(spot[3] == case)
        def _():
            for i, source in enumerate(sources):
                out[4 * i : 4 * i + 4] = source[...]


def choose(spot, right2, right1, share, left1, left2, side):
    vmem = pl.BlockSpec(memory_space=pltpu.VMEM)
    return pl.pallas_call(
        choose_kernel,
        out_shape=jax.ShapeDtypeStruct((14, NV, 128), jnp.float32),
        in_specs=[pl.BlockSpec(memory_space=pltpu.SMEM)] + [vmem] * 6,
        out_specs=vmem,
        name="choose",
    )(spot, right2, right1, share, left1, left2, side)


def exchange(device, order, blocks, share, side, plan):
    subdomain = jnp.arange(SUBS, dtype=jnp.int32)
    my_order = lax.dynamic_slice(order, (device * SUB_DEV,), (SUB_DEV,))

    right1 = shifted(share, 1)
    left1 = shifted(share, -1)
    right2 = shifted(share, 2)
    left2 = shifted(share, -2)
    payload = choose(plan, right2, right1, share, left1, left2, side)
    below = shifted(payload, N_COL)
    above = shifted(payload, -N_COL)
    flat, high_y = flatten(order, blocks, left1)
    right3 = shifted(right2, 1)
    left3 = shifted(left2, -1)
    def local_path(_):
        return (jnp.zeros((24, NV, 128), jnp.float32), plan)

    def global_path(_):
        slots = jnp.arange(12, dtype=jnp.int32)
        hit = (order[None, :] == slots[:, None]) & (slots[:, None] < PB)
        listed = jnp.where(slots < PB, jnp.sum(jnp.where(hit, subdomain[None, :], 0), axis=1), -1)
        mask = ((my_order[None, :] == slots[:, None]) & (slots[:, None] < PB)).astype(jnp.float32)
        def oriented(block, offset):
            other = lax.dynamic_slice(jnp.concatenate([order[:128], order]), (128 + device * SUB_DEV - offset,), (SUB_DEV,))
            return jnp.where((my_order > other)[:, None, None], block, jnp.swapaxes(block, 1, 2))

        kinds = jnp.stack(
            [
                blocks[:, 0, :, :NV],
                oriented(blocks[:, 2, :, :NV], SUB_DEV),
                oriented(blocks[:, 3, :, :NV], 1),
                oriented(blocks[:, 1, :, :NV], N_COL * SUB_DEV),
            ],
            axis=1,
        )
        placed = jnp.einsum("ps,skvw->pkvw", mask, kinds, precision=lax.Precision.HIGHEST)
        whole = everywhere(
            jnp.stack([packed(placed[4 * i : 4 * i + 4, :3].reshape(12, NV, NV)) for i in range(3)] + [packed(placed[:, 3])])
        )
        return (whole.reshape(24, NV, 128), jnp.concatenate([plan[:4], listed]).astype(jnp.int32))

    rescue, meta = lax.cond(plan[2] > 0, local_path, global_path, None)
    shares = (share, right1, right2, right3, left1, left2, left3)
    panel, flat = factor(order, meta, shares, below, above, rescue, blocks, high_y, flat)
    return (jnp.transpose(flat, (1, 0, 2)), panel)


def edges_kernel(deflation, along_x, along_y, sems):
    x_copy = pltpu.make_async_copy(deflation.at[1, :, :, pl.ds(48 * NV, 16 * NV)], along_x, sems.at[0])
    y_copies = [pltpu.make_async_copy(deflation.at[x, 7], along_y.at[x], sems.at[1 + x]) for x in range(2)]
    x_copy.start()
    for copy in y_copies:
        copy.start()
    x_copy.wait()
    for copy in y_copies:
        copy.wait()


def edges(deflation):
    vmem = pl.BlockSpec(memory_space=pltpu.VMEM)
    return pl.pallas_call(
        edges_kernel,
        out_shape=(
            jax.ShapeDtypeStruct((8, 16, 16 * NV), jnp.bfloat16),
            jax.ShapeDtypeStruct((2, 16, 64 * NV), jnp.bfloat16),
        ),
        in_specs=[pl.BlockSpec(memory_space=pl.ANY)],
        out_specs=(vmem, vmem),
        scratch_shapes=[pltpu.SemaphoreType.DMA((3,))],
        name="edges",
    )(deflation)


def from_next(value, axis, amount):
    size = lax.axis_size(axis)
    pairs = [(i, i + amount) for i in range(size) if 0 <= i + amount < size]
    return lax.ppermute(value, axis, pairs)


def shards(deflation, coefficient, gradients, x_penalty, y_penalty, z_penalty, coarse_order):
    device = device_index()
    along_x, along_y = edges(deflation)
    below_x = from_next(along_x, "row", 1)
    below_y = from_next(along_y, "col", 1)
    main, own_x, own_y, roots_x, roots_y = assemble(
        deflation, gradients.reshape(192, 64), coefficient, x_penalty, jnp.transpose(y_penalty, (1, 0, 2)), z_penalty
    )
    blocks, share, side, plan = lateral(coarse_order, coarse_order.reshape(8, 128), below_x, below_y, main, own_x, own_y, roots_x, roots_y)
    return exchange(device, coarse_order, blocks, share, side, plan)


def solution(mesh):
    in_specs = (
        P("row", "col", None, None),
        P("row", "col", None),
        P(),
        P("row", "col", None),
        P("row", "col", None),
        P("row", "col", None),
        P(),
    )
    out_specs = (P(("row", "col"), None, None), P(("row", "col"), None, None))
    return jax.shard_map(shards, mesh=mesh, in_specs=in_specs, out_specs=out_specs, check_vma=False)
```

```python
import jax
import jax.numpy as jnp
from jax import lax
from jax.experimental import pallas as pl
from jax.experimental.pallas import tpu as pltpu
from jax.sharding import PartitionSpec as P

NV = 48
SUB_DEV = 4
PB = 11
SUBS = 1024
N_ROW = 8
N_COL = 32


LINE_WEIGHTS = (1.0 / 6.0, 5.0 / 6.0, 5.0 / 6.0, 1.0 / 6.0)
COEF, XPEN, YPEN, ZPEN = 0, 16, 40, 58


def fetch(tiles, start, target):
    lane = lax.broadcasted_iota(jnp.int32, tiles[0].shape, 1)
    tile, offset = start // 128, start % 128
    shift = (target - offset) % 128
    first = pltpu.roll(tiles[tile], shift, 1) if shift else tiles[tile]
    if offset + NV <= 128:
        return first
    second = pltpu.roll(tiles[tile + 1], shift, 1) if shift else tiles[tile + 1]
    return jnp.where(lane >= target + 128 - offset, second, first)


def paired(even, odd, start):
    lane = lax.broadcasted_iota(jnp.int32, even[0].shape, 1)
    return jnp.where(lane < 64, fetch(even, start, 0), fetch(odd, start, 64))


def lane_tiles(values):
    wide = values.astype(jnp.float32)
    return [wide[:, 128 * t : 128 * t + 128] for t in range(wide.shape[1] // 128)]


def gram(left, right):
    return lax.dot_general(left, right, (((0,), (0,)), ((), ())), preferred_element_type=jnp.float32)


def assemble_kernel(deflation, gradients, coefficient, x_penalty, y_penalty, z_penalty, main, own_x, own_y, roots_x, roots_y, nodes, sides, stack, second, total, roots, low_z, other_z, table):
    table[...] = jnp.zeros_like(table)
    for x in range(2):
        table[COEF + 8 * x : COEF + 8 * x + 8, :16] = coefficient[x]
        table[ZPEN + 8 * x : ZPEN + 8 * x + 8, :17] = z_penalty[x]
    for g in range(3):
        table[XPEN + 8 * g : XPEN + 8 * g + 8, :16] = x_penalty[g]
    for g in range(9):
        table[YPEN + 2 * g : YPEN + 2 * g + 2, :16] = y_penalty[g]
    rooted = jnp.sqrt(jnp.transpose(table[...]))[:24]
    half = lax.broadcasted_iota(jnp.int32, (24, 128), 1) < 64

    def spread(even, odd):
        left = jnp.broadcast_to(rooted[:, even : even + 1], (24, 128))
        right = jnp.broadcast_to(rooted[:, odd : odd + 1], (24, 128))
        return jnp.where(half, left, right)

    for i in range(4):
        for x in range(2):
            roots[0, i, x] = spread(COEF + 8 * x + 2 * i, COEF + 8 * x + 2 * i + 1)
            roots[1, i, x] = spread(XPEN + 16 * x + 2 * i, XPEN + 16 * x + 2 * i + 1)
            roots[2, i, x] = spread(XPEN + 8 + 2 * i, XPEN + 8 + 2 * i + 1)
            roots[3, i, x] = spread(YPEN + 2 * (2 * i + 1) + x, YPEN + 2 * (2 * i + 2) + x)
            roots[4, i, x] = spread(ZPEN + 8 * x + 2 * i, ZPEN + 8 * x + 2 * i + 1)
            roots[5, i, x] = jnp.where(half & (i == 0), jnp.broadcast_to(rooted[:, YPEN + x : YPEN + x + 1], (24, 128)), 0.0)
        roots_x[i] = roots[1, i, 0, :16]
    roots_y[...] = spread(YPEN, YPEN + 1)[:16]

    def relay(i, carry):
        for x in range(2):
            even = lane_tiles(deflation[x, 2 * i])
            odd = lane_tiles(deflation[x, 2 * i + 1])
            for n in range(64):
                a, b, c = n // 16, n // 4 % 4, n % 4
                both = paired(even, odd, NV * n)
                nodes[i, x, pl.ds(n, 16, stride=65), :] = both
                if b % 3 == 0:
                    sides[i, x, b // 3, pl.ds(4 * a + c, 16, stride=17), :] = both
        return carry

    lax.fori_loop(0, 4, relay, 0)
    total[...] = jnp.zeros_like(total)
    node = lax.broadcasted_iota(jnp.int32, (64, 128), 0)

    def edge(position):
        return jnp.where((position == 0) | (position == 3), LINE_WEIGHTS[0], LINE_WEIGHTS[1])

    weight = jnp.sqrt(edge(node // 16) * edge(node // 4 % 4) * edge(node % 4))
    first_half = lax.broadcasted_iota(jnp.int32, (16, 128), 1) < 64

    def fill(step, stack):
        s, i = step // 4, step % 4
        low = jnp.bfloat16

        def root(kind, x, z, rows):
            return jnp.broadcast_to(roots[kind, i, x, pl.ds(z, 1), :], (rows, 128))

        inner = []
        for zz in range(4):
            z = 4 * s + zz
            at = pl.ds(65 * z, 64)
            block = [nodes[i, x, at, :] for x in range(2)]
            z_rows = jnp.concatenate(block, axis=1).astype(low)
            product = jnp.dot(gradients[...], z_rows, preferred_element_type=jnp.float32)
            factor_z = jnp.concatenate([weight * root(0, x, z, 64) for x in range(2)], axis=1)
            for d in range(3):
                stack[192 * zz + 64 * d : 192 * zz + 64 * d + 64, :] = (product[64 * d : 64 * d + 64] * factor_z).astype(low)
            near = (block[0][:16] * root(1, 0, z, 16)).astype(low)
            far = (block[1][48:] * root(1, 1, z, 16)).astype(low)
            stack[768 + 16 * zz : 784 + 16 * zz, :] = jnp.concatenate([near, far], axis=1)
            here = pl.ds(17 * z, 16)
            there = pl.ds(pl.multiple_of(16 * z, 16), 16)
            own_x[i, there, :] = near
            inner.append((root(2, 0, z, 16) * (block[0][48:] - block[1][:16])).astype(low))
            lows, jumps = [], []
            after = jnp.minimum(i + 1, 3)
            for x in range(2):
                lower = sides[i, x, 0, here, :]
                swapped = pltpu.roll(lower, 64, 1)
                later = jnp.where(i < 3, pltpu.roll(sides[after, x, 0, here, :], 64, 1), 0.0)
                jumps.append((root(3, x, z, 16) * (sides[i, x, 1, here, :] - jnp.where(first_half, swapped, later))).astype(low))
                lows.append((root(5, x, z, 16) * lower).astype(low))
            stack[864 + 16 * zz : 880 + 16 * zz, :] = jnp.concatenate(jumps, axis=1)
            stack[928 + 16 * zz : 944 + 16 * zz, :] = jnp.concatenate(lows, axis=1)
            ups, firsts, befores = [], [], []
            for x in range(2):
                upper = nodes[i, x, pl.ds(65 * z + 3, 16, stride=4), :]
                if zz < 3:
                    upper = upper - nodes[i, x, pl.ds(65 * z + 65, 16, stride=4), :]
                ups.append((root(4, x, z + 1, 16) * upper).astype(low))
                if zz == 0:
                    firsts.append((root(4, x, z, 16) * nodes[i, x, pl.ds(65 * z, 16, stride=4), :]).astype(low))
                    before = nodes[i, x, pl.ds(65 * jnp.maximum(z - 1, 0) + 3, 16, stride=4), :]
                    befores.append(jnp.where(s > 0, root(4, x, z, 16) * before, 0.0).astype(low))
            stack[992 + 16 * zz : 1008 + 16 * zz, :] = jnp.concatenate(ups, axis=1)
            if zz == 0:
                stack[1056:1072, :] = jnp.concatenate(firsts, axis=1)
                row = pl.ds(pl.multiple_of(16 * i, 16), 16)
                low_z[s, row, :] = jnp.concatenate(firsts, axis=1)
                other_z[s, row, :] = jnp.concatenate(befores, axis=1)
        stack[832:848, :] = jnp.concatenate(inner[:2], axis=1)
        stack[848:864, :] = jnp.concatenate(inner[2:], axis=1)

    def add(step, stack):
        total[step // 4] += gram(stack[...], stack[...])

    second[...] = jnp.zeros_like(second)

    def pair(step, carry):
        add(jnp.maximum(2 * step - 1, 0), second)
        fill(2 * step, stack)
        add(2 * step, stack)
        fill(2 * step + 1, second)
        return carry

    lax.fori_loop(0, 8, pair, 0)
    add(15, second)

    def folded(square):
        return (
            square[:NV, :128]
            + pltpu.roll(square[64 : 64 + NV, :128], 64, 1)
            + square[128 : 128 + NV, 128:]
            + pltpu.roll(square[192 : 192 + NV, 128:], 64, 1)
        )

    for s in range(4):
        main[s, 0] = folded(total[s])
        below = -folded(gram(low_z[s], other_z[s]))
        main[s, 1] = below
        if s:
            main[s - 1, 2] = jnp.transpose(jnp.concatenate([below, jnp.zeros((80, 128), jnp.float32)], axis=0))[:NV]
    main[3, 2] = jnp.zeros((NV, 128), jnp.float32)
    for z in range(16):
        here = slice(16 * z, 16 * z + 16)
        there = slice(17 * z, 17 * z + 16)
        lower = [sides[0, x, 0, there, :] for x in range(2)]
        near = jnp.where(first_half, lower[0], pltpu.roll(lower[1], 64, 1))
        own_y[here, :] = (near * jnp.broadcast_to(roots_y[z : z + 1, :], (16, 128))).astype(jnp.bfloat16)


def assemble(deflation, gradients, coefficient, x_penalty, y_penalty, z_penalty):
    vmem = pl.BlockSpec(memory_space=pltpu.VMEM)
    f32, low = jnp.float32, jnp.bfloat16
    return pl.pallas_call(
        assemble_kernel,
        out_shape=(
            jax.ShapeDtypeStruct((4, 3, NV, 128), f32),
            jax.ShapeDtypeStruct((4, 256, 128), low),
            jax.ShapeDtypeStruct((256, 128), low),
            jax.ShapeDtypeStruct((4, 16, 128), f32),
            jax.ShapeDtypeStruct((16, 128), f32),
        ),
        in_specs=[vmem] * 6,
        out_specs=(vmem,) * 5,
        scratch_shapes=[
            pltpu.VMEM((4, 2, 1040, 128), f32),
            pltpu.VMEM((4, 2, 2, 272, 128), f32),
            pltpu.VMEM((1072, 256), low),
            pltpu.VMEM((1072, 256), low),
            pltpu.VMEM((4, 256, 256), f32),
            pltpu.VMEM((6, 4, 2, 24, 128), f32),
            pltpu.VMEM((4, 64, 256), low),
            pltpu.VMEM((4, 64, 256), low),
            pltpu.VMEM((128, 128), f32),
        ],
        cost_estimate=pl.CostEstimate(flops=2_000_000_000, bytes_accessed=3_000_000, transcendentals=0),
        name="assemble",
    )(deflation, gradients, coefficient, x_penalty, y_penalty, z_penalty)


def device_index():
    return (lax.axis_index("row") * N_COL + lax.axis_index("col")).astype(jnp.int32)


def flipped(block):
    return jnp.transpose(jnp.concatenate([block, jnp.zeros((80, 128), jnp.float32)], axis=0))[:NV]


def lateral_kernel(order, ranks, below_x, below_y, main, own_x, own_y, roots_x, roots_y, blocks, share, side, plan, local, halo_x, halo_y):
    device = device_index()
    size = N_ROW * N_COL
    rank_all = ranks[...]
    holder = (lax.broadcasted_iota(jnp.int32, (8, 128), 0) * 128 + lax.broadcasted_iota(jnp.int32, (8, 128), 1)) // SUB_DEV
    first = jnp.sum(jnp.where(rank_all == 0, holder.astype(jnp.float32), 0.0)).astype(jnp.int32)
    distance = (((holder - first + size // 2) & (size - 1)) - size // 2).astype(jnp.float32)
    least = jnp.min(jnp.where(rank_all < PB, distance, float(size))).astype(jnp.int32)
    most = jnp.max(jnp.where(rank_all < PB, distance, float(-size))).astype(jnp.int32)
    base = (first + least) & (size - 1)
    offset = ((base - device + size // 2) & (size - 1)) - size // 2
    near = (most - least) <= 2
    from_below = ((offset + N_COL + 2) & (size - 1)) <= 2
    from_above = ((offset - N_COL + 2) & (size - 1)) <= 2
    beside = (offset >= -3) & (offset <= 1)
    plan[0] = device
    plan[1] = jnp.where(near, jnp.where(beside, offset + 3, jnp.where(from_below, 5, jnp.where(from_above, 6, 0))), 7)
    plan[2] = near.astype(jnp.int32)
    local[0] = near.astype(jnp.int32)
    plan[3] = jnp.where(offset == 0, 0, jnp.where(offset == -1, 1, 2))
    for slot in range(12):
        plan[4 + slot] = (base * SUB_DEV + slot) & (SUBS - 1)
    low = jnp.bfloat16
    inside = lax.broadcasted_iota(jnp.int32, (NV, 128), 1) < NV

    def relay(i, carry):
        even = lane_tiles(below_x[2 * i])
        odd = lane_tiles(below_x[2 * i + 1])
        for m in range(16):
            halo_x[i, pl.ds(m, 16, stride=17), :] = paired(even, odd, NV * m) * roots_x[i]
        return carry

    lax.fori_loop(0, 4, relay, 0)
    even = lane_tiles(below_y[0])
    odd = lane_tiles(below_y[1])
    for m in range(16):
        n = 16 * (m // 4) + 12 + m % 4
        halo_y[pl.ds(m, 16, stride=17), :] = paired(even, odd, NV * n) * roots_y[...]

    def folded(square):
        return jnp.where(inside, -(square[:NV] + pltpu.roll(square[64 : 64 + NV], 64, 1)), 0.0)

    diags, low_ys, low_zs = [], [], []
    for s in range(SUB_DEV):
        at = slice(64 * s, 64 * s + 64)
        diag = jnp.where(inside, main[s, 0], 0.0)
        low_z = jnp.where(inside, main[s, 1], 0.0)
        mine = jnp.concatenate([own_x[i, at, :] for i in range(4)], axis=0)
        theirs = [halo_x[i, 17 * z : 17 * z + 16, :].astype(low) for i in range(4) for z in range(4 * s, 4 * s + 4)]
        low_x = folded(gram(mine, jnp.concatenate(theirs, axis=0)))
        theirs = [halo_y[17 * z : 17 * z + 16, :].astype(low) for z in range(4 * s, 4 * s + 4)]
        low_y = folded(gram(own_y[at, :], jnp.concatenate(theirs, axis=0)))
        blocks[s, 0] = diag
        blocks[s, 1] = low_x
        blocks[s, 2] = low_y
        blocks[s, 3] = low_z
        blocks[s, 4] = jnp.where(inside, main[s, 2], 0.0)
        here = device * SUB_DEV + s
        rank = order[here]
        turned_y = jnp.where(rank > order[jnp.maximum(here - SUB_DEV, 0)], low_y, flipped(low_y))
        turned_z = jnp.where(rank > order[jnp.maximum(here - 1, 0)], low_z, flipped(low_z))
        diags.append(diag)
        low_ys.append(turned_y)
        low_zs.append(turned_z)
        if s < 2:
            side[s] = low_x
        else:
            side[s - 2] += pltpu.roll(low_x, 64, 1)
    lane = lax.broadcasted_iota(jnp.int32, (NV, 128), 1)
    row = lax.broadcasted_iota(jnp.int32, (NV, 128), 0)

    def both(lower, upper):
        last = jnp.sum(jnp.where(lane == row, upper, 0.0), axis=1, keepdims=True)
        return jnp.where(lane <= row, lower, upper) + jnp.where(lane == NV, jnp.broadcast_to(last, (NV, 128)), 0.0)

    def piece(start, target):
        moved = pltpu.roll(low_zs[3], (target - start) % 128, 1)
        return jnp.where((lane >= target) & (lane < target + 16), moved, 0.0)

    share[0] = both(diags[0], diags[1]) + pltpu.roll(both(diags[2], diags[3]), 64, 1)
    share[1] = low_ys[0] + pltpu.roll(low_ys[2], 64, 1) + piece(0, 48) + piece(16, 112)
    share[2] = low_ys[1] + pltpu.roll(low_ys[3], 64, 1) + piece(32, 48)
    share[3] = low_zs[1] + pltpu.roll(low_zs[2], 64, 1)


def lateral(order, ranks, below_x, below_y, main, own_x, own_y, roots_x, roots_y):
    smem = pl.BlockSpec(memory_space=pltpu.SMEM)
    vmem = pl.BlockSpec(memory_space=pltpu.VMEM)
    f32 = jnp.float32
    return pl.pallas_call(
        lateral_kernel,
        out_shape=(
            jax.ShapeDtypeStruct((SUB_DEV, 5, NV, 128), f32),
            jax.ShapeDtypeStruct((4, NV, 128), f32),
            jax.ShapeDtypeStruct((2, NV, 128), f32),
            jax.ShapeDtypeStruct((16,), jnp.int32),
            jax.ShapeDtypeStruct((1,), jnp.int32),
        ),
        in_specs=[smem] + [vmem] * 8,
        out_specs=(vmem, vmem, vmem, smem, smem),
        scratch_shapes=[
            pltpu.VMEM((4, 272, 128), f32),
            pltpu.VMEM((272, 128), f32),
        ],
        name="lateral",
    )(order, ranks, below_x, below_y, main, own_x, own_y, roots_x, roots_y)


def row_major(read, write):
    lane = lax.broadcasted_iota(jnp.int32, (8, 128), 1)
    for t in range(18):
        value = None
        for v in range(NV):
            shift = NV * v - 128 * t
            if shift <= -NV or shift >= 128:
                continue
            row = read(v)
            row = pltpu.roll(row, shift % 128, 1) if shift % 128 else row
            here = (lane >= shift) & (lane < shift + NV)
            value = jnp.where(here, row, 0.0 if value is None else value)
        write(t, value)


def flatten_kernel(order, blocks, above, out, high_y, turned):
    device = device_index()
    places = (0, 1, 3, 5, 6)
    for s in range(SUB_DEV):
        for kind in range(5):
            group = (SUB_DEV * kind + s) // 8
            turned[group, pl.ds((SUB_DEV * kind + s) % 8, NV, stride=8), :] = blocks[s, kind]
        packed_low = above[1 + s % 2]
        if s >= 2:
            packed_low = pltpu.roll(packed_low, 64, 1)
        packed_low = jnp.where(lax.broadcasted_iota(jnp.int32, (NV, 128), 1) < NV, packed_low, 0.0)
        here = device * SUB_DEV + s
        later = order[jnp.minimum(here + SUB_DEV, SUBS - 1)]
        upper = jnp.where(order[here] > later, packed_low, flipped(packed_low))
        high_y[s] = upper
        turned[2, pl.ds(SUB_DEV + s, NV, stride=8), :] = upper
    for group in range(3):
        low_place = places[2 * group]
        high_place = places[2 * group + 1] if group < 2 else 4

        def write(t, value):
            out[low_place, :, 128 * t : 128 * t + 128] = value[:4]
            out[high_place, :, 128 * t : 128 * t + 128] = value[4:]

        row_major(lambda v: turned[group, 8 * v : 8 * v + 8, :], write)


def flatten(order, blocks, above):
    smem = pl.BlockSpec(memory_space=pltpu.SMEM)
    vmem = pl.BlockSpec(memory_space=pltpu.VMEM)
    return pl.pallas_call(
        flatten_kernel,
        out_shape=(
            jax.ShapeDtypeStruct((7, SUB_DEV, NV * NV), jnp.float32),
            jax.ShapeDtypeStruct((SUB_DEV, NV, 128), jnp.float32),
        ),
        in_specs=[smem] + [vmem] * 2,
        out_specs=(vmem, vmem),
        scratch_shapes=[pltpu.VMEM((3, NV * 8, 128), jnp.float32)],
        cost_estimate=pl.CostEstimate(flops=1_000_000, bytes_accessed=2_000_000, transcendentals=0),
        name="flatten",
    )(order, blocks, above)


def eliminate(work, unit):
    groups = [work[8 * v : 8 * v + 8] for v in range(6)]
    sub = lax.broadcasted_iota(jnp.int32, (8, 128), 0)

    def row_of(value, k):
        return jnp.broadcast_to(value[k : k + 1, :], (8, 128))

    def column_of(value, k):
        return jnp.broadcast_to(value[:, k : k + 1], (8, 128))

    for g in range(6):
        head = groups[g]
        splat = [column_of(head, 64 + 8 * g + k) * unit for k in range(8)]
        below = [[column_of(groups[v], 64 + 8 * g + k) for k in range(8)] for v in range(g + 1, 6)]
        done = jnp.zeros((8, 128), jnp.float32)
        for k in range(0, 8, 2):
            x, y = splat[k], splat[k + 1]
            a, b, c = row_of(x, k), row_of(y, k), row_of(y, k + 1)
            inverse = 1.0 / (a * c - b * b)
            ratio = b / a
            top, low = row_of(head, k), row_of(head, k + 1)
            done = jnp.where(sub == k, top * lax.rsqrt(a), done)
            done = jnp.where(sub == k + 1, (low - ratio * top) * lax.rsqrt(c - ratio * b), done)

            def reduced(value, upper, lower):
                one = (c * upper - b * lower) * inverse
                two = (a * lower - b * upper) * inverse
                return jnp.where(sub == k, one, jnp.where(sub == k + 1, two, value - x * one - y * two))

            for m in range(k + 2, 8):
                splat[m] = reduced(splat[m], row_of(splat[m], k), row_of(splat[m], k + 1))
            head = reduced(head, top, low)
        rows = [row_of(head, k) for k in range(8)]
        for v in range(g + 1, 6):
            terms = [s * r for s, r in zip(below[v - g - 1], rows)]
            while len(terms) > 1:
                terms = [p + q for p, q in zip(terms[::2], terms[1::2])]
            groups[v] = groups[v] - terms[0]
        groups[g] = done
    return jnp.concatenate(groups, axis=0)


def halves(values):
    high = values.astype(jnp.bfloat16)
    low = (values - high.astype(jnp.float32)).astype(jnp.bfloat16)
    return high, low


def across(left, right):
    return lax.dot_general(left, right, (((1,), (1,)), ((), ())), preferred_element_type=jnp.float32)


ROWS = SUB_DEV * NV
BAND = 4


def factor_kernel(order, meta, own, right1, right2, right3, left1, left2, left3, below, above, rescue, blocks, high_y, flat_in, out, flat, grid, got, dense, lhs, rhs, binv, side, high_x, turned, slab, sems, side_sems):
    device = meta[0]
    lane = lax.broadcasted_iota(jnp.int32, (NV, 128), 1)

    def place(value, half, row, column, wanted):
        parity = column % 2
        moved = pltpu.roll(value, 64 * ((parity + half) % 2), 1)
        inside = (lane >= 64 * parity) & (lane < 64 * parity + NV)
        tile = jnp.where(wanted, column // 2, 7)
        at = pl.ds(pl.multiple_of(jnp.where(wanted, row, 0), 16), NV)
        pltpu.store(grid.at[tile, at, :], moved, mask=inside)

    def ordered(subdomain):
        return order[jnp.clip(subdomain, 0, SUBS - 1)]

    def neighbours(subdomain):
        column = (subdomain // SUB_DEV) % N_COL
        local = subdomain % SUB_DEV
        stride = N_COL * SUB_DEV
        return (
            (subdomain, subdomain >= 0),
            (subdomain - stride, subdomain >= stride),
            (subdomain + stride, (subdomain >= 0) & (subdomain < SUBS - stride)),
            (subdomain - SUB_DEV, (subdomain >= 0) & (column > 0)),
            (subdomain + SUB_DEV, (subdomain >= 0) & (column < N_COL - 1)),
            (subdomain - 1, (subdomain >= 0) & (local > 0)),
            (subdomain + 1, (subdomain >= 0) & (local < SUB_DEV - 1)),
        )

    relevant = jnp.int32(0)
    for l in range(SUB_DEV):
        for near, there in neighbours(device * SUB_DEV + l):
            relevant += (there & (ordered(near) < PB)).astype(jnp.int32)

    side_copy = pltpu.make_async_copy(above.at[pl.ds(12, 2)], side, side_sems.at[0])
    side_copy.start()

    @pl.when(relevant > 0)
    def _():
        near_sources = [right3, right2, right1, own, left1, left2, left3]
        for case in range(5):

            @pl.when(meta[1] == case)
            def _():
                for i in range(3):
                    pltpu.make_async_copy(near_sources[case + i], dense.at[i], sems.at[i]).start()

        for case, source in ((5, below), (6, above)):

            @pl.when(meta[1] == case)
            def _():
                for i in range(3):
                    pltpu.make_async_copy(source.at[pl.ds(4 * i, 4)], dense.at[i], sems.at[i]).start()

        @pl.when(meta[1] == 7)
        def _():
            for i in range(3):
                pltpu.make_async_copy(rescue.at[pl.ds(6 * i, 6)], got.at[i], sems.at[i]).start()

        pltpu.make_async_copy(rescue.at[pl.ds(18, 6)], got.at[3], sems.at[3]).start()

    side_copy.wait()
    for s in range(SUB_DEV):
        packed_low = side[s % 2]
        if s >= 2:
            packed_low = pltpu.roll(packed_low, 64, 1)
        upper = flipped(jnp.where(lane < NV, packed_low, 0.0))
        high_x[s] = upper
        turned[pl.ds(s, NV, stride=8), :] = upper

    def write(t, value):
        slab[:, 128 * t : 128 * t + 128] = value[:4]

    row_major(lambda v: turned[8 * v : 8 * v + 8, :], write)
    flat_copy = pltpu.make_async_copy(slab, flat.at[2], side_sems.at[1])
    flat_copy.start()

    @pl.when(relevant == 0)
    def _():
        out[...] = jnp.zeros_like(out)

    @pl.when(relevant > 0)
    def _():
        grid[:6, : ROWS + PB * NV + BAND * NV, :] = jnp.zeros((6, ROWS + PB * NV + BAND * NV, 128), jnp.float32)
        rhs[...] = jnp.zeros_like(rhs)
        lhs[...] = jnp.zeros_like(lhs)
        for l in range(SUB_DEV):
            for kind, (near, there) in enumerate(neighbours(device * SUB_DEV + l)):
                column = ordered(near)
                value = (blocks.at[l, 0], blocks.at[l, 1], high_x.at[l], blocks.at[l, 2], high_y.at[l], blocks.at[l, 3], blocks.at[l, 4])[kind][...]
                place(value, 0, NV * l, column, there & (column < PB))
        pltpu.make_async_copy(rescue.at[pl.ds(18, 6)], got.at[3], sems.at[3]).wait()

        @pl.when(meta[1] == 7)
        def _():
            for i in range(3):
                pltpu.make_async_copy(rescue.at[pl.ds(6 * i, 6)], got.at[i], sems.at[i]).wait()

        @pl.when(meta[1] < 7)
        def _():
            row = lax.broadcasted_iota(jnp.int32, (NV, 128), 0)
            left = lane < 64
            for i in range(3):
                pltpu.make_async_copy(own, dense.at[i], sems.at[i]).wait()
                pairs = dense[i, 0]
                whole = []
                for half in range(2):
                    slot = pltpu.roll(pairs, 64, 1) if half else pairs
                    last = jnp.broadcast_to(slot[:, NV : NV + 1], (NV, 128))
                    turned_slot = flipped(jnp.where(lane < NV, slot, 0.0))
                    whole.append(jnp.where(lane <= row, slot, turned_slot))
                    whole.append(jnp.where(lane == row, last, jnp.where(lane < row, turned_slot, slot)))
                got[i, 0] = jnp.where(left, whole[0], pltpu.roll(whole[2], 64, 1))
                got[i, 3] = jnp.where(left, whole[1], pltpu.roll(whole[3], 64, 1))
                got[i, 1] = dense[i, 1]
                got[i, 4] = dense[i, 2]
                z_pair = dense[i, 3]
                z_last = jnp.where(
                    lane < 80,
                    pltpu.roll(dense[i, 1], 16, 1),
                    jnp.where(lane < 96, pltpu.roll(dense[i, 1], 96, 1), pltpu.roll(dense[i, 2], 48, 1)),
                )
                got[i, 2] = z_pair
                got[i, 5] = jnp.where(left, z_pair, z_last)
        reach = jnp.int32(0)
        for slot in range(12):
            i, l = slot // SUB_DEV, slot % SUB_DEV
            s = meta[4 + slot]
            p = ordered(s)
            near = neighbours(s)
            for kind, (t, there) in enumerate((near[0], near[3], near[5], near[1])):
                q = ordered(t)
                wanted = there & (p < PB) & (q < PB)
                reach = jnp.maximum(reach, jnp.where(wanted, jnp.abs(p - q), 0))
                if kind < 3:
                    place(got[i, (l % 2) * 3 + kind], l // 2, ROWS + NV * jnp.maximum(p, q), jnp.minimum(p, q), wanted)

        @pl.when(meta[1] == 7)
        def _():
            for slot in range(12):
                s = meta[4 + slot]
                p = ordered(s)
                t, there = neighbours(s)[1]
                q = ordered(t)
                place(got[3, slot % 6], slot // 6, ROWS + NV * jnp.maximum(p, q), jnp.minimum(p, q), there & (p < PB) & (q < PB))

        rows48 = lax.broadcasted_iota(jnp.int32, (NV, 128), 0)

        unit = jnp.full((8, 128), jnp.where(device >= 0, 1.0, 0.0), jnp.float32)

        gap = jnp.zeros((16, 128), jnp.bfloat16)

        def diagonal(k):
            at = pl.ds(pl.multiple_of(ROWS + k * NV, 16), NV)
            return pltpu.roll(grid[k // 2, at, :], 64 * (1 - k % 2), 1)

        def invert(k, diag):
            work = jnp.where(lane < 64, (lane == rows48).astype(jnp.float32), jnp.where(lane < 64 + NV, diag, 0.0))
            inverse = jnp.where(lane < NV, eliminate(work, unit), 0.0)
            high, low = halves(pltpu.roll(inverse, 64 * (k % 2), 1))
            binv[0] = jnp.concatenate([high, gap, high, gap], axis=0)
            binv[1] = jnp.concatenate([low, gap, low, gap], axis=0)
            high, low = halves(inverse)
            return jnp.concatenate([high, gap, high, gap], axis=0), jnp.concatenate([low, gap, low, gap], axis=0)

        def solve(values, high, low):
            c_high, c_low = halves(values)
            return across(jnp.concatenate([c_high, c_low], axis=1), jnp.concatenate([high, high], axis=1)) + across(c_high, low)

        def mix(high, low):
            left_half = lax.broadcasted_iota(jnp.int32, high.shape, 1) < 64
            return jnp.where(left_half, high.astype(jnp.float32), low.astype(jnp.float32)).astype(jnp.bfloat16)

        def urgent(k, high, low):
            at = pl.ds(pl.multiple_of(ROWS + (k + 1) * NV, 16), NV)
            ahead = pltpu.roll(grid[k // 2, at, :], 64 * (k % 2), 1)
            following = diagonal(k + 1)
            s_high, s_low = halves(solve(ahead, high, low))
            mixed = mix(s_high, s_low)
            other = jnp.concatenate([mixed, gap, mixed, gap], axis=0)
            change = across(jnp.concatenate([s_high, s_low], axis=1), jnp.concatenate([other, other], axis=1))
            mine = lane // 64 == (k + 1) % 2
            grid[(k + 1) // 2, at, :] -= jnp.where(mine, change, 0.0)
            return following - change

        def finish(band, k, live):
            tile = k // 2
            depth = ROWS + band * NV
            window = pl.ds(pl.multiple_of(ROWS + k * NV, 16), NV + band * NV)
            later = pl.ds(pl.multiple_of(ROWS + (k + 1) * NV, 16), band * NV)
            at = pl.ds(pl.multiple_of(ROWS + k * NV, 16), NV)
            column = jnp.concatenate([grid[tile, :ROWS, :], grid[tile, window, :]], axis=0)
            solved = solve(column, binv[0], binv[1])
            corner = jnp.where((lane % 64) <= rows48, solved[ROWS : ROWS + NV], 0.0)
            parity = jnp.where(live, k % 2, 2)
            rest = jnp.concatenate([solved[:ROWS], solved[ROWS + NV :]], axis=0)
            chosen = lax.broadcasted_iota(jnp.int32, (depth, 128), 1) // 64 == parity
            kept = jnp.where(chosen, rest, jnp.concatenate([column[:ROWS], column[ROWS + NV :]], axis=0))
            grid[tile, :ROWS, :] = kept[:ROWS]
            grid[tile, later, :] = kept[ROWS:]
            grid[tile, at, :] = jnp.where(lane // 64 == parity, corner, column[ROWS : ROWS + NV])
            s_high, s_low = halves(rest)
            lhs[:depth, :128] = s_high
            lhs[:depth, 128:] = s_low
            mixed = mix(s_high[ROWS:], s_low[ROWS:])
            rhs[pl.ds(pl.multiple_of(64 * k, 64), 64), :] = jnp.zeros((64, 128), jnp.bfloat16)
            for w in range(band):
                rhs[pl.ds(pl.multiple_of(64 * (k + 1 + w), 64), NV), :] = mixed[NV * w : NV * w + NV]

        def trail(band, k, t, skip):
            depth = ROWS + band * NV
            later = pl.ds(pl.multiple_of(ROWS + (k + 1 + skip) * NV, 16), (band - skip) * NV)
            other = rhs[pl.ds(pl.multiple_of(128 * t, 128), 128), :]
            other = jnp.concatenate([other, other], axis=1)
            grid[t, :ROWS, :] -= across(lhs[:ROWS, :], other)
            grid[t, later, :] -= across(lhs[ROWS + skip * NV : depth, :], other)

        @pl.when(reach <= BAND)
        def _():
            binv[...] = jnp.zeros_like(binv)

            def body(k, carry):
                diag = carry
                last = jnp.maximum(k - 1, 0)
                finish(BAND, last, k > 0)
                for j in range(3):
                    trail(BAND, last, k // 2 + j, 1 if j == 0 else 0)
                high, low = invert(k, diag)
                return urgent(k, high, low)

            lax.fori_loop(0, PB, body, diagonal(0))
            finish(BAND, PB - 1, True)

        @pl.when(reach > BAND)
        def _():
            start = ROWS + PB * NV + BAND * NV
            grid[:6, start:, :] = jnp.zeros((6, grid.shape[1] - start, 128), jnp.float32)

            def body(k, carry):
                invert(k, diagonal(k))
                finish(PB - 1, k, True)

                def inner(t, c):
                    trail(PB - 1, k, t, 0)
                    return c

                lax.fori_loop((k + 1) // 2, 6, inner, 0)
                return carry

            lax.fori_loop(0, PB, body, 0)

        for l in range(SUB_DEV):
            p = ordered(device * SUB_DEV + l)
            inside = p < PB
            start = jnp.where(inside, ROWS + NV * p, NV * l)
            at = pl.ds(pl.multiple_of(start, 16), NV)
            pieces = []
            for j in range(PB):
                piece = grid[j // 2, at, :][:, 64 * (j % 2) : 64 * (j % 2) + NV]
                pieces.append(jnp.where(inside & (j > p), 0.0, piece))
            out[l] = jnp.concatenate(pieces, axis=1)

    flat_copy.wait()


def factor(order, meta, shares, below, above, rescue, blocks, high_y, flat):
    smem = pl.BlockSpec(memory_space=pltpu.SMEM)
    hbm = pl.BlockSpec(memory_space=pl.ANY)
    vmem = pl.BlockSpec(memory_space=pltpu.VMEM)
    return pl.pallas_call(
        factor_kernel,
        out_shape=(
            jax.ShapeDtypeStruct((SUB_DEV, NV, PB * NV), jnp.float32),
            jax.ShapeDtypeStruct(flat.shape, jnp.float32),
        ),
        in_specs=[smem] * 2 + [hbm] * 10 + [vmem] * 2 + [hbm],
        out_specs=(vmem, hbm),
        input_output_aliases={14: 1},
        scratch_shapes=[
            pltpu.VMEM((8, ROWS + PB * NV + PB * NV, 128), jnp.float32),
            pltpu.VMEM((4, 6, NV, 128), jnp.float32),
            pltpu.VMEM((3, 4, NV, 128), jnp.float32),
            pltpu.VMEM((ROWS + (PB - 1) * NV, 256), jnp.bfloat16),
            pltpu.VMEM(((2 * PB + 2) * 64, 128), jnp.bfloat16),
            pltpu.VMEM((2, 128, 128), jnp.bfloat16),
            pltpu.VMEM((2, NV, 128), jnp.float32),
            pltpu.VMEM((SUB_DEV, NV, 128), jnp.float32),
            pltpu.VMEM((NV * 8, 128), jnp.float32),
            pltpu.VMEM((SUB_DEV, NV * NV), jnp.float32),
            pltpu.SemaphoreType.DMA((4,)),
            pltpu.SemaphoreType.DMA((2,)),
        ],
        name="factor",
    )(order, meta, *shares, below, above, rescue, blocks, high_y, flat)


def shifted(value, amount):
    size = N_ROW * N_COL
    return lax.ppermute(value, ("row", "col"), [(i, (i + amount) % size) for i in range(size)])


def packed(blocks):
    wide = jnp.pad(blocks, ((0, 0), (0, 0), (0, 64 - NV)))
    return jnp.concatenate([wide[:6], wide[6:]], axis=2)


def everywhere(value):
    size = N_ROW * N_COL
    step = 1
    while step < size:
        value = value + lax.ppermute(value, ("row", "col"), [(i, i ^ step) for i in range(size)])
        step *= 2
    return value


def choose_kernel(spot, right2, right1, share, left1, left2, side, out):
    out[12:14] = side[...]
    for case, sources in enumerate(((share, left1, left2), (right1, share, left1), (right2, right1, share))):

        @pl.when(spot[3] == case)
        def _():
            for i, source in enumerate(sources):
                out[4 * i : 4 * i + 4] = source[...]


def choose(spot, right2, right1, share, left1, left2, side):
    vmem = pl.BlockSpec(memory_space=pltpu.VMEM)
    return pl.pallas_call(
        choose_kernel,
        out_shape=jax.ShapeDtypeStruct((14, NV, 128), jnp.float32),
        in_specs=[pl.BlockSpec(memory_space=pltpu.SMEM)] + [vmem] * 6,
        out_specs=vmem,
        name="choose",
    )(spot, right2, right1, share, left1, left2, side)


def exchange(device, order, blocks, share, side, plan, local):
    subdomain = jnp.arange(SUBS, dtype=jnp.int32)
    my_order = lax.dynamic_slice(order, (device * SUB_DEV,), (SUB_DEV,))

    right1 = shifted(share, 1)
    left1 = shifted(share, -1)
    right2 = shifted(share, 2)
    left2 = shifted(share, -2)
    payload = choose(plan, right2, right1, share, left1, left2, side)
    below = shifted(payload, N_COL)
    above = shifted(payload, -N_COL)
    flat, high_y = flatten(order, blocks, left1)
    right3 = shifted(right2, 1)
    left3 = shifted(left2, -1)
    def local_path(_):
        return (jnp.zeros((24, NV, 128), jnp.float32), plan)

    def global_path(_):
        slots = jnp.arange(12, dtype=jnp.int32)
        hit = (order[None, :] == slots[:, None]) & (slots[:, None] < PB)
        listed = jnp.where(slots < PB, jnp.sum(jnp.where(hit, subdomain[None, :], 0), axis=1), -1)
        mask = ((my_order[None, :] == slots[:, None]) & (slots[:, None] < PB)).astype(jnp.float32)
        def oriented(block, offset):
            other = lax.dynamic_slice(jnp.concatenate([order[:128], order]), (128 + device * SUB_DEV - offset,), (SUB_DEV,))
            return jnp.where((my_order > other)[:, None, None], block, jnp.swapaxes(block, 1, 2))

        kinds = jnp.stack(
            [
                blocks[:, 0, :, :NV],
                oriented(blocks[:, 2, :, :NV], SUB_DEV),
                oriented(blocks[:, 3, :, :NV], 1),
                oriented(blocks[:, 1, :, :NV], N_COL * SUB_DEV),
            ],
            axis=1,
        )
        placed = jnp.einsum("ps,skvw->pkvw", mask, kinds, precision=lax.Precision.HIGHEST)
        whole = everywhere(
            jnp.stack([packed(placed[4 * i : 4 * i + 4, :3].reshape(12, NV, NV)) for i in range(3)] + [packed(placed[:, 3])])
        )
        return (whole.reshape(24, NV, 128), jnp.concatenate([plan[:4], listed]).astype(jnp.int32))

    rescue, meta = lax.cond(local.reshape(()) > 0, local_path, global_path, None)
    shares = (share, right1, right2, right3, left1, left2, left3)
    panel, flat = factor(order, meta, shares, below, above, rescue, blocks, high_y, flat)
    return (jnp.transpose(flat, (1, 0, 2)), panel)


def edges_kernel(deflation, along_x, along_y, sems):
    x_copy = pltpu.make_async_copy(deflation.at[1, :, :, pl.ds(48 * NV, 16 * NV)], along_x, sems.at[0])
    y_copies = [pltpu.make_async_copy(deflation.at[x, 7], along_y.at[x], sems.at[1 + x]) for x in range(2)]
    x_copy.start()
    for copy in y_copies:
        copy.start()
    x_copy.wait()
    for copy in y_copies:
        copy.wait()


def edges(deflation):
    vmem = pl.BlockSpec(memory_space=pltpu.VMEM)
    return pl.pallas_call(
        edges_kernel,
        out_shape=(
            jax.ShapeDtypeStruct((8, 16, 16 * NV), jnp.bfloat16),
            jax.ShapeDtypeStruct((2, 16, 64 * NV), jnp.bfloat16),
        ),
        in_specs=[pl.BlockSpec(memory_space=pl.ANY)],
        out_specs=(vmem, vmem),
        scratch_shapes=[pltpu.SemaphoreType.DMA((3,))],
        name="edges",
    )(deflation)


def from_next(value, axis, amount):
    size = lax.axis_size(axis)
    pairs = [(i, i + amount) for i in range(size) if 0 <= i + amount < size]
    return lax.ppermute(value, axis, pairs)


def shards(deflation, coefficient, gradients, x_penalty, y_penalty, z_penalty, coarse_order):
    device = device_index()
    along_x, along_y = edges(deflation)
    below_x = from_next(along_x, "row", 1)
    below_y = from_next(along_y, "col", 1)
    main, own_x, own_y, roots_x, roots_y = assemble(
        deflation, gradients.reshape(192, 64), coefficient, x_penalty, jnp.transpose(y_penalty, (1, 0, 2)), z_penalty
    )
    blocks, share, side, plan, local = lateral(coarse_order, coarse_order.reshape(8, 128), below_x, below_y, main, own_x, own_y, roots_x, roots_y)
    return exchange(device, coarse_order, blocks, share, side, plan, local)


def solution(mesh):
    in_specs = (
        P("row", "col", None, None),
        P("row", "col", None),
        P(),
        P("row", "col", None),
        P("row", "col", None),
        P("row", "col", None),
        P(),
    )
    out_specs = (P(("row", "col"), None, None), P(("row", "col"), None, None))
    return jax.shard_map(shards, mesh=mesh, in_specs=in_specs, out_specs=out_specs, check_vma=False)
```
